32 devices in a mesh: row: 4 (over x, core), col: 2 (over y), date: 4 (over z).
Axes of the slice: x: 2, y: 2, z: 4, core: 2. Of those that a mesh axis runs over, the one named last changes fastest.
Arguments:
- slc: bfloat16 [2, 48, 24, 512], P(None, 'date', 'row', 'col'), may hold values from -6 to 6
- pairs: int32 [32, 2], P('date'), may hold values from 0 to 47, as said below
- target: float32 [2, 32, 12, 128], P(None, 'date', 'row', 'col'), may hold values from -4 to 4
- w_lift: bfloat16 [2, 3, 3, 64], replicated, may hold values from -1.5 to 1.5
- b_lift: bfloat16 [2, 64], replicated, may hold values from -2 to 2
- w_mid: bfloat16 [2, 3, 3, 64, 64], replicated, may hold values from -0.1875 to 0.1875
- b_mid: bfloat16 [2, 64], replicated, may hold values from -2 to 2
- w_proj: bfloat16 [2, 3, 3, 64], replicated, may hold values from -0.1875 to 0.1875
Outputs:
- denoised: float32 [2, 32, 12, 128], P(None, 'date', 'row', 'col')
- grad_lift: float32 [2, 3, 3, 64], replicated
- grad_lift_bias: float32 [2, 64], replicated
- grad_mid: float32 [2, 3, 3, 64, 64], replicated
- grad_mid_bias: float32 [2, 64], replicated
- grad_proj: float32 [2, 3, 3, 64], replicated
The draws below stay inside these ranges and needn't reach their ends.
Inputs may be any that keep to these rules, and one draw needn't show every extreme that they name: `pairs`: row p belongs to date index p // 8, which holds dates d * 12 to (d + 1) * 12 - 1; its earlier date lies there, and its later date is later by 1 to 24 dates. Row 0 is (0, 24).
All inputs are finite; a program needn't handle non-finite values.
Results may differ from the reference program's by a relative error of at most 0.00065.
The reference program's roundings to bfloat16 on the way count: a program that leaves them out, or rounds other values in their place, can miss the bound.
Values may be sent and summed in bfloat16 or wider, within the bound.
A program may use at most 64 MiB of HBM per device.

```python
import math
import jax
import jax.numpy as jnp
from jax import lax

CH = 64
PAIRS_DEV = 8
DD = 12
LR = 2
LC = 4
DATES = 48
PAIRS = 32
NR = 24
NC = 512
NMR = 12
NMC = 128
N_DATE = 4


def draw_pairs(key, part):
    row_count = PAIRS_DEV * N_DATE
    holder = jnp.arange(row_count, dtype=jnp.int32) // PAIRS_DEV
    key_early, key_late = jax.random.split(jax.random.fold_in(key, 7))
    slab_start = holder * DD
    slab_stop = jnp.minimum(slab_start + DD, DATES - 1)
    window = slab_stop - slab_start
    earlier = slab_start + jax.random.randint(key_early, (row_count,), 0, 1 << 20, dtype=jnp.int32) % window
    headroom = jnp.minimum(2 * DD, DATES - 1 - earlier)
    later_date = earlier + 1 + jax.random.randint(key_late, (row_count,), 0, 1 << 20, dtype=jnp.int32) % headroom
    earlier = earlier.at[0].set(0)
    later_date = later_date.at[0].set(2 * DD)
    return jnp.stack([earlier, later_date], axis=1).astype(jnp.int32)


def levels(own_key, dims, cuts, smallest, largest):
    loudness, own = 1.0, jax.random.fold_in(own_key, 6)
    for axis_at, parts in cuts:
        draws = jnp.exp(jax.random.uniform(jax.random.fold_in(own, axis_at), (parts,), jnp.float32, smallest / len(cuts), largest / len(cuts)))
        loudness = loudness * jnp.repeat(draws, dims[axis_at] // parts).reshape([-1 if axis == axis_at else 1 for axis in range(len(dims))])
    return loudness


def gaussian(rng, extent, deviation, limit, pieces=(), kind=jnp.bfloat16):
    drawn = deviation * jax.random.normal(rng, extent, jnp.float32)
    if pieces:
        drawn = drawn * levels(rng, extent, pieces, -0.22, 0.18)
    return jnp.clip(drawn, -limit, limit).astype(kind)


def setup_inputs(seed: int = 0) -> dict:
    keys = jax.random.split(jax.random.key(seed), 9)
    return {
        "slc": gaussian(keys[0], (2, DATES, NR, NC), 1.0, 6.0, ((1, 4), (2, 4), (3, 2))),
        "pairs": draw_pairs(jax.random.fold_in(keys[8], 71), 0),
        "target": gaussian(keys[2], (2, PAIRS, NMR, NMC), 0.5, 4.0, ((1, 4), (2, 4), (3, 2)), jnp.float32),
        "w_lift": gaussian(keys[3], (2, 3, 3, CH), 18 ** -0.5, 1.5),
        "b_lift": gaussian(keys[4], (2, CH), 0.3, 2.0),
        "w_mid": gaussian(keys[5], (2, 3, 3, CH, CH), (18 * CH) ** -0.5, 0.1875),
        "b_mid": gaussian(keys[6], (2, CH), 0.3, 2.0),
        "w_proj": gaussian(keys[7], (2, 3, 3, CH), (18 * CH) ** -0.5, 0.1875),
    }


def real_block(weights):
    real_part = weights[0]
    imag_part = weights[1]
    upper = jnp.concatenate([real_part, imag_part], axis=-1)
    lower = jnp.concatenate([-imag_part, real_part], axis=-1)
    return jnp.concatenate([upper, lower], axis=-2)

def fold_grads(gram, inner):
    outer = gram.shape[-1] // 2
    real_part = gram[:, :, :inner, :outer] + gram[:, :, inner:, outer:]
    imag_part = gram[:, :, :inner, outer:] - gram[:, :, inner:, :outer]
    return jnp.stack([real_part, imag_part])

def field_pad(field):
    return jnp.pad(field, ((0, 0), (0, 0), (1, 1), (1, 1)))

def hidden_pad(hidden):
    return jnp.pad(hidden, ((0, 0), (1, 1), (1, 1), (0, 0)))

def tap_sum(padded_in, kernel, form, offset, on_field):
    height = padded_in.shape[2] - 2 if on_field else padded_in.shape[1] - 2
    breadth = padded_in.shape[3] - 2 if on_field else padded_in.shape[2] - 2
    summed = 0.0
    for row_tap in range(3):
        for col_tap in range(3):
            row_at = 2 - row_tap if offset else row_tap
            col_at = 2 - col_tap if offset else col_tap
            if on_field:
                window = padded_in[:, :, row_at:row_at + height, col_at:col_at + breadth]
            else:
                window = padded_in[:, row_at:row_at + height, col_at:col_at + breadth, :]
            summed = summed + jnp.einsum(form, window.astype(jnp.float32), kernel[row_tap, col_tap].astype(jnp.float32))
    return summed

def tap_gram(padded_in, grad_out, form, on_field):
    height = padded_in.shape[2] - 2 if on_field else padded_in.shape[1] - 2
    breadth = padded_in.shape[3] - 2 if on_field else padded_in.shape[2] - 2
    grams = []
    for row_tap in range(3):
        for col_tap in range(3):
            if on_field:
                window = padded_in[:, :, row_tap:row_tap + height, col_tap:col_tap + breadth]
            else:
                window = padded_in[:, row_tap:row_tap + height, col_tap:col_tap + breadth, :]
            grams.append(jnp.einsum(form, window.astype(jnp.float32), grad_out.astype(jnp.float32)))
    stacked = jnp.stack(grams)
    return stacked.reshape((3, 3) + stacked.shape[1:])

def reference(slc, pairs, target, w_lift, b_lift, w_mid, b_mid, w_proj):
    earlier = jnp.take(slc, pairs[:, 0], axis=1).astype(jnp.float32)
    later_date = jnp.take(slc, pairs[:, 1], axis=1).astype(jnp.float32)
    real_part = earlier[0] * later_date[0] + earlier[1] * later_date[1]
    imag_part = earlier[1] * later_date[0] - earlier[0] * later_date[1]
    product = jnp.stack([real_part, imag_part])
    looks = product.reshape(2, PAIRS, NMR, LR, NMC, LC).mean(axis=(3, 5)).astype(jnp.bfloat16)
    lift_block = real_block(w_lift[:, :, :, None, :])
    mid_block = real_block(w_mid)
    proj_block = real_block(w_proj[..., None])
    lift_bias = b_lift.reshape(2 * CH).astype(jnp.float32)
    mid_bias = b_mid.reshape(2 * CH).astype(jnp.float32)
    loss_scale = 1.0 / math.sqrt(2.0 * PAIRS * NMR * NMC)

    def one_pair(inputs):
        image, goal = inputs
        image = image[:, None]
        goal = goal[:, None]
        image_pad = field_pad(image)
        pre1 = tap_sum(image_pad, lift_block, 'zprc,zo->prco', 0, True) + lift_bias
        hidden1 = jnp.maximum(pre1, 0.0).astype(jnp.bfloat16)
        hidden1_pad = hidden_pad(hidden1)
        pre2 = tap_sum(hidden1_pad, mid_block, 'prci,io->prco', 0, False) + mid_bias
        hidden2 = jnp.maximum(pre2, 0.0).astype(jnp.bfloat16)
        hidden2_pad = hidden_pad(hidden2)
        noise = tap_sum(hidden2_pad, proj_block, 'prci,iz->zprc', 0, False)
        cleaned = image.astype(jnp.float32) - noise
        d_noise = ((goal - cleaned) * loss_scale).astype(jnp.bfloat16)
        d_hidden2 = tap_sum(field_pad(d_noise), proj_block, 'zprc,iz->prci', 2, True)
        d_pre2 = jnp.where(hidden2 > 0, d_hidden2, 0.0).astype(jnp.bfloat16)
        d_hidden1 = tap_sum(hidden_pad(d_pre2), mid_block, 'prco,io->prci', 2, False)
        d_pre1 = jnp.where(hidden1 > 0, d_hidden1, 0.0).astype(jnp.bfloat16)
        gram_lift = tap_gram(image_pad, d_pre1, 'zprc,prco->zo', True)
        gram_mid = tap_gram(hidden1_pad, d_pre2, 'prci,prco->io', False)
        gram_proj = tap_gram(hidden2_pad, d_noise, 'prci,zprc->iz', False)
        lift_bias_grad = lax.optimization_barrier(jnp.sum(d_pre1.astype(jnp.float32), axis=(0, 1, 2)))
        mid_bias_grad = lax.optimization_barrier(jnp.sum(d_pre2.astype(jnp.float32), axis=(0, 1, 2)))
        return (cleaned[:, 0], gram_lift, lift_bias_grad, gram_mid, mid_bias_grad, gram_proj)
    results = lax.map(one_pair, (jnp.moveaxis(looks, 1, 0), jnp.moveaxis(target, 1, 0)))
    denoised = jnp.moveaxis(results[0], 0, 1)
    gram_lift = lax.optimization_barrier(jnp.sum(results[1], axis=0))
    lift_bias_grad = lax.optimization_barrier(jnp.sum(results[2], axis=0))
    gram_mid = lax.optimization_barrier(jnp.sum(results[3], axis=0))
    mid_bias_grad = lax.optimization_barrier(jnp.sum(results[4], axis=0))
    gram_proj = lax.optimization_barrier(jnp.sum(results[5], axis=0))
    grad_lift = fold_grads(gram_lift, 1)[:, :, :, 0, :]
    grad_mid = fold_grads(gram_mid, CH)
    grad_proj = fold_grads(gram_proj, CH)[..., 0]
    return (denoised, grad_lift, lift_bias_grad.reshape(2, CH), grad_mid, mid_bias_grad.reshape(2, CH), grad_proj)
```

```python
import functools
import math

import jax
import jax.numpy as jnp
from jax import lax
from jax.experimental import pallas as pl
from jax.experimental.pallas import tpu as pltpu
from jax.sharding import PartitionSpec as P

MESH = pl.DeviceIdType.MESH

LR = 2
LC = 4


def mm(a, b):
    return jnp.dot(a, b, preferred_element_type=jnp.float32)


def mm_t(a, b):
    return lax.dot_general(a, b, (((1,), (1,)), ((), ())), preferred_element_type=jnp.float32)


def step_kernel(
    dims, scale,
    slc_ref, pick_ref, avg_ref, tgt_ref, wl_any, bl_any, wmid_any, bmid_any, wproj_any,
    den_ref, o_ref, small_ref,
    pool, look_f, look_s, look_r, tgt_r, fld, tfld, i3a, i3b, h2s, tsum, dn3, dnm3, dp2m, dp1, outs, x_ref,
    wl_in, bl_in, wm_in, bm_in, wj_in, w_sem, w1_ref, wp_ref, wpb_ref, wf_ref, wb_ref, bm_ref, wtmp,
    plane_in, date_in, small_in, small_date, small_sem, small_date_sem, slab_sem, look_sem, tgt_sem, den_sem, plane_sem, date_sem, gather_sem,
):
    n_row, n_col, n_date, pp, tr, tc = dims
    r, c, d = lax.axis_index("row"), lax.axis_index("col"), lax.axis_index("date")
    n_plane = n_row * n_col
    me = r * n_col + c
    rows = n_row * tr
    gap = rows + 1
    nb = gap * pp
    n = nb * 128
    base = (128 - tc) // 2
    pairs = pp * n_row
    f32, bf16 = jnp.float32, jnp.bfloat16

    def plane_peer(k):
        peer = lax.rem(me + k, n_plane)
        return peer, (lax.div(peer, n_col), lax.rem(peer, n_col), d)

    def date_peer(k):
        return (r, c, lax.rem(d + k, n_date))

    def remote(src, dst, sems, at, where):
        copy = pltpu.make_async_remote_copy(
            src_ref=src, dst_ref=dst, send_sem=sems.at[0, at], recv_sem=sems.at[1, at],
            device_id=where, device_id_type=MESH,
        )
        copy.start()
        return copy

    fetches = []
    wide = zip((wl_any, bl_any, wmid_any, bmid_any, wproj_any), (wl_in, bl_in, wm_in, bm_in, wj_in))
    for k, (src, dst) in enumerate(wide):
        copy = pltpu.make_async_copy(src, dst, w_sem.at[k])
        copy.start()
        fetches.append(copy)
    barrier = pltpu.get_barrier_semaphore()
    for k in range(1, n_plane):
        pl.semaphore_signal(barrier, inc=1, device_id=plane_peer(k)[1], device_id_type=MESH)
    for k in range(1, n_date):
        pl.semaphore_signal(barrier, inc=1, device_id=date_peer(k), device_id_type=MESH)
    pl.semaphore_wait(barrier, n_plane + n_date - 2)

    sent = []
    slabs = [remote(slc_ref, pool.at[k - 1], slab_sem, k, date_peer(n_date - k)) for k in (1, 2)]

    def exchange(src, dst, sems):
        copies = []
        for way in range(3):
            col = lax.rem(c + (0, 1, n_col - 1)[way], n_col)
            for o in range(n_row):
                k = lax.rem(r + o, n_row)
                at = way * n_row + o
                if way == 0 and o == 0:
                    copy = pltpu.make_async_copy(src.at[k], dst.at[0, r], sems.at[0, at])
                    copy.start()
                    copies.append((copy, True))
                else:
                    copies.append((remote(src.at[k], dst.at[way, r], sems, at, (k, col, d)), False))
        return copies

    tgt_copies = exchange(tgt_ref, tgt_r, tgt_sem)
    for ref in (fld, tfld, dn3, dnm3, tsum):
        ref[...] = jnp.zeros_like(ref)
    edge = jnp.zeros((i3a.shape[0], 128), bf16)
    for ref in (i3a, i3b):
        ref[:, 0:128] = edge
        ref[:, (nb + 1) * 128 : (nb + 2) * 128] = edge
    x_ref[...] = jnp.zeros_like(x_ref)
    lane = lax.broadcasted_iota(jnp.int32, (1, 128), 1)
    spot = c * tc + lane - base
    inside = (spot >= 0) & (spot < n_col * tc)
    own = (lane >= base) & (lane < base + tc)
    for copy in fetches:
        copy.wait()
    wtmp[...] = jnp.zeros_like(wtmp)

    def joined(a, b):
        return jnp.concatenate([a, b], axis=1)

    for t in range(3):
        for u in range(3):
            pair = wl_in[t, u].astype(f32)
            at = 8 * t + 2 * u
            wtmp[0, at : at + 1, :] = joined(pair[0:1], pair[1:2])
            wtmp[0, at + 1 : at + 2, :] = joined(-pair[1:2], pair[0:1])
            pair = wj_in[t, u].astype(f32)
            real, imag = joined(pair[0:1], -pair[1:2]), joined(pair[1:2], pair[0:1])
            flip = 8 * (2 - t) + 2 * (2 - u)
            wtmp[1, at : at + 1, :] = real
            wtmp[1, at + 1 : at + 2, :] = imag
            wtmp[2, flip : flip + 1, :] = real
            wtmp[2, flip + 1 : flip + 2, :] = imag
            wr, wi = wm_in[0, t, u].astype(f32), wm_in[1, t, u].astype(f32)
            block = jnp.concatenate([joined(wr, wi), joined(-wi, wr)], axis=0)
            wb_ref[2 - t, :, (2 - u) * 128 : (3 - u) * 128] = block.astype(bf16)
            wf_ref[t, :, u * 128 : (u + 1) * 128] = block.T.astype(bf16)
    bias = bl_in[...].astype(f32)
    wtmp[0, 14:15, :] = joined(bias[0:1], bias[1:2])
    bias = bm_in[...].astype(f32)
    wtmp[3, 0:1, :] = joined(bias[0:1], bias[1:2])
    w1_ref[...] = wtmp[0].T[:, 0:32].astype(bf16)
    wp_ref[...] = wtmp[1, 0:32].astype(bf16)
    wpb_ref[...] = wtmp[2].T[:, 0:32].astype(bf16)
    bm_ref[...] = wtmp[3].T[:, 0:1]
    for copy in slabs:
        copy.wait_recv()
    sent += slabs

    depth = slc_ref.shape[0]
    picked = (
        mm(pick_ref[:, :depth], slc_ref[...])
        + mm(pick_ref[:, depth : 2 * depth], pool[0])
        + mm(pick_ref[:, 2 * depth :], pool[1])
    )
    parts = slc_ref.shape[1] // (LR * tr)
    halves = tc * LC // parts
    sides = []
    for h in range(halves):
        at = [picked[q * pairs : (q + 1) * pairs] for q in (h, halves + h, 2 * halves + h, 3 * halves + h)]
        a0, a1, b0, b1 = at
        rowsum = []
        for prod in (a0 * b0 + a1 * b1, a1 * b0 - a0 * b1):
            for t in range(tr):
                rowsum.append(
                    sum(prod[:, (t * LR + q) * parts : (t * LR + q + 1) * parts] for q in range(LR))
                )
        sides.append(jnp.concatenate(rowsum, axis=0))
    looked = jnp.dot(
        jnp.concatenate(sides, axis=1), avg_ref[...],
        precision=lax.Precision.HIGHEST, preferred_element_type=f32,
    )
    look_f[...] = jnp.zeros_like(look_f)
    for k in range(n_row):
        for q in range(2 * tr):
            look_f[k, q * pp : (q + 1) * pp, :] = looked[q * pairs + k * pp : q * pairs + (k + 1) * pp]
    look_s[...] = look_f[...].astype(bf16)
    look_copies = exchange(look_s, look_r, look_sem)

    def settle(copies):
        for copy, near in copies:
            if near:
                copy.wait()
            else:
                copy.wait_recv()
                sent.append(copy)

    def assemble(ref, s):
        mid = pltpu.roll(ref[0, s].astype(f32), base, 1)
        low = pltpu.roll(ref[1, s].astype(f32), (base - tc) % 128, 1)
        high = pltpu.roll(ref[2, s].astype(f32), base + tc, 1)
        joined = jnp.where(own, mid, jnp.where(lane < base, low, high))
        near = (lane >= base - 5) & (lane < base + tc + 5)
        return jnp.where(inside & near, joined, 0.0)

    settle(tgt_copies)
    for s in range(n_row):
        block = assemble(tgt_r, s)
        for z in range(2):
            for t in range(tr):
                for p in range(pp):
                    i = (z * tr + t) * pp + p
                    b = p * gap + s * tr + t
                    tfld[z : z + 1, b * 128 : (b + 1) * 128] = block[i : i + 1]
    settle(look_copies)
    for s in range(n_row):
        block = assemble(look_r, s)
        for u, turned in enumerate((pltpu.roll(block, 1, 1), block, pltpu.roll(block, 127, 1))):
            for z in range(2):
                for t in range(tr):
                    for p in range(pp):
                        i = (z * tr + t) * pp + p
                        b = p * gap + s * tr + t + 1
                        fld[2 * u + z : 2 * u + z + 1, b * 128 : (b + 1) * 128] = turned[i : i + 1]
    fld[6:7, :] = jnp.ones((1, (nb + 2) * 128), f32)

    def taps(ref, at, width):
        three = [ref[:, pl.ds(pl.multiple_of(at + t * 128, 128), width)] for t in range(3)]
        return jnp.concatenate(three + [jnp.zeros((8, width), f32)], axis=0).astype(bf16)

    def turned_store(ref, value, at):
        for u, turn in enumerate((1, 0, 127)):
            for q in range(2):
                piece = value[:, q * 128 : (q + 1) * 128]
                if turn:
                    piece = pltpu.roll(piece, turn, 1)
                ref[u * 128 : (u + 1) * 128, pl.ds(pl.multiple_of(at + (q + 1) * 128, 128), 128)] = (
                    piece.astype(bf16)
                )

    def good(b):
        one = [inside & (lax.rem(b + q, gap) != gap - 1) for q in range(2)]
        return jnp.concatenate(one, axis=1)

    own2 = jnp.concatenate([own, own], axis=1)

    def rounded(value):
        return value.astype(bf16).astype(f32)

    def lift(i, carry):
        at = pl.multiple_of(i * 256, 256)
        pre1 = mm(w1_ref[...], taps(fld, at, 256))
        turned_store(i3a, rounded(jnp.where(good(2 * i), jnp.maximum(pre1, 0.0), 0.0)), at)
        return carry

    lax.fori_loop(0, nb // 2, lift, 0, unroll=True)

    def conv(w_ref, ref, at):
        total = 0.0
        for t in range(3):
            total = total + mm(w_ref[t], ref[:, pl.ds(pl.multiple_of(at + t * 128, 128), 256)])
        return total

    def mid(i, carry):
        at = pl.multiple_of(i * 256, 256)
        pre2 = conv(wf_ref, i3a, at) + bm_ref[...]
        h2 = jnp.where(good(2 * i), jnp.maximum(pre2, 0.0), 0.0).astype(bf16)
        h2s[:, pl.ds(at, 256)] = h2
        tsum[:, pl.ds(pl.multiple_of(at + 128, 128), 256)] = mm(wp_ref[...], h2)
        return carry

    lax.fori_loop(0, nb // 2, mid, 0, unroll=True)

    six = sum(tsum[8 * t : 8 * t + 8, t * 128 : t * 128 + n] for t in range(3))
    noise = pltpu.roll(six, 1, 1)[0:2] + six[2:4] + pltpu.roll(six, n - 1, 1)[4:6]
    den = fld[2:4, 128 : 128 + n] - noise
    shifted = pltpu.roll(den, n - base, 1)
    outs[...] = jnp.zeros_like(outs)
    for s in range(n_row):
        for z in range(2):
            for t in range(tr):
                for p in range(pp):
                    i = (z * tr + t) * pp + p
                    b = p * gap + s * tr + t
                    outs[s, i : i + 1, :] = shifted[z : z + 1, b * 128 : (b + 1) * 128]
    den_copies = []
    for o in range(n_row):
        k = lax.rem(r + o, n_row)
        if o == 0:
            copy = pltpu.make_async_copy(outs.at[k], den_ref.at[r], den_sem.at[0, o])
            copy.start()
            den_copies.append((copy, True))
        else:
            den_copies.append((remote(outs.at[k], den_ref.at[r], den_sem, o, (k, c, d)), False))
    dn = rounded((tfld[0:2, :] - den) * scale)
    rowok = [jnp.full((1, 128), b % gap != gap - 1) for b in range(nb)]
    mask = jnp.concatenate([inside & ok for ok in rowok], axis=1)
    own_all = jnp.concatenate([own & ok for ok in rowok], axis=1)
    for ref, keep in ((dn3, mask), (dnm3, own_all)):
        kept = jnp.where(keep, dn, 0.0)
        ref[0:2, 128 : 128 + n] = pltpu.roll(kept, 1, 1)
        ref[2:4, 128 : 128 + n] = kept
        ref[4:6, 128 : 128 + n] = pltpu.roll(kept, n - 1, 1)

    def back2(i, carry):
        at = pl.multiple_of(i * 256, 256)
        grad = mm(wpb_ref[...], taps(dn3, at, 256))
        grad = rounded(jnp.where(h2s[:, pl.ds(at, 256)].astype(f32) > 0, grad, 0.0))
        turned_store(i3b, grad, at)
        dp2m[:, pl.ds(at, 256)] = jnp.where(own2, grad, 0.0).astype(bf16)
        return carry

    lax.fori_loop(0, nb // 2, back2, 0, unroll=True)

    sign = jnp.where(lane < 64, 1.0, -1.0)
    for t in range(3):
        gram = mm_t(i3a[:, t * 128 : t * 128 + n], dp2m[...])
        for u in range(3):
            upper = gram[u * 128 : u * 128 + 64]
            lower = gram[u * 128 + 64 : u * 128 + 128]
            x_ref[(3 * t + u) * 64 : (3 * t + u) * 64 + 64, :] = upper + sign * pltpu.roll(lower, 64, 1)
    x_ref[576:600, :] = mm_t(taps(dnm3, 0, n), h2s[...])[0:24]
    x_ref[600:608, :] = mm_t(jnp.ones((16, n), bf16), dp2m[...])[0:8]

    piece = plane_in.shape[1]

    def slot(ref, k):
        return ref.at[pl.ds(pl.multiple_of(k * piece, 8), piece)]

    scatter = []
    for k in range(1, n_plane):
        peer, where = plane_peer(k)
        scatter.append(remote(slot(x_ref, peer), plane_in.at[k], plane_sem, k, where))

    def back1(i, carry):
        at = pl.multiple_of(i * 256, 256)
        h1 = i3a[128:256, pl.ds(pl.multiple_of(at + 128, 128), 256)].astype(f32)
        grad = jnp.where((h1 > 0) & own2, conv(wb_ref, i3b, at), 0.0)
        dp1[:, pl.ds(at, 256)] = grad.astype(bf16)
        return carry

    lax.fori_loop(0, nb // 2, back1, 0, unroll=True)

    small_in[me] = mm_t(taps(fld, 0, n), dp1[...])[0:24]
    small = [
        remote(small_in.at[me], small_in.at[me], small_sem, k, plane_peer(k)[1]) for k in range(1, n_plane)
    ]
    part = slot(x_ref, me)[...]
    for k, copy in zip(range(1, n_plane), scatter):
        copy.wait_recv()
        part = part + plane_in[k]
    date_in[d] = part
    spread = [remote(date_in.at[d], date_in.at[d], date_sem, k, date_peer(k)) for k in range(1, n_date)]

    def total(ref, count):
        return functools.reduce(lambda a, b: a + b, [ref[k] for k in range(count)])

    for copy in small:
        copy.wait_recv()
    small_date[d] = total(small_in, n_plane)
    small_spread = [
        remote(small_date.at[d], small_date.at[d], small_date_sem, k, date_peer(k)) for k in range(1, n_date)
    ]
    for copy in spread:
        copy.wait_recv()
    slot(o_ref, me)[...] = total(date_in, n_date)
    gather = [
        remote(slot(o_ref, me), slot(o_ref, me), gather_sem, k, plane_peer(k)[1])
        for k in range(1, n_plane)
    ]
    for copy in small_spread:
        copy.wait_recv()
    small_ref[...] = total(small_date, n_date)
    settle(den_copies)
    for copy in gather:
        copy.wait_recv()
    for copy in sent + scatter + small + spread + small_spread + gather:
        copy.wait_send()


def finish_kernel(dims, den, sums, small, den_out, lift_out, lbias_out, mid_out, mbias_out, proj_out):
    n_row, pp, tr, tc, ch = dims
    for k in range(n_row):
        for z in range(2):
            for t in range(tr):
                at = (z * tr + t) * pp
                den_out[z, t, k * pp : (k + 1) * pp, :] = den[k, at : at + pp, 0:tc]
    finish_grads(ch, sums, small, lift_out, lbias_out, mid_out, mbias_out, proj_out)


def finish_grads(ch, sums, small, lift_out, lbias_out, mid_out, mbias_out, proj_out):
    for t in range(3):
        for u in range(3):
            at = 8 * t + 2 * u
            upper, lower = small[at : at + 1, :], small[at + 1 : at + 2, :]
            lift_out[t, u, 0:1, :] = upper[:, 0:ch] + lower[:, ch:]
            lift_out[t, u, 1:2, :] = upper[:, ch:] - lower[:, 0:ch]
            at = 576 + 8 * (2 - t) + 2 * (2 - u)
            upper, lower = sums[at : at + 1, :], sums[at + 1 : at + 2, :]
            proj_out[t, u, 0:1, :] = upper[:, 0:ch] + lower[:, ch:]
            proj_out[t, u, 1:2, :] = lower[:, 0:ch] - upper[:, ch:]
            at = (3 * t + u) * ch
            for z in range(2):
                mid_out[z, t, u] = sums[at : at + ch, z * ch : (z + 1) * ch]
    for z in range(2):
        lbias_out[z : z + 1, :] = small[14:15, z * ch : (z + 1) * ch]
        mbias_out[z : z + 1, :] = sums[600:601, z * ch : (z + 1) * ch]


def halo_local(slc, pairs, target, w_lift, b_lift, w_mid, b_mid, w_proj):
    n_row, n_col, n_date = (lax.axis_size(axis) for axis in ("row", "col", "date"))
    dates, srows, scols = slc.shape[1:]
    count, tr, tc = target.shape[1:]
    ch = w_mid.shape[-1]
    pp = count // n_row
    halves = scols // 128
    bf16, f32 = jnp.bfloat16, jnp.float32
    rows = 2 * tr * pp
    pad_rows = -(-rows // 16) * 16
    packed = slc.reshape(2, dates, srows, halves, 128).transpose(1, 0, 3, 2, 4)
    packed = packed.reshape(dates * 2 * halves, srows * 128)
    index = (pairs - lax.axis_index("date") * dates).T
    kinds = 2 * halves
    want = (index[:, None, :] * kinds + jnp.arange(kinds, dtype=jnp.int32)[None, :, None]).reshape(-1)
    pick = (want[:, None] == jnp.arange(3 * dates * kinds, dtype=jnp.int32)[None, :]).astype(bf16)
    spots = jnp.arange(scols, dtype=jnp.int32)[:, None] // LC
    avg = jnp.where(spots == jnp.arange(128, dtype=jnp.int32)[None, :], 1.0 / (LR * LC), 0.0).astype(f32)
    tgt = target.reshape(2, n_row, pp, tr, tc).transpose(1, 0, 3, 2, 4).reshape(n_row, rows, tc)
    tgt = jnp.pad(tgt, ((0, 0), (0, pad_rows - rows), (0, 128 - tc)))
    w_lift, w_proj = w_lift.transpose(1, 2, 0, 3), w_proj.transpose(1, 2, 0, 3)
    scale = 1.0 / math.sqrt(2.0 * count * n_date * tr * n_row * tc * n_col)
    nb = (n_row * tr + 1) * pp
    n, wide = nb * 128, (nb + 2) * 128
    n_plane = n_row * n_col
    piece = -(-608 // (8 * n_plane)) * 8
    dma = pltpu.SemaphoreType.DMA
    vmem = pltpu.VMEM
    den, sums, small = pl.pallas_call(
        functools.partial(step_kernel, (n_row, n_col, n_date, pp, tr, tc), scale),
        out_shape=(
            jax.ShapeDtypeStruct((n_row, pad_rows, 128), f32),
            jax.ShapeDtypeStruct((n_plane * piece, 128), f32),
            jax.ShapeDtypeStruct((24, 128), f32),
        ),
        in_specs=[pl.BlockSpec(memory_space=vmem)] * 4 + [pl.BlockSpec(memory_space=pl.ANY)] * 5,
        out_specs=(pl.BlockSpec(memory_space=vmem),) * 3,
        scratch_shapes=[
            vmem((2,) + packed.shape, bf16),
            vmem((n_row, pad_rows, 128), f32),
            vmem((n_row, pad_rows, 128), bf16),
            vmem((3, n_row, pad_rows, 128), bf16),
            vmem((3, n_row, pad_rows, 128), f32),
            vmem((8, wide), f32),
            vmem((8, n), f32),
            vmem((6 * ch, wide), bf16),
            vmem((6 * ch, wide), bf16),
            vmem((2 * ch, n), bf16),
            vmem((32, wide), f32),
            vmem((8, wide), f32),
            vmem((8, wide), f32),
            vmem((2 * ch, n), bf16),
            vmem((2 * ch, n), bf16),
            vmem((n_row, pad_rows, 128), f32),
            vmem((n_plane * piece, 128), f32),
            vmem(w_lift.shape, bf16),
            vmem(b_lift.shape, bf16),
            vmem(w_mid.shape, bf16),
            vmem(b_mid.shape, bf16),
            vmem(w_proj.shape, bf16),
            dma((5,)),
            vmem((2 * ch, 32), bf16),
            vmem((32, 2 * ch), bf16),
            vmem((2 * ch, 32), bf16),
            vmem((3, 2 * ch, 6 * ch), bf16),
            vmem((3, 2 * ch, 6 * ch), bf16),
            vmem((2 * ch, 1), f32),
            vmem((4, 128, 128), f32),
            vmem((n_plane, piece, 128), f32),
            vmem((n_date, piece, 128), f32),
            vmem((n_plane, 24, 128), f32),
            vmem((n_date, 24, 128), f32),
            dma((2, n_plane)),
            dma((2, n_date)),
            dma((2, 3)),
            dma((2, 3 * n_row)),
            dma((2, 3 * n_row)),
            dma((2, n_row)),
            dma((2, n_plane)),
            dma((2, n_date)),
            dma((2, n_plane)),
        ],
        compiler_params=pltpu.CompilerParams(
            collective_id=0, has_side_effects=True, vmem_limit_bytes=48 * 1024 * 1024
        ),
    )(packed, pick, avg, tgt, w_lift, b_lift, w_mid, b_mid, w_proj)
    shape = jax.ShapeDtypeStruct
    denoised, grad_lift, lift_bias, grad_mid, mid_bias, grad_proj = pl.pallas_call(
        functools.partial(finish_kernel, (n_row, pp, tr, tc, ch)),
        out_shape=(
            shape((2, tr, count, tc), f32),
            shape((3, 3, 2, ch), f32),
            shape((2, ch), f32),
            shape((2, 3, 3, ch, ch), f32),
            shape((2, ch), f32),
            shape((3, 3, 2, ch), f32),
        ),
        in_specs=[pl.BlockSpec(memory_space=vmem)] * 3,
        out_specs=(pl.BlockSpec(memory_space=vmem),) * 6,
        compiler_params=pltpu.CompilerParams(vmem_limit_bytes=8 * 1024 * 1024),
    )(den, sums, small)
    return (
        denoised.transpose(0, 2, 1, 3),
        grad_lift.transpose(2, 0, 1, 3),
        lift_bias,
        grad_mid,
        mid_bias,
        grad_proj.transpose(2, 0, 1, 3),
    )


def whole_kernel(
    dims, scale,
    slc_ref, idx_any, tgt_any, wl_any, bl_any, wmid_any, bmid_any, wproj_any,
    den_ref, o_ref, small_ref,
    pool, idx_in, tgt_in, look_s, look_r, tgt_s, tgt_r, fld, tfld, i3a, i3b, h2s, tsum, dn3, dp1, outs, x_ref,
    wl_in, bl_in, wm_in, bm_in, wj_in, w_sem, w1_ref, wp_ref, wpb_ref, wf_ref, wb_ref, bm_ref, wtmp,
    plane_in, date_in, small_in, small_date, small_sem, small_date_sem, slab_sem, look_sem, tgt_sem, den_sem, plane_sem, date_sem, gather_sem,
):
    n_row, n_col, n_date, dates, tr, tc = dims
    r, c, d = lax.axis_index("row"), lax.axis_index("col"), lax.axis_index("date")
    n_plane = n_row * n_col
    me = r * n_col + c
    pairs = n_plane
    nb = n_row * tr
    n = nb * 128
    wide = n + 256
    f32, bf16 = jnp.float32, jnp.bfloat16

    def plane_peer(k):
        peer = lax.rem(me + k, n_plane)
        return peer, (lax.div(peer, n_col), lax.rem(peer, n_col), d)

    def date_peer(k):
        return (r, c, lax.rem(d + k, n_date))

    def remote_of(src, dst, sems, at, where):
        return pltpu.make_async_remote_copy(
            src_ref=src, dst_ref=dst, send_sem=sems.at[0, at], recv_sem=sems.at[1, at],
            device_id=where, device_id_type=MESH,
        )

    def remote(src, dst, sems, at, where):
        copy = remote_of(src, dst, sems, at, where)
        copy.start()
        return copy

    barrier = pltpu.get_barrier_semaphore()
    for k in range(1, n_date):
        pl.semaphore_signal(barrier, inc=1, device_id=date_peer(k), device_id_type=MESH)
    for k in range(1, n_plane):
        pl.semaphore_signal(barrier, inc=1, device_id=plane_peer(k)[1], device_id_type=MESH)
    fetches = []
    wide_in = zip(
        (idx_any, tgt_any, wl_any, bl_any, wmid_any, bmid_any, wproj_any),
        (idx_in, tgt_in, wl_in, bl_in, wm_in, bm_in, wj_in),
    )
    for k, (src, dst) in enumerate(wide_in):
        copy = pltpu.make_async_copy(src, dst, w_sem.at[k])
        copy.start()
        fetches.append(copy)
    pl.semaphore_wait(barrier, n_plane + n_date - 2)

    slab = slc_ref.shape[0]
    chunk = LR * 128
    down = lax.max(d - 1, 0)

    def own_slab(t):
        lanes = pl.ds(t * chunk, chunk)
        return remote_of(slc_ref.at[:, lanes], pool.at[pl.ds(slab, slab), lanes], slab_sem, t, (r, c, down))

    def far_slab(t):
        lanes = pl.ds(t * chunk, chunk)
        return remote_of(
            pool.at[pl.ds(slab, slab), lanes], pool.at[pl.ds(2 * slab, slab), lanes], slab_sem, tr + t, (r, c, down)
        )

    has_down = d > 0
    has_one = d < n_date - 1
    has_two = d < n_date - 2

    @pl.when(has_down)
    def _():
        for t in range(tr):
            own_slab(t).start()

    @pl.when(jnp.logical_not(has_one))
    def _():
        pool[slab : 2 * slab, :] = jnp.zeros((slab, tr * chunk), bf16)

    @pl.when(jnp.logical_not(has_two))
    def _():
        pool[2 * slab : 3 * slab, :] = jnp.zeros((slab, tr * chunk), bf16)

    pool[0:slab, :] = slc_ref[...]
    for ref in (fld, tfld, dn3, tsum, tgt_s, look_s):
        ref[...] = jnp.zeros_like(ref)
    edge = jnp.zeros((i3a.shape[0], 128), bf16)
    for ref in (i3a, i3b):
        ref[:, 0:128] = edge
        ref[:, (nb + 1) * 128 : (nb + 2) * 128] = edge
    x_ref[608:, :] = jnp.zeros((x_ref.shape[0] - 608, 128), f32)
    outs[...] = jnp.zeros_like(outs)
    lane = lax.broadcasted_iota(jnp.int32, (1, 128), 1)
    for copy in fetches[:2]:
        copy.wait()

    def to_lane(value):
        return pltpu.roll(jnp.concatenate([value, jnp.zeros((value.shape[0], 128 - tc), f32)], axis=1), c * tc, 1)

    for z in range(2):
        for t in range(tr):
            block = to_lane(tgt_in[z, t])
            for k in range(pairs):
                tgt_s[k, z * tr + t : z * tr + t + 1, :] = block[k : k + 1]

    def exchange(src, dst, sems):
        dst[me] = src[me]
        return [remote(src.at[plane_peer(k)[0]], dst.at[me], sems, k, plane_peer(k)[1]) for k in range(1, n_plane)]

    halves = tc * LC // 128
    kinds = 2 * halves
    index = idx_in[...] - d * dates
    spread_lanes = jnp.concatenate([index[0:1]] * kinds + [index[1:2]] * kinds, axis=1)
    row_of = lax.broadcasted_iota(jnp.int32, (slab, 2 * kinds * pairs), 0)
    lane_of = lax.broadcasted_iota(jnp.int32, (slab, 2 * kinds * pairs), 1)
    same_kind = lax.rem(row_of, kinds) == lax.rem(lax.div(lane_of, pairs), kinds)
    picks = []
    for s in range(3):
        hit = same_kind & (lax.div(row_of, kinds) + s * dates == spread_lanes)
        picks.append(jnp.where(hit, 1.0, 0.0).astype(f32))
    pick = jnp.concatenate(picks, axis=0).T.astype(bf16)
    spots = lax.broadcasted_iota(jnp.int32, (tc * LC, 128), 0)
    avg_lane = lax.broadcasted_iota(jnp.int32, (tc * LC, 128), 1)
    avg = jnp.where(lax.div(spots, LC) + c * tc == avg_lane, 1.0 / (LR * LC), 0.0).astype(f32)

    @pl.when(has_one)
    def _():
        for t in range(tr):
            own_slab(t).wait_recv()

            @pl.when(has_down)
            def _():
                far_slab(t).start()

    tgt_copies = exchange(tgt_s, tgt_r, tgt_sem)

    for copy in fetches[2:]:
        copy.wait()
    wtmp[...] = jnp.zeros_like(wtmp)

    def joined(a, b):
        return jnp.concatenate([a, b], axis=1)

    for t in range(3):
        for u in range(3):
            pair = wl_in[t, u].astype(f32)
            at = 8 * t + 2 * u
            wtmp[0, at : at + 1, :] = joined(pair[0:1], pair[1:2])
            wtmp[0, at + 1 : at + 2, :] = joined(-pair[1:2], pair[0:1])
            pair = wj_in[t, u].astype(f32)
            real, imag = joined(pair[0:1], -pair[1:2]), joined(pair[1:2], pair[0:1])
            flip = 8 * (2 - t) + 2 * (2 - u)
            wtmp[1, at : at + 1, :] = real
            wtmp[1, at + 1 : at + 2, :] = imag
            wtmp[2, flip : flip + 1, :] = real
            wtmp[2, flip + 1 : flip + 2, :] = imag
            wr, wi = wm_in[0, t, u].astype(f32), wm_in[1, t, u].astype(f32)
            block = jnp.concatenate([joined(wr, wi), joined(-wi, wr)], axis=0)
            wb_ref[2 - t, :, (2 - u) * 128 : (3 - u) * 128] = block.astype(bf16)
            wf_ref[t, :, u * 128 : (u + 1) * 128] = block.T.astype(bf16)
    bias = bl_in[...].astype(f32)
    wtmp[0, 14:15, :] = joined(bias[0:1], bias[1:2])
    bias = bm_in[...].astype(f32)
    wtmp[3, 0:1, :] = joined(bias[0:1], bias[1:2])
    w1_ref[...] = wtmp[0].T[:, 0:32].astype(bf16)
    wp_ref[...] = wtmp[1, 0:32].astype(bf16)
    wpb_ref[...] = wtmp[2].T[:, 0:32].astype(bf16)
    bm_ref[...] = wtmp[3].T[:, 0:1]
    fld[6:7, :] = jnp.ones((1, wide), f32)

    def rounded(value):
        return value.astype(bf16).astype(f32)

    for t in range(tr):

        @pl.when(has_two)
        def _():
            far_slab(t).wait_recv()

        picked = mm(pick, pool[:, t * chunk : (t + 1) * chunk])
        sides = []
        for h in range(halves):
            a0, a1, b0, b1 = [picked[q * pairs : (q + 1) * pairs] for q in (h, halves + h, 2 * halves + h, 3 * halves + h)]
            both = []
            for prod in (a0 * b0 + a1 * b1, a1 * b0 - a0 * b1):
                both.append(sum(prod[:, q * 128 : (q + 1) * 128] for q in range(LR)))
            sides.append(jnp.concatenate(both, axis=0))
        looked = rounded(
            jnp.dot(
                jnp.concatenate(sides, axis=1), avg,
                precision=lax.Precision.HIGHEST, preferred_element_type=f32,
            )
        )
        for z in range(2):
            for k in range(pairs):
                at = z * tr + t
                look_s[k, at : at + 1, :] = looked[z * pairs + k : z * pairs + k + 1]
    look_copies = exchange(look_s, look_r, look_sem)

    def settle(copies):
        for copy in copies:
            copy.wait_recv()

    first, last = lane == 0, lane == 127

    def right(value):
        return jnp.where(first, 0.0, pltpu.roll(value, 1, 1))

    def left(value):
        return jnp.where(last, 0.0, pltpu.roll(value, 127, 1))

    def assemble(ref, s):
        return functools.reduce(lambda a, b: a + b, [ref[s * n_col + q] for q in range(n_col)])

    settle(tgt_copies)
    for s in range(n_row):
        block = assemble(tgt_r, s)
        for z in range(2):
            for t in range(tr):
                b = s * tr + t
                tfld[z : z + 1, b * 128 : (b + 1) * 128] = block[z * tr + t : z * tr + t + 1]
    settle(look_copies)
    for s in range(n_row):
        block = assemble(look_r, s)
        for u, turned in enumerate((right(block), block, left(block))):
            for z in range(2):
                for t in range(tr):
                    b = s * tr + t + 1
                    fld[2 * u + z : 2 * u + z + 1, b * 128 : (b + 1) * 128] = turned[z * tr + t : z * tr + t + 1]

    def taps(ref, at, width):
        three = [ref[:, at + t * 128 : at + t * 128 + width] for t in range(3)]
        return jnp.concatenate(three + [jnp.zeros((8, width), f32)], axis=0).astype(bf16)

    def turned_store(ref, value, at):
        for q in range(2):
            piece = value[:, q * 128 : (q + 1) * 128]
            lanes = slice(at + (q + 1) * 128, at + (q + 2) * 128)
            for u, turned in enumerate((right(piece), piece, left(piece))):
                ref[u * 128 : (u + 1) * 128, lanes] = turned.astype(bf16)

    for at in range(0, n, 256):
        pre1 = mm(w1_ref[...], taps(fld, at, 256))
        turned_store(i3a, rounded(jnp.maximum(pre1, 0.0)), at)

    def conv(w_ref, ref, at):
        total = 0.0
        for t in range(3):
            total = total + mm(w_ref[t], ref[:, at + t * 128 : at + t * 128 + 256])
        return total

    for at in range(0, n, 256):
        pre2 = conv(wf_ref, i3a, at) + bm_ref[...]
        h2 = jnp.maximum(pre2, 0.0).astype(bf16)
        h2s[:, at : at + 256] = h2
        tsum[:, at + 128 : at + 384] = mm(wp_ref[...], h2)

    wide_lane = lax.rem(lax.broadcasted_iota(jnp.int32, (1, n), 1), 128)
    wide_first, wide_last = wide_lane == 0, wide_lane == 127

    def wide_right(value):
        return jnp.where(wide_first, 0.0, pltpu.roll(value, 1, 1))

    def wide_left(value):
        return jnp.where(wide_last, 0.0, pltpu.roll(value, n - 1, 1))

    six = sum(tsum[8 * t : 8 * t + 8, t * 128 : t * 128 + n] for t in range(3))
    noise = wide_right(six)[0:2] + six[2:4] + wide_left(six)[4:6]
    den = fld[2:4, 128 : 128 + n] - noise
    for q in range(n_col):
        shifted = pltpu.roll(den, n - q * tc, 1) if q else den
        for s in range(n_row):
            for z in range(2):
                for t in range(tr):
                    i, b = z * tr + t, s * tr + t
                    outs[s * n_col + q, i : i + 1, :] = shifted[z : z + 1, b * 128 : (b + 1) * 128]
    den_copies = exchange(outs, den_ref, den_sem)
    dn = rounded((tfld[0:2, :] - den) * scale)
    dn3[0:2, 128 : 128 + n] = wide_right(dn)
    dn3[2:4, 128 : 128 + n] = dn
    dn3[4:6, 128 : 128 + n] = wide_left(dn)

    for at in range(0, n, 256):
        grad = mm(wpb_ref[...], taps(dn3, at, 256))
        grad = rounded(jnp.where(h2s[:, at : at + 256].astype(f32) > 0, grad, 0.0))
        turned_store(i3b, grad, at)

    sign = jnp.where(lane < 64, 1.0, -1.0)
    dp2 = i3b[128:256, 128 : 128 + n]
    for t in range(3):
        gram = mm_t(i3a[:, t * 128 : t * 128 + n], dp2)
        for u in range(3):
            upper = gram[u * 128 : u * 128 + 64]
            lower = gram[u * 128 + 64 : u * 128 + 128]
            x_ref[(3 * t + u) * 64 : (3 * t + u) * 64 + 64, :] = upper + sign * pltpu.roll(lower, 64, 1)
    x_ref[576:600, :] = mm_t(taps(dn3, 0, n), h2s[...])[0:24]
    x_ref[600:608, :] = mm_t(jnp.ones((16, n), bf16), dp2)[0:8]

    piece = plane_in.shape[1]

    def slot(ref, k):
        return ref.at[pl.ds(pl.multiple_of(k * piece, 8), piece)]

    scatter = []
    for k in range(1, n_plane):
        peer, where = plane_peer(k)
        scatter.append(remote(slot(x_ref, peer), plane_in.at[k], plane_sem, k, where))

    for at in range(0, n, 256):
        h1 = i3a[128:256, at + 128 : at + 384].astype(f32)
        grad = jnp.where(h1 > 0, conv(wb_ref, i3b, at), 0.0)
        dp1[:, at : at + 256] = grad.astype(bf16)

    small_in[me] = mm_t(taps(fld, 0, n), dp1[...])[0:24]
    small = [
        remote(small_in.at[me], small_in.at[me], small_sem, k, plane_peer(k)[1]) for k in range(1, n_plane)
    ]
    part = slot(x_ref, me)[...]
    for k, copy in zip(range(1, n_plane), scatter):
        copy.wait_recv()
        part = part + plane_in[k]
    date_in[d] = part
    spread = [remote(date_in.at[d], date_in.at[d], date_sem, k, date_peer(k)) for k in range(1, n_date)]

    def total(ref, count):
        return functools.reduce(lambda a, b: a + b, [ref[k] for k in range(count)])

    settle(small)
    small_date[d] = total(small_in, n_plane)
    small_spread = [
        remote(small_date.at[d], small_date.at[d], small_date_sem, k, date_peer(k)) for k in range(1, n_date)
    ]
    settle(spread)
    slot(o_ref, me)[...] = total(date_in, n_date)
    gather = [
        remote(slot(o_ref, me), slot(o_ref, me), gather_sem, k, plane_peer(k)[1])
        for k in range(1, n_plane)
    ]
    settle(small_spread)
    small_ref[...] = total(small_date, n_date)
    settle(den_copies)
    settle(gather)

    @pl.when(has_down)
    def _():
        for t in range(tr):
            own_slab(t).wait_send()

    @pl.when(has_down & has_one)
    def _():
        for t in range(tr):
            far_slab(t).wait_send()

    for copy in tgt_copies + look_copies + den_copies + scatter + small + spread + small_spread + gather:
        copy.wait_send()


def whole_finish(dims, den, sums, small, den_out, lift_out, lbias_out, mid_out, mbias_out, proj_out):
    n_plane, tr, tc, ch = dims
    for z in range(2):
        for t in range(tr):
            for k in range(n_plane):
                den_out[z, t, k : k + 1, :] = den[k, z * tr + t : z * tr + t + 1, 0:tc]
    finish_grads(ch, sums, small, lift_out, lbias_out, mid_out, mbias_out, proj_out)


def whole_local(slc, pairs, target, w_lift, b_lift, w_mid, b_mid, w_proj):
    n_row, n_col, n_date = (lax.axis_size(axis) for axis in ("row", "col", "date"))
    dates, srows, scols = slc.shape[1:]
    count, tr, tc = target.shape[1:]
    ch = w_mid.shape[-1]
    halves = scols // 128
    bf16, f32 = jnp.bfloat16, jnp.float32
    packed = slc.reshape(2, dates, srows, halves, 128).transpose(1, 0, 3, 2, 4)
    packed = packed.reshape(dates * 2 * halves, srows * 128)
    tgt = target.transpose(0, 2, 1, 3)
    w_lift, w_proj = w_lift.transpose(1, 2, 0, 3), w_proj.transpose(1, 2, 0, 3)
    scale = 1.0 / math.sqrt(2.0 * count * n_date * tr * n_row * tc * n_col)
    nb = n_row * tr
    n, wide = nb * 128, (nb + 2) * 128
    n_plane = n_row * n_col
    piece = -(-608 // (8 * n_plane)) * 8
    zt = -(-2 * tr // 8) * 8
    dma = pltpu.SemaphoreType.DMA
    vmem = pltpu.VMEM
    shape = jax.ShapeDtypeStruct
    den, sums, small = pl.pallas_call(
        functools.partial(whole_kernel, (n_row, n_col, n_date, dates, tr, tc), scale),
        out_shape=(
            shape((n_plane, zt, 128), f32),
            shape((n_plane * piece, 128), f32),
            shape((24, 128), f32),
        ),
        in_specs=[pl.BlockSpec(memory_space=vmem)] + [pl.BlockSpec(memory_space=pltpu.HBM)] * 7,
        out_specs=(pl.BlockSpec(memory_space=vmem),) * 3,
        scratch_shapes=[
            vmem((3 * packed.shape[0], packed.shape[1]), bf16),
            vmem((2, count), jnp.int32),
            vmem(tgt.shape, f32),
            vmem((n_plane, zt, 128), f32),
            vmem((n_plane, zt, 128), f32),
            vmem((n_plane, zt, 128), f32),
            vmem((n_plane, zt, 128), f32),
            vmem((8, wide), f32),
            vmem((8, n), f32),
            vmem((6 * ch, wide), bf16),
            vmem((6 * ch, wide), bf16),
            vmem((2 * ch, n), bf16),
            vmem((32, wide), f32),
            vmem((8, wide), f32),
            vmem((2 * ch, n), bf16),
            vmem((n_plane, zt, 128), f32),
            vmem((n_plane * piece, 128), f32),
            vmem(w_lift.shape, bf16),
            vmem(b_lift.shape, bf16),
            vmem(w_mid.shape, bf16),
            vmem(b_mid.shape, bf16),
            vmem(w_proj.shape, bf16),
            dma((7,)),
            vmem((2 * ch, 32), bf16),
            vmem((32, 2 * ch), bf16),
            vmem((2 * ch, 32), bf16),
            vmem((3, 2 * ch, 6 * ch), bf16),
            vmem((3, 2 * ch, 6 * ch), bf16),
            vmem((2 * ch, 1), f32),
            vmem((4, 128, 128), f32),
            vmem((n_plane, piece, 128), f32),
            vmem((n_date, piece, 128), f32),
            vmem((n_plane, 24, 128), f32),
            vmem((n_date, 24, 128), f32),
            dma((2, n_plane)),
            dma((2, n_date)),
            dma((2, 2 * tr)),
            dma((2, n_plane)),
            dma((2, n_plane)),
            dma((2, n_plane)),
            dma((2, n_plane)),
            dma((2, n_date)),
            dma((2, n_plane)),
        ],
        compiler_params=pltpu.CompilerParams(
            collective_id=0, has_side_effects=True, vmem_limit_bytes=48 * 1024 * 1024
        ),
    )(packed, pairs.T, tgt, w_lift, b_lift, w_mid, b_mid, w_proj)
    denoised, grad_lift, lift_bias, grad_mid, mid_bias, grad_proj = pl.pallas_call(
        functools.partial(whole_finish, (n_plane, tr, tc, ch)),
        out_shape=(
            shape((2, tr, count, tc), f32),
            shape((3, 3, 2, ch), f32),
            shape((2, ch), f32),
            shape((2, 3, 3, ch, ch), f32),
            shape((2, ch), f32),
            shape((3, 3, 2, ch), f32),
        ),
        in_specs=[pl.BlockSpec(memory_space=vmem)] * 3,
        out_specs=(pl.BlockSpec(memory_space=vmem),) * 6,
        compiler_params=pltpu.CompilerParams(vmem_limit_bytes=8 * 1024 * 1024),
    )(den, sums, small)
    return (
        denoised.transpose(0, 2, 1, 3),
        grad_lift.transpose(2, 0, 1, 3),
        lift_bias,
        grad_mid,
        mid_bias,
        grad_proj.transpose(2, 0, 1, 3),
    )


def local(slc, pairs, target, *weights):
    n_row, n_col = lax.axis_size("row"), lax.axis_size("col")
    count, tr, tc = target.shape[1:]
    whole = (
        count == n_row * n_col
        and tc * n_col == 128
        and (n_row * tr) % 2 == 0
        and 2 * tr <= 8
        and count == 8
        and (2 * slc.shape[1] * slc.shape[3] // 128) % 16 == 0
    )
    return (whole_local if whole else halo_local)(slc, pairs, target, *weights)


def solution(mesh):
    in_specs = (
        P(None, "date", "row", "col"),
        P("date", None),
        P(None, "date", "row", "col"),
        P(),
        P(),
        P(),
        P(),
        P(),
    )
    out_specs = (P(None, "date", "row", "col"), P(), P(), P(), P(), P())
    return jax.shard_map(local, mesh=mesh, in_specs=in_specs, out_specs=out_specs, check_vma=False)
```

```python
import functools
import math

import jax
import jax.numpy as jnp
from jax import lax
from jax.experimental import pallas as pl
from jax.experimental.pallas import tpu as pltpu
from jax.sharding import PartitionSpec as P

MESH = pl.DeviceIdType.MESH

LR = 2
LC = 4


def mm(a, b):
    return jnp.dot(a, b, preferred_element_type=jnp.float32)


def mm_t(a, b):
    return lax.dot_general(a, b, (((1,), (1,)), ((), ())), preferred_element_type=jnp.float32)


def step_kernel(
    dims, scale,
    slc_ref, pick_ref, avg_ref, tgt_ref, wl_any, bl_any, wmid_any, bmid_any, wproj_any,
    den_ref, o_ref, small_ref,
    pool, look_f, look_s, look_r, tgt_r, fld, tfld, i3a, i3b, h2s, tsum, dn3, dnm3, dp2m, dp1, outs, x_ref,
    wl_in, bl_in, wm_in, bm_in, wj_in, w_sem, w1_ref, wp_ref, wpb_ref, wf_ref, wb_ref, bm_ref, wtmp,
    plane_in, date_in, small_in, small_date, small_sem, small_date_sem, slab_sem, look_sem, tgt_sem, den_sem, plane_sem, date_sem, gather_sem,
):
    n_row, n_col, n_date, pp, tr, tc = dims
    r, c, d = lax.axis_index("row"), lax.axis_index("col"), lax.axis_index("date")
    n_plane = n_row * n_col
    me = r * n_col + c
    rows = n_row * tr
    gap = rows + 1
    nb = gap * pp
    n = nb * 128
    base = (128 - tc) // 2
    pairs = pp * n_row
    f32, bf16 = jnp.float32, jnp.bfloat16

    def plane_peer(k):
        peer = lax.rem(me + k, n_plane)
        return peer, (lax.div(peer, n_col), lax.rem(peer, n_col), d)

    def date_peer(k):
        return (r, c, lax.rem(d + k, n_date))

    def remote(src, dst, sems, at, where):
        copy = pltpu.make_async_remote_copy(
            src_ref=src, dst_ref=dst, send_sem=sems.at[0, at], recv_sem=sems.at[1, at],
            device_id=where, device_id_type=MESH,
        )
        copy.start()
        return copy

    fetches = []
    wide = zip((wl_any, bl_any, wmid_any, bmid_any, wproj_any), (wl_in, bl_in, wm_in, bm_in, wj_in))
    for k, (src, dst) in enumerate(wide):
        copy = pltpu.make_async_copy(src, dst, w_sem.at[k])
        copy.start()
        fetches.append(copy)
    barrier = pltpu.get_barrier_semaphore()
    for k in range(1, n_plane):
        pl.semaphore_signal(barrier, inc=1, device_id=plane_peer(k)[1], device_id_type=MESH)
    for k in range(1, n_date):
        pl.semaphore_signal(barrier, inc=1, device_id=date_peer(k), device_id_type=MESH)
    pl.semaphore_wait(barrier, n_plane + n_date - 2)

    sent = []
    slabs = [remote(slc_ref, pool.at[k - 1], slab_sem, k, date_peer(n_date - k)) for k in (1, 2)]

    def exchange(src, dst, sems):
        copies = []
        for way in range(3):
            col = lax.rem(c + (0, 1, n_col - 1)[way], n_col)
            for o in range(n_row):
                k = lax.rem(r + o, n_row)
                at = way * n_row + o
                if way == 0 and o == 0:
                    copy = pltpu.make_async_copy(src.at[k], dst.at[0, r], sems.at[0, at])
                    copy.start()
                    copies.append((copy, True))
                else:
                    copies.append((remote(src.at[k], dst.at[way, r], sems, at, (k, col, d)), False))
        return copies

    tgt_copies = exchange(tgt_ref, tgt_r, tgt_sem)
    for ref in (fld, tfld, dn3, dnm3, tsum):
        ref[...] = jnp.zeros_like(ref)
    edge = jnp.zeros((i3a.shape[0], 128), bf16)
    for ref in (i3a, i3b):
        ref[:, 0:128] = edge
        ref[:, (nb + 1) * 128 : (nb + 2) * 128] = edge
    x_ref[...] = jnp.zeros_like(x_ref)
    lane = lax.broadcasted_iota(jnp.int32, (1, 128), 1)
    spot = c * tc + lane - base
    inside = (spot >= 0) & (spot < n_col * tc)
    own = (lane >= base) & (lane < base + tc)
    for copy in fetches:
        copy.wait()
    wtmp[...] = jnp.zeros_like(wtmp)

    def joined(a, b):
        return jnp.concatenate([a, b], axis=1)

    for t in range(3):
        for u in range(3):
            pair = wl_in[t, u].astype(f32)
            at = 8 * t + 2 * u
            wtmp[0, at : at + 1, :] = joined(pair[0:1], pair[1:2])
            wtmp[0, at + 1 : at + 2, :] = joined(-pair[1:2], pair[0:1])
            pair = wj_in[t, u].astype(f32)
            real, imag = joined(pair[0:1], -pair[1:2]), joined(pair[1:2], pair[0:1])
            flip = 8 * (2 - t) + 2 * (2 - u)
            wtmp[1, at : at + 1, :] = real
            wtmp[1, at + 1 : at + 2, :] = imag
            wtmp[2, flip : flip + 1, :] = real
            wtmp[2, flip + 1 : flip + 2, :] = imag
            wr, wi = wm_in[0, t, u].astype(f32), wm_in[1, t, u].astype(f32)
            block = jnp.concatenate([joined(wr, wi), joined(-wi, wr)], axis=0)
            wb_ref[2 - t, :, (2 - u) * 128 : (3 - u) * 128] = block.astype(bf16)
            wf_ref[t, :, u * 128 : (u + 1) * 128] = block.T.astype(bf16)
    bias = bl_in[...].astype(f32)
    wtmp[0, 14:15, :] = joined(bias[0:1], bias[1:2])
    bias = bm_in[...].astype(f32)
    wtmp[3, 0:1, :] = joined(bias[0:1], bias[1:2])
    w1_ref[...] = wtmp[0].T[:, 0:32].astype(bf16)
    wp_ref[...] = wtmp[1, 0:32].astype(bf16)
    wpb_ref[...] = wtmp[2].T[:, 0:32].astype(bf16)
    bm_ref[...] = wtmp[3].T[:, 0:1]
    for copy in slabs:
        copy.wait_recv()
    sent += slabs

    depth = slc_ref.shape[0]
    picked = (
        mm(pick_ref[:, :depth], slc_ref[...])
        + mm(pick_ref[:, depth : 2 * depth], pool[0])
        + mm(pick_ref[:, 2 * depth :], pool[1])
    )
    parts = slc_ref.shape[1] // (LR * tr)
    halves = tc * LC // parts
    sides = []
    for h in range(halves):
        at = [picked[q * pairs : (q + 1) * pairs] for q in (h, halves + h, 2 * halves + h, 3 * halves + h)]
        a0, a1, b0, b1 = at
        rowsum = []
        for prod in (a0 * b0 + a1 * b1, a1 * b0 - a0 * b1):
            for t in range(tr):
                rowsum.append(
                    sum(prod[:, (t * LR + q) * parts : (t * LR + q + 1) * parts] for q in range(LR))
                )
        sides.append(jnp.concatenate(rowsum, axis=0))
    looked = jnp.dot(
        jnp.concatenate(sides, axis=1), avg_ref[...],
        precision=lax.Precision.HIGHEST, preferred_element_type=f32,
    )
    look_f[...] = jnp.zeros_like(look_f)
    for k in range(n_row):
        for q in range(2 * tr):
            look_f[k, q * pp : (q + 1) * pp, :] = looked[q * pairs + k * pp : q * pairs + (k + 1) * pp]
    look_s[...] = look_f[...].astype(bf16)
    look_copies = exchange(look_s, look_r, look_sem)

    def settle(copies):
        for copy, near in copies:
            if near:
                copy.wait()
            else:
                copy.wait_recv()
                sent.append(copy)

    def assemble(ref, s):
        mid = pltpu.roll(ref[0, s].astype(f32), base, 1)
        low = pltpu.roll(ref[1, s].astype(f32), (base - tc) % 128, 1)
        high = pltpu.roll(ref[2, s].astype(f32), base + tc, 1)
        joined = jnp.where(own, mid, jnp.where(lane < base, low, high))
        near = (lane >= base - 5) & (lane < base + tc + 5)
        return jnp.where(inside & near, joined, 0.0)

    settle(tgt_copies)
    for s in range(n_row):
        block = assemble(tgt_r, s)
        for z in range(2):
            for t in range(tr):
                for p in range(pp):
                    i = (z * tr + t) * pp + p
                    b = p * gap + s * tr + t
                    tfld[z : z + 1, b * 128 : (b + 1) * 128] = block[i : i + 1]
    settle(look_copies)
    for s in range(n_row):
        block = assemble(look_r, s)
        for u, turned in enumerate((pltpu.roll(block, 1, 1), block, pltpu.roll(block, 127, 1))):
            for z in range(2):
                for t in range(tr):
                    for p in range(pp):
                        i = (z * tr + t) * pp + p
                        b = p * gap + s * tr + t + 1
                        fld[2 * u + z : 2 * u + z + 1, b * 128 : (b + 1) * 128] = turned[i : i + 1]
    fld[6:7, :] = jnp.ones((1, (nb + 2) * 128), f32)

    def taps(ref, at, width):
        three = [ref[:, pl.ds(pl.multiple_of(at + t * 128, 128), width)] for t in range(3)]
        return jnp.concatenate(three + [jnp.zeros((8, width), f32)], axis=0).astype(bf16)

    def turned_store(ref, value, at):
        for u, turn in enumerate((1, 0, 127)):
            for q in range(2):
                piece = value[:, q * 128 : (q + 1) * 128]
                if turn:
                    piece = pltpu.roll(piece, turn, 1)
                ref[u * 128 : (u + 1) * 128, pl.ds(pl.multiple_of(at + (q + 1) * 128, 128), 128)] = (
                    piece.astype(bf16)
                )

    def good(b):
        one = [inside & (lax.rem(b + q, gap) != gap - 1) for q in range(2)]
        return jnp.concatenate(one, axis=1)

    own2 = jnp.concatenate([own, own], axis=1)

    def rounded(value):
        return value.astype(bf16).astype(f32)

    def lift(i, carry):
        at = pl.multiple_of(i * 256, 256)
        pre1 = mm(w1_ref[...], taps(fld, at, 256))
        turned_store(i3a, rounded(jnp.where(good(2 * i), jnp.maximum(pre1, 0.0), 0.0)), at)
        return carry

    lax.fori_loop(0, nb // 2, lift, 0, unroll=True)

    def conv(w_ref, ref, at):
        total = 0.0
        for t in range(3):
            total = total + mm(w_ref[t], ref[:, pl.ds(pl.multiple_of(at + t * 128, 128), 256)])
        return total

    def mid(i, carry):
        at = pl.multiple_of(i * 256, 256)
        pre2 = conv(wf_ref, i3a, at) + bm_ref[...]
        h2 = jnp.where(good(2 * i), jnp.maximum(pre2, 0.0), 0.0).astype(bf16)
        h2s[:, pl.ds(at, 256)] = h2
        tsum[:, pl.ds(pl.multiple_of(at + 128, 128), 256)] = mm(wp_ref[...], h2)
        return carry

    lax.fori_loop(0, nb // 2, mid, 0, unroll=True)

    six = sum(tsum[8 * t : 8 * t + 8, t * 128 : t * 128 + n] for t in range(3))
    noise = pltpu.roll(six, 1, 1)[0:2] + six[2:4] + pltpu.roll(six, n - 1, 1)[4:6]
    den = fld[2:4, 128 : 128 + n] - noise
    shifted = pltpu.roll(den, n - base, 1)
    outs[...] = jnp.zeros_like(outs)
    for s in range(n_row):
        for z in range(2):
            for t in range(tr):
                for p in range(pp):
                    i = (z * tr + t) * pp + p
                    b = p * gap + s * tr + t
                    outs[s, i : i + 1, :] = shifted[z : z + 1, b * 128 : (b + 1) * 128]
    den_copies = []
    for o in range(n_row):
        k = lax.rem(r + o, n_row)
        if o == 0:
            copy = pltpu.make_async_copy(outs.at[k], den_ref.at[r], den_sem.at[0, o])
            copy.start()
            den_copies.append((copy, True))
        else:
            den_copies.append((remote(outs.at[k], den_ref.at[r], den_sem, o, (k, c, d)), False))
    dn = rounded((tfld[0:2, :] - den) * scale)
    rowok = [jnp.full((1, 128), b % gap != gap - 1) for b in range(nb)]
    mask = jnp.concatenate([inside & ok for ok in rowok], axis=1)
    own_all = jnp.concatenate([own & ok for ok in rowok], axis=1)
    for ref, keep in ((dn3, mask), (dnm3, own_all)):
        kept = jnp.where(keep, dn, 0.0)
        ref[0:2, 128 : 128 + n] = pltpu.roll(kept, 1, 1)
        ref[2:4, 128 : 128 + n] = kept
        ref[4:6, 128 : 128 + n] = pltpu.roll(kept, n - 1, 1)

    def back2(i, carry):
        at = pl.multiple_of(i * 256, 256)
        grad = mm(wpb_ref[...], taps(dn3, at, 256))
        grad = rounded(jnp.where(h2s[:, pl.ds(at, 256)].astype(f32) > 0, grad, 0.0))
        turned_store(i3b, grad, at)
        dp2m[:, pl.ds(at, 256)] = jnp.where(own2, grad, 0.0).astype(bf16)
        return carry

    lax.fori_loop(0, nb // 2, back2, 0, unroll=True)

    sign = jnp.where(lane < 64, 1.0, -1.0)
    for t in range(3):
        gram = mm_t(i3a[:, t * 128 : t * 128 + n], dp2m[...])
        for u in range(3):
            upper = gram[u * 128 : u * 128 + 64]
            lower = gram[u * 128 + 64 : u * 128 + 128]
            x_ref[(3 * t + u) * 64 : (3 * t + u) * 64 + 64, :] = upper + sign * pltpu.roll(lower, 64, 1)
    x_ref[576:600, :] = mm_t(taps(dnm3, 0, n), h2s[...])[0:24]
    x_ref[600:608, :] = mm_t(jnp.ones((16, n), bf16), dp2m[...])[0:8]

    piece = plane_in.shape[1]

    def slot(ref, k):
        return ref.at[pl.ds(pl.multiple_of(k * piece, 8), piece)]

    scatter = []
    for k in range(1, n_plane):
        peer, where = plane_peer(k)
        scatter.append(remote(slot(x_ref, peer), plane_in.at[k], plane_sem, k, where))

    def back1(i, carry):
        at = pl.multiple_of(i * 256, 256)
        h1 = i3a[128:256, pl.ds(pl.multiple_of(at + 128, 128), 256)].astype(f32)
        grad = jnp.where((h1 > 0) & own2, conv(wb_ref, i3b, at), 0.0)
        dp1[:, pl.ds(at, 256)] = grad.astype(bf16)
        return carry

    lax.fori_loop(0, nb // 2, back1, 0, unroll=True)

    small_in[me] = mm_t(taps(fld, 0, n), dp1[...])[0:24]
    small = [
        remote(small_in.at[me], small_in.at[me], small_sem, k, plane_peer(k)[1]) for k in range(1, n_plane)
    ]
    part = slot(x_ref, me)[...]
    for k, copy in zip(range(1, n_plane), scatter):
        copy.wait_recv()
        part = part + plane_in[k]
    date_in[d] = part
    spread = [remote(date_in.at[d], date_in.at[d], date_sem, k, date_peer(k)) for k in range(1, n_date)]

    def total(ref, count):
        return functools.reduce(lambda a, b: a + b, [ref[k] for k in range(count)])

    for copy in small:
        copy.wait_recv()
    small_date[d] = total(small_in, n_plane)
    small_spread = [
        remote(small_date.at[d], small_date.at[d], small_date_sem, k, date_peer(k)) for k in range(1, n_date)
    ]
    for copy in spread:
        copy.wait_recv()
    slot(o_ref, me)[...] = total(date_in, n_date)
    gather = [
        remote(slot(o_ref, me), slot(o_ref, me), gather_sem, k, plane_peer(k)[1])
        for k in range(1, n_plane)
    ]
    for copy in small_spread:
        copy.wait_recv()
    small_ref[...] = total(small_date, n_date)
    settle(den_copies)
    for copy in gather:
        copy.wait_recv()
    for copy in sent + scatter + small + spread + small_spread + gather:
        copy.wait_send()


def finish_kernel(dims, den, sums, small, den_out, lift_out, lbias_out, mid_out, mbias_out, proj_out):
    n_row, pp, tr, tc, ch = dims
    for k in range(n_row):
        for z in range(2):
            for t in range(tr):
                at = (z * tr + t) * pp
                den_out[z, t, k * pp : (k + 1) * pp, :] = den[k, at : at + pp, 0:tc]
    finish_grads(ch, sums, small, lift_out, lbias_out, mid_out, mbias_out, proj_out)


def finish_grads(ch, sums, small, lift_out, lbias_out, mid_out, mbias_out, proj_out):
    for t in range(3):
        for u in range(3):
            at = 8 * t + 2 * u
            upper, lower = small[at : at + 1, :], small[at + 1 : at + 2, :]
            lift_out[t, u, 0:1, :] = upper[:, 0:ch] + lower[:, ch:]
            lift_out[t, u, 1:2, :] = upper[:, ch:] - lower[:, 0:ch]
            at = 576 + 8 * (2 - t) + 2 * (2 - u)
            upper, lower = sums[at : at + 1, :], sums[at + 1 : at + 2, :]
            proj_out[t, u, 0:1, :] = upper[:, 0:ch] + lower[:, ch:]
            proj_out[t, u, 1:2, :] = lower[:, 0:ch] - upper[:, ch:]
            at = (3 * t + u) * ch
            for z in range(2):
                mid_out[z, t, u] = sums[at : at + ch, z * ch : (z + 1) * ch]
    for z in range(2):
        lbias_out[z : z + 1, :] = small[14:15, z * ch : (z + 1) * ch]
        mbias_out[z : z + 1, :] = sums[600:601, z * ch : (z + 1) * ch]


def halo_local(slc, pairs, target, w_lift, b_lift, w_mid, b_mid, w_proj):
    n_row, n_col, n_date = (lax.axis_size(axis) for axis in ("row", "col", "date"))
    dates, srows, scols = slc.shape[1:]
    count, tr, tc = target.shape[1:]
    ch = w_mid.shape[-1]
    pp = count // n_row
    halves = scols // 128
    bf16, f32 = jnp.bfloat16, jnp.float32
    rows = 2 * tr * pp
    pad_rows = -(-rows // 16) * 16
    packed = slc.reshape(2, dates, srows, halves, 128).transpose(1, 0, 3, 2, 4)
    packed = packed.reshape(dates * 2 * halves, srows * 128)
    index = (pairs - lax.axis_index("date") * dates).T
    kinds = 2 * halves
    want = (index[:, None, :] * kinds + jnp.arange(kinds, dtype=jnp.int32)[None, :, None]).reshape(-1)
    pick = (want[:, None] == jnp.arange(3 * dates * kinds, dtype=jnp.int32)[None, :]).astype(bf16)
    spots = jnp.arange(scols, dtype=jnp.int32)[:, None] // LC
    avg = jnp.where(spots == jnp.arange(128, dtype=jnp.int32)[None, :], 1.0 / (LR * LC), 0.0).astype(f32)
    tgt = target.reshape(2, n_row, pp, tr, tc).transpose(1, 0, 3, 2, 4).reshape(n_row, rows, tc)
    tgt = jnp.pad(tgt, ((0, 0), (0, pad_rows - rows), (0, 128 - tc)))
    w_lift, w_proj = w_lift.transpose(1, 2, 0, 3), w_proj.transpose(1, 2, 0, 3)
    scale = 1.0 / math.sqrt(2.0 * count * n_date * tr * n_row * tc * n_col)
    nb = (n_row * tr + 1) * pp
    n, wide = nb * 128, (nb + 2) * 128
    n_plane = n_row * n_col
    piece = -(-608 // (8 * n_plane)) * 8
    dma = pltpu.SemaphoreType.DMA
    vmem = pltpu.VMEM
    den, sums, small = pl.pallas_call(
        functools.partial(step_kernel, (n_row, n_col, n_date, pp, tr, tc), scale),
        out_shape=(
            jax.ShapeDtypeStruct((n_row, pad_rows, 128), f32),
            jax.ShapeDtypeStruct((n_plane * piece, 128), f32),
            jax.ShapeDtypeStruct((24, 128), f32),
        ),
        in_specs=[pl.BlockSpec(memory_space=vmem)] * 4 + [pl.BlockSpec(memory_space=pl.ANY)] * 5,
        out_specs=(pl.BlockSpec(memory_space=vmem),) * 3,
        scratch_shapes=[
            vmem((2,) + packed.shape, bf16),
            vmem((n_row, pad_rows, 128), f32),
            vmem((n_row, pad_rows, 128), bf16),
            vmem((3, n_row, pad_rows, 128), bf16),
            vmem((3, n_row, pad_rows, 128), f32),
            vmem((8, wide), f32),
            vmem((8, n), f32),
            vmem((6 * ch, wide), bf16),
            vmem((6 * ch, wide), bf16),
            vmem((2 * ch, n), bf16),
            vmem((32, wide), f32),
            vmem((8, wide), f32),
            vmem((8, wide), f32),
            vmem((2 * ch, n), bf16),
            vmem((2 * ch, n), bf16),
            vmem((n_row, pad_rows, 128), f32),
            vmem((n_plane * piece, 128), f32),
            vmem(w_lift.shape, bf16),
            vmem(b_lift.shape, bf16),
            vmem(w_mid.shape, bf16),
            vmem(b_mid.shape, bf16),
            vmem(w_proj.shape, bf16),
            dma((5,)),
            vmem((2 * ch, 32), bf16),
            vmem((32, 2 * ch), bf16),
            vmem((2 * ch, 32), bf16),
            vmem((3, 2 * ch, 6 * ch), bf16),
            vmem((3, 2 * ch, 6 * ch), bf16),
            vmem((2 * ch, 1), f32),
            vmem((4, 128, 128), f32),
            vmem((n_plane, piece, 128), f32),
            vmem((n_date, piece, 128), f32),
            vmem((n_plane, 24, 128), f32),
            vmem((n_date, 24, 128), f32),
            dma((2, n_plane)),
            dma((2, n_date)),
            dma((2, 3)),
            dma((2, 3 * n_row)),
            dma((2, 3 * n_row)),
            dma((2, n_row)),
            dma((2, n_plane)),
            dma((2, n_date)),
            dma((2, n_plane)),
        ],
        compiler_params=pltpu.CompilerParams(
            collective_id=0, has_side_effects=True, vmem_limit_bytes=48 * 1024 * 1024
        ),
    )(packed, pick, avg, tgt, w_lift, b_lift, w_mid, b_mid, w_proj)
    shape = jax.ShapeDtypeStruct
    denoised, grad_lift, lift_bias, grad_mid, mid_bias, grad_proj = pl.pallas_call(
        functools.partial(finish_kernel, (n_row, pp, tr, tc, ch)),
        out_shape=(
            shape((2, tr, count, tc), f32),
            shape((3, 3, 2, ch), f32),
            shape((2, ch), f32),
            shape((2, 3, 3, ch, ch), f32),
            shape((2, ch), f32),
            shape((3, 3, 2, ch), f32),
        ),
        in_specs=[pl.BlockSpec(memory_space=vmem)] * 3,
        out_specs=(pl.BlockSpec(memory_space=vmem),) * 6,
        compiler_params=pltpu.CompilerParams(vmem_limit_bytes=8 * 1024 * 1024),
    )(den, sums, small)
    return (
        denoised.transpose(0, 2, 1, 3),
        grad_lift.transpose(2, 0, 1, 3),
        lift_bias,
        grad_mid,
        mid_bias,
        grad_proj.transpose(2, 0, 1, 3),
    )


def whole_kernel(
    dims, scale,
    slc_ref, idx_any, tgt_any, wl_any, bl_any, wmid_any, bmid_any, wproj_any,
    den_ref, o_ref,
    pool, idx_in, tgt_in, look_s, look_r, tgt_s, tgt_r, fld, tfld, i3a, i3b, h2s, tsum, dn3, dp1, outs, x_ref,
    wl_in, bl_in, wm_in, bm_in, wj_in, w_sem, w1_ref, wp_ref, wpb_ref, wf_ref, wb_ref, bm_ref, wtmp,
    plane_in, date_in, slab_sem, look_sem, tgt_sem, den_sem, sum_sem,
):
    n_row, n_col, n_date, dates, tr, tc = dims
    r, c, d = lax.axis_index("row"), lax.axis_index("col"), lax.axis_index("date")
    n_plane = n_row * n_col
    me = r * n_col + c
    pairs = n_plane
    nb = n_row * tr
    n = nb * 128
    wide = n + 256
    f32, bf16 = jnp.float32, jnp.bfloat16

    def wrapped(value, size):
        return jnp.where(value >= size, value - size, value)

    plane_peers = []
    for k in range(1, n_plane):
        row, col = wrapped(r + k // n_col, n_row), wrapped(c + k % n_col, n_col)
        plane_peers.append((row * n_col + col, (row, col, d)))
    date_peers = [(r, c, wrapped(d + k, n_date)) for k in range(1, n_date)]

    def remote_of(src, dst, send_sem, recv_sem, where):
        return pltpu.make_async_remote_copy(
            src_ref=src, dst_ref=dst, send_sem=send_sem, recv_sem=recv_sem,
            device_id=where, device_id_type=MESH,
        )

    def wait_bytes(ref, sem):
        pltpu.make_async_copy(ref, ref, sem).wait()

    barrier = pltpu.get_barrier_semaphore()
    for where in date_peers + [where for _, where in plane_peers]:
        pl.semaphore_signal(barrier, inc=1, device_id=where, device_id_type=MESH)
    fetches = []
    wide_in = zip(
        (idx_any, tgt_any, wl_any, bl_any, wmid_any, bmid_any, wproj_any),
        (idx_in, tgt_in, wl_in, bl_in, wm_in, bm_in, wj_in),
    )
    for k, (src, dst) in enumerate(wide_in):
        copy = pltpu.make_async_copy(src, dst, w_sem.at[min(k, 2)])
        copy.start()
        fetches.append(copy)
    pl.semaphore_wait(barrier, n_plane + n_date - 2)

    slab = slc_ref.shape[0]
    chunk = LR * 128
    def slab_copy(way, t):
        lanes = pl.ds(t * chunk, chunk)
        where = (r, c, lax.max(d - way, 0))
        return remote_of(slc_ref.at[:, lanes], pool.at[pl.ds(way * slab, slab), lanes], slab_sem.at[way - 1], slab_sem.at[2 + (way - 1) * tr + t], where)

    sends = (d > 0, d > 1)
    gets = (d < n_date - 1, d < n_date - 2)
    for t in range(tr):
        for way in (2, 1):

            @pl.when(sends[way - 1])
            def _():
                slab_copy(way, t).start()

    @pl.when(jnp.logical_not(gets[0]))
    def _():
        pool[slab : 2 * slab, :] = jnp.zeros((slab, tr * chunk), bf16)

    @pl.when(jnp.logical_not(gets[1]))
    def _():
        pool[2 * slab : 3 * slab, :] = jnp.zeros((slab, tr * chunk), bf16)

    pool[0:slab, :] = slc_ref[...]
    for ref in (fld, tfld, dn3, tsum, tgt_s, look_s):
        ref[...] = jnp.zeros_like(ref)
    edge = jnp.zeros((i3a.shape[0], 128), bf16)
    for ref in (i3a, i3b):
        ref[:, 0:128] = edge
        ref[:, (nb + 1) * 128 : (nb + 2) * 128] = edge
    x_ref[632:, :] = jnp.zeros((x_ref.shape[0] - 632, 128), f32)
    outs[...] = jnp.zeros_like(outs)
    lane = lax.broadcasted_iota(jnp.int32, (1, 128), 1)
    for copy in fetches[:2]:
        copy.wait()

    def to_lane(value):
        return pltpu.roll(jnp.concatenate([value, jnp.zeros((value.shape[0], 128 - tc), f32)], axis=1), c * tc, 1)

    for z in range(2):
        for t in range(tr):
            block = to_lane(tgt_in[z, t])
            for k in range(pairs):
                tgt_s[k, z * tr + t : z * tr + t + 1, :] = block[k : k + 1]

    def exchange(src, dst, sems):
        dst[me] = src[me]
        for peer, where in plane_peers:
            remote_of(src.at[peer], dst.at[me], sems.at[0], sems.at[1], where).start()

    def arrived(dst, sems):
        wait_bytes(dst.at[pl.ds(0, n_plane - 1)], sems.at[1])

    def departed(src, sems):
        wait_bytes(src.at[pl.ds(0, n_plane - 1)], sems.at[0])

    halves = tc * LC // 128
    kinds = 2 * halves
    index = idx_in[...] - d * dates
    spread_lanes = jnp.concatenate([index[0:1]] * kinds + [index[1:2]] * kinds, axis=1)
    row_of = lax.broadcasted_iota(jnp.int32, (slab, 2 * kinds * pairs), 0)
    lane_of = lax.broadcasted_iota(jnp.int32, (slab, 2 * kinds * pairs), 1)
    same_kind = lax.rem(row_of, kinds) == lax.rem(lax.div(lane_of, pairs), kinds)
    picks = []
    for s in range(3):
        hit = same_kind & (lax.div(row_of, kinds) + s * dates == spread_lanes)
        picks.append(jnp.where(hit, 1.0, 0.0).astype(f32))
    pick = jnp.concatenate(picks, axis=0).T.astype(bf16)
    spots = lax.broadcasted_iota(jnp.int32, (tc * LC, 128), 0)
    avg_lane = lax.broadcasted_iota(jnp.int32, (tc * LC, 128), 1)
    avg = jnp.where(lax.div(spots, LC) + c * tc == avg_lane, 1.0 / (LR * LC), 0.0).astype(f32)

    exchange(tgt_s, tgt_r, tgt_sem)

    for copy in fetches[2:]:
        copy.wait()
    wtmp[...] = jnp.zeros_like(wtmp)

    def joined(a, b):
        return jnp.concatenate([a, b], axis=1)

    for t in range(3):
        for u in range(3):
            pair = wl_in[t, u].astype(f32)
            at = 8 * t + 2 * u
            wtmp[0, at : at + 1, :] = joined(pair[0:1], pair[1:2])
            wtmp[0, at + 1 : at + 2, :] = joined(-pair[1:2], pair[0:1])
            pair = wj_in[t, u].astype(f32)
            real, imag = joined(pair[0:1], -pair[1:2]), joined(pair[1:2], pair[0:1])
            flip = 8 * (2 - t) + 2 * (2 - u)
            wtmp[1, at : at + 1, :] = real
            wtmp[1, at + 1 : at + 2, :] = imag
            wtmp[2, flip : flip + 1, :] = real
            wtmp[2, flip + 1 : flip + 2, :] = imag
            wr, wi = wm_in[0, t, u].astype(f32), wm_in[1, t, u].astype(f32)
            block = jnp.concatenate([joined(wr, wi), joined(-wi, wr)], axis=0)
            wb_ref[2 - t, :, (2 - u) * 128 : (3 - u) * 128] = block.astype(bf16)
            wf_ref[t, :, u * 128 : (u + 1) * 128] = block.T.astype(bf16)
    bias = bl_in[...].astype(f32)
    wtmp[0, 14:15, :] = joined(bias[0:1], bias[1:2])
    bias = bm_in[...].astype(f32)
    wtmp[3, 0:1, :] = joined(bias[0:1], bias[1:2])
    w1_ref[...] = wtmp[0].T[:, 0:32].astype(bf16)
    wp_ref[...] = wtmp[1, 0:32].astype(bf16)
    wpb_ref[...] = wtmp[2].T[:, 0:32].astype(bf16)
    bm_ref[...] = wtmp[3].T[:, 0:1]
    fld[6:7, :] = jnp.ones((1, wide), f32)

    def rounded(value):
        return value.astype(bf16).astype(f32)

    for t in range(tr):

        for way in (1, 2):

            @pl.when(gets[way - 1])
            def _():
                slab_copy(way, t).wait_recv()

        picked = mm(pick, pool[:, t * chunk : (t + 1) * chunk])
        sides = []
        for h in range(halves):
            a0, a1, b0, b1 = [picked[q * pairs : (q + 1) * pairs] for q in (h, halves + h, 2 * halves + h, 3 * halves + h)]
            both = []
            for prod in (a0 * b0 + a1 * b1, a1 * b0 - a0 * b1):
                both.append(sum(prod[:, q * 128 : (q + 1) * 128] for q in range(LR)))
            sides.append(jnp.concatenate(both, axis=0))
        looked = rounded(
            jnp.dot(
                jnp.concatenate(sides, axis=1), avg,
                precision=lax.Precision.HIGHEST, preferred_element_type=f32,
            )
        )
        for z in range(2):
            for k in range(pairs):
                at = z * tr + t
                look_s[k, at : at + 1, :] = looked[z * pairs + k : z * pairs + k + 1]
    exchange(look_s, look_r, look_sem)

    first, last = lane == 0, lane == 127

    def right(value):
        return jnp.where(first, 0.0, pltpu.roll(value, 1, 1))

    def left(value):
        return jnp.where(last, 0.0, pltpu.roll(value, 127, 1))

    def assemble(ref, s):
        return functools.reduce(lambda a, b: a + b, [ref[s * n_col + q] for q in range(n_col)])

    arrived(tgt_r, tgt_sem)
    for s in range(n_row):
        block = assemble(tgt_r, s)
        for z in range(2):
            for t in range(tr):
                b = s * tr + t
                tfld[z : z + 1, b * 128 : (b + 1) * 128] = block[z * tr + t : z * tr + t + 1]
    arrived(look_r, look_sem)
    for s in range(n_row):
        block = assemble(look_r, s)
        for u, turned in enumerate((right(block), block, left(block))):
            for z in range(2):
                for t in range(tr):
                    b = s * tr + t + 1
                    fld[2 * u + z : 2 * u + z + 1, b * 128 : (b + 1) * 128] = turned[z * tr + t : z * tr + t + 1]

    def taps(ref, at, width):
        three = [ref[:, at + t * 128 : at + t * 128 + width] for t in range(3)]
        return jnp.concatenate(three + [jnp.zeros((8, width), f32)], axis=0).astype(bf16)

    def turned_store(ref, value, at):
        for q in range(2):
            piece = value[:, q * 128 : (q + 1) * 128]
            lanes = slice(at + (q + 1) * 128, at + (q + 2) * 128)
            for u, turned in enumerate((right(piece), piece, left(piece))):
                ref[u * 128 : (u + 1) * 128, lanes] = turned.astype(bf16)

    for at in range(0, n, 256):
        pre1 = mm(w1_ref[...], taps(fld, at, 256))
        turned_store(i3a, rounded(jnp.maximum(pre1, 0.0)), at)

    def conv(w_ref, ref, at):
        total = 0.0
        for t in range(3):
            total = total + mm(w_ref[t], ref[:, at + t * 128 : at + t * 128 + 256])
        return total

    for at in range(0, n, 256):
        pre2 = conv(wf_ref, i3a, at) + bm_ref[...]
        h2 = jnp.maximum(pre2, 0.0).astype(bf16)
        h2s[:, at : at + 256] = h2
        tsum[:, at + 128 : at + 384] = mm(wp_ref[...], h2)

    wide_lane = lax.rem(lax.broadcasted_iota(jnp.int32, (1, n), 1), 128)
    wide_first, wide_last = wide_lane == 0, wide_lane == 127

    def wide_right(value):
        return jnp.where(wide_first, 0.0, pltpu.roll(value, 1, 1))

    def wide_left(value):
        return jnp.where(wide_last, 0.0, pltpu.roll(value, n - 1, 1))

    six = sum(tsum[8 * t : 8 * t + 8, t * 128 : t * 128 + n] for t in range(3))
    noise = wide_right(six)[0:2] + six[2:4] + wide_left(six)[4:6]
    den = fld[2:4, 128 : 128 + n] - noise
    for q in range(n_col):
        shifted = pltpu.roll(den, n - q * tc, 1) if q else den
        for s in range(n_row):
            for z in range(2):
                for t in range(tr):
                    i, b = z * tr + t, s * tr + t
                    outs[s * n_col + q, i : i + 1, :] = shifted[z : z + 1, b * 128 : (b + 1) * 128]
    exchange(outs, den_ref, den_sem)
    dn = rounded((tfld[0:2, :] - den) * scale)
    dn3[0:2, 128 : 128 + n] = wide_right(dn)
    dn3[2:4, 128 : 128 + n] = dn
    dn3[4:6, 128 : 128 + n] = wide_left(dn)

    for at in range(0, n, 256):
        grad = mm(wpb_ref[...], taps(dn3, at, 256))
        grad = rounded(jnp.where(h2s[:, at : at + 256].astype(f32) > 0, grad, 0.0))
        turned_store(i3b, grad, at)

    sizes = (192, 192, 192, 64)
    bases = (0, 192, 384, 576)
    per = [size // n_plane for size in sizes]
    count = len(sizes)

    def piece(ref, j, at):
        return ref.at[pl.ds(pl.multiple_of(bases[j] + at * per[j], 8), per[j])]

    def scatter(j):
        for k, (peer, where) in enumerate(plane_peers):
            dst = plane_in.at[j * n_plane + k, pl.ds(0, per[j])]
            remote_of(piece(x_ref, j, peer), dst, sum_sem.at[0], sum_sem.at[3 + j], where).start()

    def across(j):
        wait_bytes(plane_in.at[pl.ds(j * n_plane, n_plane - 1), pl.ds(0, per[j])], sum_sem.at[3 + j])
        part = piece(x_ref, j, me)[...]
        for k in range(n_plane - 1):
            part = part + plane_in[j * n_plane + k, 0 : per[j]]
        slot = date_in.at[j * n_date + d, pl.ds(0, per[j])]
        slot[...] = part
        for where in date_peers:
            remote_of(slot, slot, sum_sem.at[1], sum_sem.at[3 + count + j], where).start()

    def spread(j):
        wait_bytes(date_in.at[pl.ds(j * n_date, n_date - 1), pl.ds(0, per[j])], sum_sem.at[3 + count + j])
        mine = piece(o_ref, j, me)
        mine[...] = functools.reduce(lambda a, b: a + b, [date_in[j * n_date + k, 0 : per[j]] for k in range(n_date)])
        for _, where in plane_peers:
            remote_of(mine, mine, sum_sem.at[2], sum_sem.at[3 + 2 * count + j], where).start()

    sign = jnp.where(lane < 64, 1.0, -1.0)
    dp2 = i3b[128:256, 128 : 128 + n]
    for t in range(3):
        gram = mm_t(i3a[:, t * 128 : t * 128 + n], dp2)
        for u in range(3):
            upper = gram[u * 128 : u * 128 + 64]
            lower = gram[u * 128 + 64 : u * 128 + 128]
            x_ref[(3 * t + u) * 64 : (3 * t + u) * 64 + 64, :] = upper + sign * pltpu.roll(lower, 64, 1)
        scatter(t)

    def back1(at):
        h1 = i3a[128:256, at + 128 : at + 384].astype(f32)
        grad = jnp.where(h1 > 0, conv(wb_ref, i3b, at), 0.0)
        dp1[:, at : at + 256] = grad.astype(bf16)

    x_ref[576:600, :] = mm_t(taps(dn3, 0, n), h2s[...])[0:24]
    x_ref[600:608, :] = mm_t(jnp.ones((16, n), bf16), dp2)[0:8]
    for at in range(0, n, 256):
        back1(at)
    x_ref[608:632, :] = mm_t(taps(fld, 0, n), dp1[...])[0:24]
    scatter(3)
    for j in range(count):
        across(j)
    for j in range(count):
        spread(j)
    arrived(den_ref, den_sem)
    for j in range(count):
        wait_bytes(o_ref.at[pl.ds(0, (n_plane - 1) * per[j])], sum_sem.at[3 + 2 * count + j])
    for way in (1, 2):

        @pl.when(sends[way - 1])
        def _():
            wait_bytes(slc_ref, slab_sem.at[way - 1])

    departed(tgt_s, tgt_sem)
    departed(look_s, look_sem)
    departed(outs, den_sem)
    for q, rows in enumerate(((n_plane - 1) * sum(per), (n_date - 1) * sum(per), (n_plane - 1) * sum(per))):
        wait_bytes(x_ref.at[pl.ds(0, rows)], sum_sem.at[q])


def whole_finish(dims, den, sums, den_out, lift_out, lbias_out, mid_out, mbias_out, proj_out):
    n_plane, tr, tc, ch = dims
    for z in range(2):
        for t in range(tr):
            for k in range(n_plane):
                den_out[z, t, k : k + 1, :] = den[k, z * tr + t : z * tr + t + 1, 0:tc]
    finish_grads(ch, sums, sums.at[608:632], lift_out, lbias_out, mid_out, mbias_out, proj_out)


def whole_local(slc, pairs, target, w_lift, b_lift, w_mid, b_mid, w_proj):
    n_row, n_col, n_date = (lax.axis_size(axis) for axis in ("row", "col", "date"))
    dates, srows, scols = slc.shape[1:]
    count, tr, tc = target.shape[1:]
    ch = w_mid.shape[-1]
    halves = scols // 128
    bf16, f32 = jnp.bfloat16, jnp.float32
    packed = slc.reshape(2, dates, srows, halves, 128).transpose(1, 0, 3, 2, 4)
    packed = packed.reshape(dates * 2 * halves, srows * 128)
    tgt = target.transpose(0, 2, 1, 3)
    w_lift, w_proj = w_lift.transpose(1, 2, 0, 3), w_proj.transpose(1, 2, 0, 3)
    scale = 1.0 / math.sqrt(2.0 * count * n_date * tr * n_row * tc * n_col)
    nb = n_row * tr
    n, wide = nb * 128, (nb + 2) * 128
    n_plane = n_row * n_col
    zt = -(-2 * tr // 8) * 8
    dma = pltpu.SemaphoreType.DMA
    vmem = pltpu.VMEM
    shape = jax.ShapeDtypeStruct
    den, sums = pl.pallas_call(
        functools.partial(whole_kernel, (n_row, n_col, n_date, dates, tr, tc), scale),
        out_shape=(
            shape((n_plane, zt, 128), f32),
            shape((640, 128), f32),
        ),
        in_specs=[pl.BlockSpec(memory_space=vmem)] + [pl.BlockSpec(memory_space=pltpu.HBM)] * 7,
        out_specs=(pl.BlockSpec(memory_space=vmem),) * 2,
        scratch_shapes=[
            vmem((3 * packed.shape[0], packed.shape[1]), bf16),
            vmem((2, count), jnp.int32),
            vmem(tgt.shape, f32),
            vmem((n_plane, zt, 128), f32),
            vmem((n_plane, zt, 128), f32),
            vmem((n_plane, zt, 128), f32),
            vmem((n_plane, zt, 128), f32),
            vmem((8, wide), f32),
            vmem((8, n), f32),
            vmem((6 * ch, wide), bf16),
            vmem((6 * ch, wide), bf16),
            vmem((2 * ch, n), bf16),
            vmem((32, wide), f32),
            vmem((8, wide), f32),
            vmem((2 * ch, n), bf16),
            vmem((n_plane, zt, 128), f32),
            vmem((640, 128), f32),
            vmem(w_lift.shape, bf16),
            vmem(b_lift.shape, bf16),
            vmem(w_mid.shape, bf16),
            vmem(b_mid.shape, bf16),
            vmem(w_proj.shape, bf16),
            dma((3,)),
            vmem((2 * ch, 32), bf16),
            vmem((32, 2 * ch), bf16),
            vmem((2 * ch, 32), bf16),
            vmem((3, 2 * ch, 6 * ch), bf16),
            vmem((3, 2 * ch, 6 * ch), bf16),
            vmem((2 * ch, 1), f32),
            vmem((4, 128, 128), f32),
            vmem((4 * n_plane, 24, 128), f32),
            vmem((4 * n_date, 24, 128), f32),
            dma((2 + 2 * tr,)),
            dma((2,)),
            dma((2,)),
            dma((2,)),
            dma((15,)),
        ],
        compiler_params=pltpu.CompilerParams(
            collective_id=0, has_side_effects=True, vmem_limit_bytes=48 * 1024 * 1024
        ),
    )(packed, pairs.T, tgt, w_lift, b_lift, w_mid, b_mid, w_proj)
    denoised, grad_lift, lift_bias, grad_mid, mid_bias, grad_proj = pl.pallas_call(
        functools.partial(whole_finish, (n_plane, tr, tc, ch)),
        out_shape=(
            shape((2, tr, count, tc), f32),
            shape((3, 3, 2, ch), f32),
            shape((2, ch), f32),
            shape((2, 3, 3, ch, ch), f32),
            shape((2, ch), f32),
            shape((3, 3, 2, ch), f32),
        ),
        in_specs=[pl.BlockSpec(memory_space=vmem)] * 2,
        out_specs=(pl.BlockSpec(memory_space=vmem),) * 6,
        compiler_params=pltpu.CompilerParams(vmem_limit_bytes=8 * 1024 * 1024),
    )(den, sums)
    return (
        denoised.transpose(0, 2, 1, 3),
        grad_lift.transpose(2, 0, 1, 3),
        lift_bias,
        grad_mid,
        mid_bias,
        grad_proj.transpose(2, 0, 1, 3),
    )


def local(slc, pairs, target, w_lift, b_lift, w_mid, b_mid, w_proj):
    n_row, n_col = lax.axis_size("row"), lax.axis_size("col")
    count, tr, tc = target.shape[1:]
    whole = (
        count == n_row * n_col
        and tc * n_col == 128
        and (n_row * tr) % 2 == 0
        and 2 * tr <= 8
        and count == 8
        and n_row % 2 == 0
        and w_mid.shape[-1] == 64
        and (2 * slc.shape[1] * slc.shape[3] // 128) % 16 == 0
    )
    return (whole_local if whole else halo_local)(
        slc, pairs, target, w_lift, b_lift, w_mid, b_mid, w_proj
    )


def solution(mesh):
    in_specs = (
        P(None, "date", "row", "col"),
        P("date", None),
        P(None, "date", "row", "col"),
        P(),
        P(),
        P(),
        P(),
        P(),
    )
    out_specs = (P(None, "date", "row", "col"), P(), P(), P(), P(), P())
    return jax.shard_map(local, mesh=mesh, in_specs=in_specs, out_specs=out_specs, check_vma=False)
```

```python
import functools
import math

import jax
import jax.numpy as jnp
from jax import lax
from jax.experimental import pallas as pl
from jax.experimental.pallas import tpu as pltpu
from jax.sharding import PartitionSpec as P

MESH = pl.DeviceIdType.MESH

LR = 2
LC = 4


def mm(a, b):
    return jnp.dot(a, b, preferred_element_type=jnp.float32)


def mm_t(a, b):
    return lax.dot_general(a, b, (((1,), (1,)), ((), ())), preferred_element_type=jnp.float32)


def step_kernel(
    dims, scale,
    slc_ref, pick_ref, avg_ref, tgt_ref, wl_any, bl_any, wmid_any, bmid_any, wproj_any,
    den_ref, o_ref, small_ref,
    pool, look_f, look_s, look_r, tgt_r, fld, tfld, i3a, i3b, h2s, tsum, dn3, dnm3, dp2m, dp1, outs, x_ref,
    wl_in, bl_in, wm_in, bm_in, wj_in, w_sem, w1_ref, wp_ref, wpb_ref, wf_ref, wb_ref, bm_ref, wtmp,
    plane_in, date_in, small_in, small_date, small_sem, small_date_sem, slab_sem, look_sem, tgt_sem, den_sem, plane_sem, date_sem, gather_sem,
):
    n_row, n_col, n_date, pp, tr, tc = dims
    r, c, d = lax.axis_index("row"), lax.axis_index("col"), lax.axis_index("date")
    n_plane = n_row * n_col
    me = r * n_col + c
    rows = n_row * tr
    gap = rows + 1
    nb = gap * pp
    n = nb * 128
    base = (128 - tc) // 2
    pairs = pp * n_row
    f32, bf16 = jnp.float32, jnp.bfloat16

    def plane_peer(k):
        peer = lax.rem(me + k, n_plane)
        return peer, (lax.div(peer, n_col), lax.rem(peer, n_col), d)

    def date_peer(k):
        return (r, c, lax.rem(d + k, n_date))

    def remote(src, dst, sems, at, where):
        copy = pltpu.make_async_remote_copy(
            src_ref=src, dst_ref=dst, send_sem=sems.at[0, at], recv_sem=sems.at[1, at],
            device_id=where, device_id_type=MESH,
        )
        copy.start()
        return copy

    fetches = []
    wide = zip((wl_any, bl_any, wmid_any, bmid_any, wproj_any), (wl_in, bl_in, wm_in, bm_in, wj_in))
    for k, (src, dst) in enumerate(wide):
        copy = pltpu.make_async_copy(src, dst, w_sem.at[k])
        copy.start()
        fetches.append(copy)
    barrier = pltpu.get_barrier_semaphore()
    for k in range(1, n_plane):
        pl.semaphore_signal(barrier, inc=1, device_id=plane_peer(k)[1], device_id_type=MESH)
    for k in range(1, n_date):
        pl.semaphore_signal(barrier, inc=1, device_id=date_peer(k), device_id_type=MESH)
    pl.semaphore_wait(barrier, n_plane + n_date - 2)

    sent = []
    slabs = [remote(slc_ref, pool.at[k - 1], slab_sem, k, date_peer(n_date - k)) for k in (1, 2)]

    def exchange(src, dst, sems):
        copies = []
        for way in range(3):
            col = lax.rem(c + (0, 1, n_col - 1)[way], n_col)
            for o in range(n_row):
                k = lax.rem(r + o, n_row)
                at = way * n_row + o
                if way == 0 and o == 0:
                    copy = pltpu.make_async_copy(src.at[k], dst.at[0, r], sems.at[0, at])
                    copy.start()
                    copies.append((copy, True))
                else:
                    copies.append((remote(src.at[k], dst.at[way, r], sems, at, (k, col, d)), False))
        return copies

    tgt_copies = exchange(tgt_ref, tgt_r, tgt_sem)
    for ref in (fld, tfld, dn3, dnm3, tsum):
        ref[...] = jnp.zeros_like(ref)
    edge = jnp.zeros((i3a.shape[0], 128), bf16)
    for ref in (i3a, i3b):
        ref[:, 0:128] = edge
        ref[:, (nb + 1) * 128 : (nb + 2) * 128] = edge
    x_ref[...] = jnp.zeros_like(x_ref)
    lane = lax.broadcasted_iota(jnp.int32, (1, 128), 1)
    spot = c * tc + lane - base
    inside = (spot >= 0) & (spot < n_col * tc)
    own = (lane >= base) & (lane < base + tc)
    for copy in fetches:
        copy.wait()
    wtmp[...] = jnp.zeros_like(wtmp)

    def joined(a, b):
        return jnp.concatenate([a, b], axis=1)

    for t in range(3):
        for u in range(3):
            pair = wl_in[t, u].astype(f32)
            at = 8 * t + 2 * u
            wtmp[0, at : at + 1, :] = joined(pair[0:1], pair[1:2])
            wtmp[0, at + 1 : at + 2, :] = joined(-pair[1:2], pair[0:1])
            pair = wj_in[t, u].astype(f32)
            real, imag = joined(pair[0:1], -pair[1:2]), joined(pair[1:2], pair[0:1])
            flip = 8 * (2 - t) + 2 * (2 - u)
            wtmp[1, at : at + 1, :] = real
            wtmp[1, at + 1 : at + 2, :] = imag
            wtmp[2, flip : flip + 1, :] = real
            wtmp[2, flip + 1 : flip + 2, :] = imag
            wr, wi = wm_in[0, t, u].astype(f32), wm_in[1, t, u].astype(f32)
            block = jnp.concatenate([joined(wr, wi), joined(-wi, wr)], axis=0)
            wb_ref[2 - t, :, (2 - u) * 128 : (3 - u) * 128] = block.astype(bf16)
            wf_ref[t, :, u * 128 : (u + 1) * 128] = block.T.astype(bf16)
    bias = bl_in[...].astype(f32)
    wtmp[0, 14:15, :] = joined(bias[0:1], bias[1:2])
    bias = bm_in[...].astype(f32)
    wtmp[3, 0:1, :] = joined(bias[0:1], bias[1:2])
    w1_ref[...] = wtmp[0].T[:, 0:32].astype(bf16)
    wp_ref[...] = wtmp[1, 0:32].astype(bf16)
    wpb_ref[...] = wtmp[2].T[:, 0:32].astype(bf16)
    bm_ref[...] = wtmp[3].T[:, 0:1]
    for copy in slabs:
        copy.wait_recv()
    sent += slabs

    depth = slc_ref.shape[0]
    picked = (
        mm(pick_ref[:, :depth], slc_ref[...])
        + mm(pick_ref[:, depth : 2 * depth], pool[0])
        + mm(pick_ref[:, 2 * depth :], pool[1])
    )
    parts = slc_ref.shape[1] // (LR * tr)
    halves = tc * LC // parts
    sides = []
    for h in range(halves):
        at = [picked[q * pairs : (q + 1) * pairs] for q in (h, halves + h, 2 * halves + h, 3 * halves + h)]
        a0, a1, b0, b1 = at
        rowsum = []
        for prod in (a0 * b0 + a1 * b1, a1 * b0 - a0 * b1):
            for t in range(tr):
                rowsum.append(
                    sum(prod[:, (t * LR + q) * parts : (t * LR + q + 1) * parts] for q in range(LR))
                )
        sides.append(jnp.concatenate(rowsum, axis=0))
    looked = jnp.dot(
        jnp.concatenate(sides, axis=1), avg_ref[...],
        precision=lax.Precision.HIGHEST, preferred_element_type=f32,
    )
    look_f[...] = jnp.zeros_like(look_f)
    for k in range(n_row):
        for q in range(2 * tr):
            look_f[k, q * pp : (q + 1) * pp, :] = looked[q * pairs + k * pp : q * pairs + (k + 1) * pp]
    look_s[...] = look_f[...].astype(bf16)
    look_copies = exchange(look_s, look_r, look_sem)

    def settle(copies):
        for copy, near in copies:
            if near:
                copy.wait()
            else:
                copy.wait_recv()
                sent.append(copy)

    def assemble(ref, s):
        mid = pltpu.roll(ref[0, s].astype(f32), base, 1)
        low = pltpu.roll(ref[1, s].astype(f32), (base - tc) % 128, 1)
        high = pltpu.roll(ref[2, s].astype(f32), base + tc, 1)
        joined = jnp.where(own, mid, jnp.where(lane < base, low, high))
        near = (lane >= base - 5) & (lane < base + tc + 5)
        return jnp.where(inside & near, joined, 0.0)

    settle(tgt_copies)
    for s in range(n_row):
        block = assemble(tgt_r, s)
        for z in range(2):
            for t in range(tr):
                for p in range(pp):
                    i = (z * tr + t) * pp + p
                    b = p * gap + s * tr + t
                    tfld[z : z + 1, b * 128 : (b + 1) * 128] = block[i : i + 1]
    settle(look_copies)
    for s in range(n_row):
        block = assemble(look_r, s)
        for u, turned in enumerate((pltpu.roll(block, 1, 1), block, pltpu.roll(block, 127, 1))):
            for z in range(2):
                for t in range(tr):
                    for p in range(pp):
                        i = (z * tr + t) * pp + p
                        b = p * gap + s * tr + t + 1
                        fld[2 * u + z : 2 * u + z + 1, b * 128 : (b + 1) * 128] = turned[i : i + 1]
    fld[6:7, :] = jnp.ones((1, (nb + 2) * 128), f32)

    def taps(ref, at, width):
        three = [ref[:, pl.ds(pl.multiple_of(at + t * 128, 128), width)] for t in range(3)]
        return jnp.concatenate(three + [jnp.zeros((8, width), f32)], axis=0).astype(bf16)

    def turned_store(ref, value, at):
        for u, turn in enumerate((1, 0, 127)):
            for q in range(2):
                piece = value[:, q * 128 : (q + 1) * 128]
                if turn:
                    piece = pltpu.roll(piece, turn, 1)
                ref[u * 128 : (u + 1) * 128, pl.ds(pl.multiple_of(at + (q + 1) * 128, 128), 128)] = (
                    piece.astype(bf16)
                )

    def good(b):
        one = [inside & (lax.rem(b + q, gap) != gap - 1) for q in range(2)]
        return jnp.concatenate(one, axis=1)

    own2 = jnp.concatenate([own, own], axis=1)

    def rounded(value):
        return value.astype(bf16).astype(f32)

    def lift(i, carry):
        at = pl.multiple_of(i * 256, 256)
        pre1 = mm(w1_ref[...], taps(fld, at, 256))
        turned_store(i3a, rounded(jnp.where(good(2 * i), jnp.maximum(pre1, 0.0), 0.0)), at)
        return carry

    lax.fori_loop(0, nb // 2, lift, 0, unroll=True)

    def conv(w_ref, ref, at):
        total = 0.0
        for t in range(3):
            total = total + mm(w_ref[t], ref[:, pl.ds(pl.multiple_of(at + t * 128, 128), 256)])
        return total

    def mid(i, carry):
        at = pl.multiple_of(i * 256, 256)
        pre2 = conv(wf_ref, i3a, at) + bm_ref[...]
        h2 = jnp.where(good(2 * i), jnp.maximum(pre2, 0.0), 0.0).astype(bf16)
        h2s[:, pl.ds(at, 256)] = h2
        tsum[:, pl.ds(pl.multiple_of(at + 128, 128), 256)] = mm(wp_ref[...], h2)
        return carry

    lax.fori_loop(0, nb // 2, mid, 0, unroll=True)

    six = sum(tsum[8 * t : 8 * t + 8, t * 128 : t * 128 + n] for t in range(3))
    noise = pltpu.roll(six, 1, 1)[0:2] + six[2:4] + pltpu.roll(six, n - 1, 1)[4:6]
    den = fld[2:4, 128 : 128 + n] - noise
    shifted = pltpu.roll(den, n - base, 1)
    outs[...] = jnp.zeros_like(outs)
    for s in range(n_row):
        for z in range(2):
            for t in range(tr):
                for p in range(pp):
                    i = (z * tr + t) * pp + p
                    b = p * gap + s * tr + t
                    outs[s, i : i + 1, :] = shifted[z : z + 1, b * 128 : (b + 1) * 128]
    den_copies = []
    for o in range(n_row):
        k = lax.rem(r + o, n_row)
        if o == 0:
            copy = pltpu.make_async_copy(outs.at[k], den_ref.at[r], den_sem.at[0, o])
            copy.start()
            den_copies.append((copy, True))
        else:
            den_copies.append((remote(outs.at[k], den_ref.at[r], den_sem, o, (k, c, d)), False))
    dn = rounded((tfld[0:2, :] - den) * scale)
    rowok = [jnp.full((1, 128), b % gap != gap - 1) for b in range(nb)]
    mask = jnp.concatenate([inside & ok for ok in rowok], axis=1)
    own_all = jnp.concatenate([own & ok for ok in rowok], axis=1)
    for ref, keep in ((dn3, mask), (dnm3, own_all)):
        kept = jnp.where(keep, dn, 0.0)
        ref[0:2, 128 : 128 + n] = pltpu.roll(kept, 1, 1)
        ref[2:4, 128 : 128 + n] = kept
        ref[4:6, 128 : 128 + n] = pltpu.roll(kept, n - 1, 1)

    def back2(i, carry):
        at = pl.multiple_of(i * 256, 256)
        grad = mm(wpb_ref[...], taps(dn3, at, 256))
        grad = rounded(jnp.where(h2s[:, pl.ds(at, 256)].astype(f32) > 0, grad, 0.0))
        turned_store(i3b, grad, at)
        dp2m[:, pl.ds(at, 256)] = jnp.where(own2, grad, 0.0).astype(bf16)
        return carry

    lax.fori_loop(0, nb // 2, back2, 0, unroll=True)

    sign = jnp.where(lane < 64, 1.0, -1.0)
    for t in range(3):
        gram = mm_t(i3a[:, t * 128 : t * 128 + n], dp2m[...])
        for u in range(3):
            upper = gram[u * 128 : u * 128 + 64]
            lower = gram[u * 128 + 64 : u * 128 + 128]
            x_ref[(3 * t + u) * 64 : (3 * t + u) * 64 + 64, :] = upper + sign * pltpu.roll(lower, 64, 1)
    x_ref[576:600, :] = mm_t(taps(dnm3, 0, n), h2s[...])[0:24]
    x_ref[600:608, :] = mm_t(jnp.ones((16, n), bf16), dp2m[...])[0:8]

    piece = plane_in.shape[1]

    def slot(ref, k):
        return ref.at[pl.ds(pl.multiple_of(k * piece, 8), piece)]

    scatter = []
    for k in range(1, n_plane):
        peer, where = plane_peer(k)
        scatter.append(remote(slot(x_ref, peer), plane_in.at[k], plane_sem, k, where))

    def back1(i, carry):
        at = pl.multiple_of(i * 256, 256)
        h1 = i3a[128:256, pl.ds(pl.multiple_of(at + 128, 128), 256)].astype(f32)
        grad = jnp.where((h1 > 0) & own2, conv(wb_ref, i3b, at), 0.0)
        dp1[:, pl.ds(at, 256)] = grad.astype(bf16)
        return carry

    lax.fori_loop(0, nb // 2, back1, 0, unroll=True)

    small_in[me] = mm_t(taps(fld, 0, n), dp1[...])[0:24]
    small = [
        remote(small_in.at[me], small_in.at[me], small_sem, k, plane_peer(k)[1]) for k in range(1, n_plane)
    ]
    part = slot(x_ref, me)[...]
    for k, copy in zip(range(1, n_plane), scatter):
        copy.wait_recv()
        part = part + plane_in[k]
    date_in[d] = part
    spread = [remote(date_in.at[d], date_in.at[d], date_sem, k, date_peer(k)) for k in range(1, n_date)]

    def total(ref, count):
        return functools.reduce(lambda a, b: a + b, [ref[k] for k in range(count)])

    for copy in small:
        copy.wait_recv()
    small_date[d] = total(small_in, n_plane)
    small_spread = [
        remote(small_date.at[d], small_date.at[d], small_date_sem, k, date_peer(k)) for k in range(1, n_date)
    ]
    for copy in spread:
        copy.wait_recv()
    slot(o_ref, me)[...] = total(date_in, n_date)
    gather = [
        remote(slot(o_ref, me), slot(o_ref, me), gather_sem, k, plane_peer(k)[1])
        for k in range(1, n_plane)
    ]
    for copy in small_spread:
        copy.wait_recv()
    small_ref[...] = total(small_date, n_date)
    settle(den_copies)
    for copy in gather:
        copy.wait_recv()
    for copy in sent + scatter + small + spread + small_spread + gather:
        copy.wait_send()


def finish_kernel(dims, den, sums, small, den_out, lift_out, lbias_out, mid_out, mbias_out, proj_out):
    n_row, pp, tr, tc, ch = dims
    for k in range(n_row):
        for z in range(2):
            for t in range(tr):
                at = (z * tr + t) * pp
                den_out[z, t, k * pp : (k + 1) * pp, :] = den[k, at : at + pp, 0:tc]
    finish_grads(ch, sums, small, lift_out, lbias_out, mid_out, mbias_out, proj_out)


def finish_grads(ch, sums, small, lift_out, lbias_out, mid_out, mbias_out, proj_out):
    for t in range(3):
        for u in range(3):
            at = 8 * t + 2 * u
            upper, lower = small[at : at + 1, :], small[at + 1 : at + 2, :]
            lift_out[t, u, 0:1, :] = upper[:, 0:ch] + lower[:, ch:]
            lift_out[t, u, 1:2, :] = upper[:, ch:] - lower[:, 0:ch]
            at = 576 + 8 * (2 - t) + 2 * (2 - u)
            upper, lower = sums[at : at + 1, :], sums[at + 1 : at + 2, :]
            proj_out[t, u, 0:1, :] = upper[:, 0:ch] + lower[:, ch:]
            proj_out[t, u, 1:2, :] = lower[:, 0:ch] - upper[:, ch:]
            at = (3 * t + u) * ch
            for z in range(2):
                mid_out[z, t, u] = sums[at : at + ch, z * ch : (z + 1) * ch]
    for z in range(2):
        lbias_out[z : z + 1, :] = small[14:15, z * ch : (z + 1) * ch]
        mbias_out[z : z + 1, :] = sums[600:601, z * ch : (z + 1) * ch]


def halo_local(slc, pairs, target, w_lift, b_lift, w_mid, b_mid, w_proj):
    n_row, n_col, n_date = (lax.axis_size(axis) for axis in ("row", "col", "date"))
    dates, srows, scols = slc.shape[1:]
    count, tr, tc = target.shape[1:]
    ch = w_mid.shape[-1]
    pp = count // n_row
    halves = scols // 128
    bf16, f32 = jnp.bfloat16, jnp.float32
    rows = 2 * tr * pp
    pad_rows = -(-rows // 16) * 16
    packed = slc.reshape(2, dates, srows, halves, 128).transpose(1, 0, 3, 2, 4)
    packed = packed.reshape(dates * 2 * halves, srows * 128)
    index = (pairs - lax.axis_index("date") * dates).T
    kinds = 2 * halves
    want = (index[:, None, :] * kinds + jnp.arange(kinds, dtype=jnp.int32)[None, :, None]).reshape(-1)
    pick = (want[:, None] == jnp.arange(3 * dates * kinds, dtype=jnp.int32)[None, :]).astype(bf16)
    spots = jnp.arange(scols, dtype=jnp.int32)[:, None] // LC
    avg = jnp.where(spots == jnp.arange(128, dtype=jnp.int32)[None, :], 1.0 / (LR * LC), 0.0).astype(f32)
    tgt = target.reshape(2, n_row, pp, tr, tc).transpose(1, 0, 3, 2, 4).reshape(n_row, rows, tc)
    tgt = jnp.pad(tgt, ((0, 0), (0, pad_rows - rows), (0, 128 - tc)))
    w_lift, w_proj = w_lift.transpose(1, 2, 0, 3), w_proj.transpose(1, 2, 0, 3)
    scale = 1.0 / math.sqrt(2.0 * count * n_date * tr * n_row * tc * n_col)
    nb = (n_row * tr + 1) * pp
    n, wide = nb * 128, (nb + 2) * 128
    n_plane = n_row * n_col
    piece = -(-608 // (8 * n_plane)) * 8
    dma = pltpu.SemaphoreType.DMA
    vmem = pltpu.VMEM
    den, sums, small = pl.pallas_call(
        functools.partial(step_kernel, (n_row, n_col, n_date, pp, tr, tc), scale),
        out_shape=(
            jax.ShapeDtypeStruct((n_row, pad_rows, 128), f32),
            jax.ShapeDtypeStruct((n_plane * piece, 128), f32),
            jax.ShapeDtypeStruct((24, 128), f32),
        ),
        in_specs=[pl.BlockSpec(memory_space=vmem)] * 4 + [pl.BlockSpec(memory_space=pl.ANY)] * 5,
        out_specs=(pl.BlockSpec(memory_space=vmem),) * 3,
        scratch_shapes=[
            vmem((2,) + packed.shape, bf16),
            vmem((n_row, pad_rows, 128), f32),
            vmem((n_row, pad_rows, 128), bf16),
            vmem((3, n_row, pad_rows, 128), bf16),
            vmem((3, n_row, pad_rows, 128), f32),
            vmem((8, wide), f32),
            vmem((8, n), f32),
            vmem((6 * ch, wide), bf16),
            vmem((6 * ch, wide), bf16),
            vmem((2 * ch, n), bf16),
            vmem((32, wide), f32),
            vmem((8, wide), f32),
            vmem((8, wide), f32),
            vmem((2 * ch, n), bf16),
            vmem((2 * ch, n), bf16),
            vmem((n_row, pad_rows, 128), f32),
            vmem((n_plane * piece, 128), f32),
            vmem(w_lift.shape, bf16),
            vmem(b_lift.shape, bf16),
            vmem(w_mid.shape, bf16),
            vmem(b_mid.shape, bf16),
            vmem(w_proj.shape, bf16),
            dma((5,)),
            vmem((2 * ch, 32), bf16),
            vmem((32, 2 * ch), bf16),
            vmem((2 * ch, 32), bf16),
            vmem((3, 2 * ch, 6 * ch), bf16),
            vmem((3, 2 * ch, 6 * ch), bf16),
            vmem((2 * ch, 1), f32),
            vmem((4, 128, 128), f32),
            vmem((n_plane, piece, 128), f32),
            vmem((n_date, piece, 128), f32),
            vmem((n_plane, 24, 128), f32),
            vmem((n_date, 24, 128), f32),
            dma((2, n_plane)),
            dma((2, n_date)),
            dma((2, 3)),
            dma((2, 3 * n_row)),
            dma((2, 3 * n_row)),
            dma((2, n_row)),
            dma((2, n_plane)),
            dma((2, n_date)),
            dma((2, n_plane)),
        ],
        compiler_params=pltpu.CompilerParams(
            collective_id=0, has_side_effects=True, vmem_limit_bytes=48 * 1024 * 1024
        ),
    )(packed, pick, avg, tgt, w_lift, b_lift, w_mid, b_mid, w_proj)
    shape = jax.ShapeDtypeStruct
    denoised, grad_lift, lift_bias, grad_mid, mid_bias, grad_proj = pl.pallas_call(
        functools.partial(finish_kernel, (n_row, pp, tr, tc, ch)),
        out_shape=(
            shape((2, tr, count, tc), f32),
            shape((3, 3, 2, ch), f32),
            shape((2, ch), f32),
            shape((2, 3, 3, ch, ch), f32),
            shape((2, ch), f32),
            shape((3, 3, 2, ch), f32),
        ),
        in_specs=[pl.BlockSpec(memory_space=vmem)] * 3,
        out_specs=(pl.BlockSpec(memory_space=vmem),) * 6,
        compiler_params=pltpu.CompilerParams(vmem_limit_bytes=8 * 1024 * 1024),
    )(den, sums, small)
    return (
        denoised.transpose(0, 2, 1, 3),
        grad_lift.transpose(2, 0, 1, 3),
        lift_bias,
        grad_mid,
        mid_bias,
        grad_proj.transpose(2, 0, 1, 3),
    )


def whole_kernel(
    dims, scale,
    slc_any, idx_any, tgt_any, wl_any, bl_any, wmid_any, bmid_any, wproj_any,
    den_ref, o_ref, small_ref,
    raw, pool, idx_in, tgt_in, look_s, look_r, tgt_s, tgt_r, fld, tfld, i3a, i3b, h2s, tsum, dn3, dp1, outs, x_ref,
    wl_in, bl_in, wm_in, bm_in, wj_in, w_sem, w1_ref, wp_ref, wpb_ref, wf_ref, wb_ref, bm_ref, wtmp,
    plane_in, date_in, small_in, small_date, slab_sem, look_sem, tgt_sem, den_sem, sum_sem, small_sem,
):
    n_row, n_col, n_date, dates, tr, tc = dims
    r, c, d = lax.axis_index("row"), lax.axis_index("col"), lax.axis_index("date")
    n_plane = n_row * n_col
    me = r * n_col + c
    pairs = n_plane
    nb = n_row * tr
    n = nb * 128
    wide = n + 256
    f32, bf16 = jnp.float32, jnp.bfloat16

    def wrapped(value, size):
        return jnp.where(value >= size, value - size, value)

    plane_peers = []
    for k in range(1, n_plane):
        row, col = wrapped(r + k // n_col, n_row), wrapped(c + k % n_col, n_col)
        plane_peers.append((row * n_col + col, (row, col, d)))
    date_peers = [(r, c, wrapped(d + k, n_date)) for k in range(1, n_date)]

    def remote_of(src, dst, send_sem, recv_sem, where):
        return pltpu.make_async_remote_copy(
            src_ref=src, dst_ref=dst, send_sem=send_sem, recv_sem=recv_sem,
            device_id=where, device_id_type=MESH,
        )

    def wait_bytes(ref, sem):
        pltpu.make_async_copy(ref, ref, sem).wait()

    barrier = pltpu.get_barrier_semaphore()
    for where in date_peers + [where for _, where in plane_peers]:
        pl.semaphore_signal(barrier, inc=1, device_id=where, device_id_type=MESH)
    fetches = []
    wide_in = zip(
        (slc_any, idx_any, tgt_any, wl_any, bl_any, wmid_any, bmid_any, wproj_any),
        (raw.at[0], idx_in, tgt_in, wl_in, bl_in, wm_in, bm_in, wj_in),
    )
    for k, (src, dst) in enumerate(wide_in):
        copy = pltpu.make_async_copy(src, dst, w_sem.at[min(k, 3)])
        copy.start()
        fetches.append(copy)
    pl.semaphore_wait(barrier, n_plane + n_date - 2)

    halves = tc * LC // 128
    chunk = LR * 128
    depth = pool.shape[0] // (3 * halves)

    def slab_copy(way, t):
        rows = pl.ds(t * LR, LR)
        where = (r, c, lax.max(d - way, 0))
        return remote_of(
            slc_any.at[:, rows], raw.at[way, :, rows], slab_sem.at[way - 1], slab_sem.at[2 + (way - 1) * tr + t], where
        )

    sends = (d > 0, d > 1)
    gets = (d < n_date - 1, d < n_date - 2)
    for t in range(tr):
        for way in (2, 1):

            @pl.when(sends[way - 1])
            def _():
                slab_copy(way, t).start()

    pool[...] = jnp.zeros_like(pool)
    for ref in (fld, tfld, dn3, tsum, tgt_s, look_s):
        ref[...] = jnp.zeros_like(ref)
    edge = jnp.zeros((i3a.shape[0], 128), bf16)
    for ref in (i3a, i3b):
        ref[:, 0:128] = edge
        ref[:, (nb + 1) * 128 : (nb + 2) * 128] = edge
    x_ref[608:, :] = jnp.zeros((x_ref.shape[0] - 608, 128), f32)
    outs[...] = jnp.zeros_like(outs)
    lane = lax.broadcasted_iota(jnp.int32, (1, 128), 1)
    for copy in fetches[:3]:
        copy.wait()

    def to_lane(value):
        return pltpu.roll(jnp.concatenate([value, jnp.zeros((value.shape[0], 128 - tc), f32)], axis=1), c * tc, 1)

    for z in range(2):
        for t in range(tr):
            block = to_lane(tgt_in[z, t])
            for k in range(pairs):
                tgt_s[k, z * tr + t : z * tr + t + 1, :] = block[k : k + 1]

    def exchange(src, dst, sems):
        dst[me] = src[me]
        for peer, where in plane_peers:
            remote_of(src.at[peer], dst.at[me], sems.at[0], sems.at[1], where).start()

    def arrived(dst, sems):
        wait_bytes(dst.at[pl.ds(0, n_plane - 1)], sems.at[1])

    def departed(src, sems):
        wait_bytes(src.at[pl.ds(0, n_plane - 1)], sems.at[0])

    kinds = 2 * halves
    index = idx_in[...] - d * dates
    spread_lanes = jnp.concatenate([index[0:1]] * kinds + [index[1:2]] * kinds, axis=1)
    row_of = lax.broadcasted_iota(jnp.int32, (depth * halves, 2 * kinds * pairs), 0)
    lane_of = lax.broadcasted_iota(jnp.int32, (depth * halves, 2 * kinds * pairs), 1)
    inner = lax.rem(row_of, depth)
    kind = lax.rem(inner, 2) * halves + lax.div(row_of, depth)
    same_kind = (kind == lax.rem(lax.div(lane_of, pairs), kinds)) & (inner < 2 * dates)
    picks = []
    for s in range(3):
        hit = same_kind & (lax.div(inner, 2) + s * dates == spread_lanes)
        picks.append(jnp.where(hit, 1.0, 0.0).astype(f32))
    pick = jnp.concatenate(picks, axis=0).T.astype(bf16)
    spots = lax.broadcasted_iota(jnp.int32, (tc * LC, 128), 0)
    avg_lane = lax.broadcasted_iota(jnp.int32, (tc * LC, 128), 1)
    avg = jnp.where(lax.div(spots, LC) + c * tc == avg_lane, 1.0 / (LR * LC), 0.0).astype(bf16)

    exchange(tgt_s, tgt_r, tgt_sem)

    for copy in fetches[3:]:
        copy.wait()
    wtmp[...] = jnp.zeros_like(wtmp)

    def joined(a, b):
        return jnp.concatenate([a, b], axis=1)

    for t in range(3):
        for u in range(3):
            pair = wl_in[t, u].astype(f32)
            at = 8 * t + 2 * u
            wtmp[0, at : at + 1, :] = joined(pair[0:1], pair[1:2])
            wtmp[0, at + 1 : at + 2, :] = joined(-pair[1:2], pair[0:1])
            pair = wj_in[t, u].astype(f32)
            real, imag = joined(pair[0:1], -pair[1:2]), joined(pair[1:2], pair[0:1])
            flip = 8 * (2 - t) + 2 * (2 - u)
            wtmp[1, at : at + 1, :] = real
            wtmp[1, at + 1 : at + 2, :] = imag
            wtmp[2, flip : flip + 1, :] = real
            wtmp[2, flip + 1 : flip + 2, :] = imag
            wr, wi = wm_in[0, t, u].astype(f32), wm_in[1, t, u].astype(f32)
            block = jnp.concatenate([joined(wr, wi), joined(-wi, wr)], axis=0)
            at = (3 * t + u) * 128
            wb_ref[:, 1024 - at : 1152 - at] = block.astype(bf16)
            wf_ref[:, at : at + 128] = block.T.astype(bf16)
    bias = bl_in[...].astype(f32)
    wtmp[0, 14:15, :] = joined(bias[0:1], bias[1:2])
    bias = bm_in[...].astype(f32)
    wtmp[3, 0:1, :] = joined(bias[0:1], bias[1:2])
    w1_ref[...] = wtmp[0].T[:, 0:32].astype(bf16)
    wp_ref[...] = wtmp[1, 0:32].astype(bf16)
    wpb_ref[...] = wtmp[2].T[:, 0:32].astype(bf16)
    bm_ref[...] = wtmp[3].T[:, 0:1]
    fld[6:7, :] = jnp.ones((1, wide), f32)

    def rounded(value):
        return value.astype(bf16).astype(f32)

    def pack(way, t):
        for q in range(LR):
            for h in range(halves):
                at = (way * halves + h) * depth
                lanes = slice((t * LR + q) * 128, (t * LR + q + 1) * 128)
                pool[at : at + 2 * dates, lanes] = raw[way, :, t * LR + q, :, h * 128 : (h + 1) * 128].reshape(
                    2 * dates, 128
                )

    for t in range(tr):
        pack(0, t)
    for t in range(tr):
        for way in (1, 2):

            @pl.when(gets[way - 1])
            def _():
                slab_copy(way, t).wait_recv()
                pack(way, t)

        picked = mm(pick, pool[:, t * chunk : (t + 1) * chunk])
        sides = []
        for h in range(halves):
            a0, a1, b0, b1 = [picked[q * pairs : (q + 1) * pairs] for q in (h, halves + h, 2 * halves + h, 3 * halves + h)]
            both = []
            for prod in (a0 * b0 + a1 * b1, a1 * b0 - a0 * b1):
                both.append(sum(prod[:, q * 128 : (q + 1) * 128] for q in range(LR)))
            sides.append(jnp.concatenate(both, axis=0))
        summed = jnp.concatenate(sides, axis=1)
        high = summed.astype(bf16)
        rest = summed - high.astype(f32)
        middle = rest.astype(bf16)
        low = (rest - middle.astype(f32)).astype(bf16)
        three = mm(jnp.concatenate([high, middle, low], axis=0), avg)
        looked = rounded(three[0 : 2 * pairs] + (three[2 * pairs : 4 * pairs] + three[4 * pairs :]))
        for z in range(2):
            for k in range(pairs):
                at = z * tr + t
                look_s[k, at : at + 1, :] = looked[z * pairs + k : z * pairs + k + 1]
    exchange(look_s, look_r, look_sem)

    first, last = lane == 0, lane == 127

    def right(value):
        return jnp.where(first, 0.0, pltpu.roll(value, 1, 1))

    def left(value):
        return jnp.where(last, 0.0, pltpu.roll(value, 127, 1))

    def assemble(ref, s):
        return functools.reduce(lambda a, b: a + b, [ref[s * n_col + q] for q in range(n_col)])

    arrived(tgt_r, tgt_sem)
    for s in range(n_row):
        block = assemble(tgt_r, s)
        for z in range(2):
            for t in range(tr):
                b = s * tr + t
                tfld[z : z + 1, b * 128 : (b + 1) * 128] = block[z * tr + t : z * tr + t + 1]
    arrived(look_r, look_sem)
    for s in range(n_row):
        block = assemble(look_r, s)
        for u, turned in enumerate((right(block), block, left(block))):
            for z in range(2):
                for t in range(tr):
                    b = s * tr + t + 1
                    fld[2 * u + z : 2 * u + z + 1, b * 128 : (b + 1) * 128] = turned[z * tr + t : z * tr + t + 1]

    def taps(ref, at, width):
        three = [ref[:, at + t * 128 : at + t * 128 + width] for t in range(3)]
        return jnp.concatenate(three + [jnp.zeros((8, width), f32)], axis=0).astype(bf16)

    def turned_store(ref, value, at):
        for q in range(2):
            piece = value[:, q * 128 : (q + 1) * 128]
            lanes = slice(at + (q + 1) * 128, at + (q + 2) * 128)
            for u, turned in enumerate((right(piece), piece, left(piece))):
                ref[u * 128 : (u + 1) * 128, lanes] = turned.astype(bf16)

    for at in range(0, n, 256):
        pre1 = mm(w1_ref[...], taps(fld, at, 256))
        turned_store(i3a, jnp.maximum(pre1, 0.0), at)

    def conv(w_ref, ref, at):
        rows = [ref[:, at + t * 128 : at + t * 128 + 256] for t in range(3)]
        return mm(w_ref[...], jnp.concatenate(rows, axis=0))

    for at in range(0, n, 256):
        pre2 = conv(wf_ref, i3a, at) + bm_ref[...]
        h2 = jnp.maximum(pre2, 0.0).astype(bf16)
        h2s[:, at : at + 256] = h2
        tsum[:, at + 128 : at + 384] = mm(wp_ref[...], h2)

    wide_lane = lax.rem(lax.broadcasted_iota(jnp.int32, (1, n), 1), 128)
    wide_first, wide_last = wide_lane == 0, wide_lane == 127

    def wide_right(value):
        return jnp.where(wide_first, 0.0, pltpu.roll(value, 1, 1))

    def wide_left(value):
        return jnp.where(wide_last, 0.0, pltpu.roll(value, n - 1, 1))

    six = sum(tsum[8 * t : 8 * t + 8, t * 128 : t * 128 + n] for t in range(3))
    noise = wide_right(six)[0:2] + six[2:4] + wide_left(six)[4:6]
    den = fld[2:4, 128 : 128 + n] - noise
    for q in range(n_col):
        shifted = pltpu.roll(den, n - q * tc, 1) if q else den
        for s in range(n_row):
            for z in range(2):
                for t in range(tr):
                    i, b = z * tr + t, s * tr + t
                    outs[s * n_col + q, i : i + 1, :] = shifted[z : z + 1, b * 128 : (b + 1) * 128]
    exchange(outs, den_ref, den_sem)
    dn = rounded((tfld[0:2, :] - den) * scale)
    dn3[0:2, 128 : 128 + n] = wide_right(dn)
    dn3[2:4, 128 : 128 + n] = dn
    dn3[4:6, 128 : 128 + n] = wide_left(dn)

    for at in range(0, n, 256):
        grad = mm(wpb_ref[...], taps(dn3, at, 256))
        grad = jnp.where(h2s[:, at : at + 256].astype(f32) > 0, grad, 0.0)
        turned_store(i3b, grad, at)

    sizes = (192, 192, 256)
    bases = (0, 192, 384)
    per = [size // n_plane for size in sizes]
    count = len(sizes)

    def piece(ref, j, at):
        return ref.at[pl.ds(pl.multiple_of(bases[j] + at * per[j], 8), per[j])]

    def scatter(j):
        for k, (peer, where) in enumerate(plane_peers):
            dst = plane_in.at[j * n_plane + k, pl.ds(0, per[j])]
            remote_of(piece(x_ref, j, peer), dst, sum_sem.at[0], sum_sem.at[3 + j], where).start()

    def across(j):
        wait_bytes(plane_in.at[pl.ds(j * n_plane, n_plane - 1), pl.ds(0, per[j])], sum_sem.at[3 + j])
        part = piece(x_ref, j, me)[...]
        for k in range(n_plane - 1):
            part = part + plane_in[j * n_plane + k, 0 : per[j]]
        slot = date_in.at[j * n_date + d, pl.ds(0, per[j])]
        slot[...] = part
        for where in date_peers:
            remote_of(slot, slot, sum_sem.at[1], sum_sem.at[3 + count + j], where).start()

    def spread(j):
        wait_bytes(date_in.at[pl.ds(j * n_date, n_date - 1), pl.ds(0, per[j])], sum_sem.at[3 + count + j])
        mine = piece(o_ref, j, me)
        mine[...] = functools.reduce(lambda a, b: a + b, [date_in[j * n_date + k, 0 : per[j]] for k in range(n_date)])
        for _, where in plane_peers:
            remote_of(mine, mine, sum_sem.at[2], sum_sem.at[3 + 2 * count + j], where).start()

    sign = jnp.where(lane < 64, 1.0, -1.0)
    dp2 = i3b[128:256, 128 : 128 + n]
    x_ref[576:600, :] = mm_t(taps(dn3, 0, n), h2s[...])[0:24]
    for t in range(3):
        rows = i3a[:, t * 128 : t * 128 + n]
        if t == 2:
            rows = jnp.concatenate([rows, jnp.ones((16, n), bf16)], axis=0)
        gram = mm_t(rows, dp2)
        for u in range(3):
            upper = gram[u * 128 : u * 128 + 64]
            lower = gram[u * 128 + 64 : u * 128 + 128]
            x_ref[(3 * t + u) * 64 : (3 * t + u) * 64 + 64, :] = upper + sign * pltpu.roll(lower, 64, 1)
        if t == 2:
            x_ref[600:608, :] = gram[384:392]
        scatter(t)

    for at in range(0, n, 256):
        h1 = i3a[128:256, at + 128 : at + 384].astype(f32)
        grad = jnp.where(h1 > 0, conv(wb_ref, i3b, at), 0.0)
        dp1[:, at : at + 256] = grad.astype(bf16)
    small_in[me] = mm_t(taps(fld, 0, n), dp1[...])[0:24]
    for _, where in plane_peers:
        remote_of(small_in.at[me], small_in.at[me], small_sem.at[0], small_sem.at[1], where).start()
    for j in range(count):
        across(j)
    wait_bytes(small_in.at[pl.ds(0, n_plane - 1)], small_sem.at[1])
    small_date[d] = functools.reduce(lambda a, b: a + b, [small_in[k] for k in range(n_plane)])
    for where in date_peers:
        remote_of(small_date.at[d], small_date.at[d], small_sem.at[2], small_sem.at[3], where).start()
    for j in range(count):
        spread(j)
    wait_bytes(small_date.at[pl.ds(0, n_date - 1)], small_sem.at[3])
    small_ref[...] = functools.reduce(lambda a, b: a + b, [small_date[k] for k in range(n_date)])
    arrived(den_ref, den_sem)
    for j in range(count):
        wait_bytes(o_ref.at[pl.ds(0, (n_plane - 1) * per[j])], sum_sem.at[3 + 2 * count + j])
    for way in (1, 2):

        @pl.when(sends[way - 1])
        def _():
            wait_bytes(raw.at[0], slab_sem.at[way - 1])

    departed(tgt_s, tgt_sem)
    departed(look_s, look_sem)
    departed(outs, den_sem)
    wait_bytes(small_in.at[pl.ds(0, n_plane - 1)], small_sem.at[0])
    wait_bytes(small_date.at[pl.ds(0, n_date - 1)], small_sem.at[2])
    for q, rows in enumerate(((n_plane - 1) * sum(per), (n_date - 1) * sum(per), (n_plane - 1) * sum(per))):
        wait_bytes(x_ref.at[pl.ds(0, rows)], sum_sem.at[q])


def whole_finish(dims, den, sums, small, den_out, lift_out, lbias_out, mid_out, mbias_out, proj_out):
    n_plane, tr, tc, ch = dims
    for z in range(2):
        for t in range(tr):
            for k in range(n_plane):
                den_out[z, t, k : k + 1, :] = den[k, z * tr + t : z * tr + t + 1, 0:tc]
    finish_grads(ch, sums, small, lift_out, lbias_out, mid_out, mbias_out, proj_out)


def whole_local(slc, pairs, target, w_lift, b_lift, w_mid, b_mid, w_proj):
    n_row, n_col, n_date = (lax.axis_size(axis) for axis in ("row", "col", "date"))
    dates, srows, scols = slc.shape[1:]
    count, tr, tc = target.shape[1:]
    ch = w_mid.shape[-1]
    halves = scols // 128
    bf16, f32 = jnp.bfloat16, jnp.float32
    images = slc.transpose(1, 2, 0, 3)
    depth = -(-2 * dates // 16) * 16
    tgt = target.transpose(0, 2, 1, 3)
    w_lift, w_proj = w_lift.transpose(1, 2, 0, 3), w_proj.transpose(1, 2, 0, 3)
    scale = 1.0 / math.sqrt(2.0 * count * n_date * tr * n_row * tc * n_col)
    nb = n_row * tr
    n, wide = nb * 128, (nb + 2) * 128
    n_plane = n_row * n_col
    zt = -(-2 * tr // 8) * 8
    dma = pltpu.SemaphoreType.DMA
    vmem = pltpu.VMEM
    shape = jax.ShapeDtypeStruct
    images, index, tgt, w_lift, b_lift, w_mid, b_mid, w_proj = (
        pltpu.with_memory_space_constraint(x, pltpu.HBM)
        for x in (images, pairs.T, tgt, w_lift, b_lift, w_mid, b_mid, w_proj)
    )
    den, sums, small = pl.pallas_call(
        functools.partial(whole_kernel, (n_row, n_col, n_date, dates, tr, tc), scale),
        out_shape=(
            shape((n_plane, zt, 128), f32),
            shape((640, 128), f32),
            shape((24, 128), f32),
        ),
        in_specs=[pl.BlockSpec(memory_space=pltpu.HBM)] * 8,
        out_specs=(pl.BlockSpec(memory_space=vmem),) * 3,
        scratch_shapes=[
            vmem((3,) + images.shape, bf16),
            vmem((3 * halves * depth, srows * 128), bf16),
            vmem((2, count), jnp.int32),
            vmem(tgt.shape, f32),
            vmem((n_plane, zt, 128), f32),
            vmem((n_plane, zt, 128), f32),
            vmem((n_plane, zt, 128), f32),
            vmem((n_plane, zt, 128), f32),
            vmem((8, wide), f32),
            vmem((8, n), f32),
            vmem((6 * ch, wide), bf16),
            vmem((6 * ch, wide), bf16),
            vmem((2 * ch, n), bf16),
            vmem((32, wide), f32),
            vmem((8, wide), f32),
            vmem((2 * ch, n), bf16),
            vmem((n_plane, zt, 128), f32),
            vmem((640, 128), f32),
            vmem(w_lift.shape, bf16),
            vmem(b_lift.shape, bf16),
            vmem(w_mid.shape, bf16),
            vmem(b_mid.shape, bf16),
            vmem(w_proj.shape, bf16),
            dma((4,)),
            vmem((2 * ch, 32), bf16),
            vmem((32, 2 * ch), bf16),
            vmem((2 * ch, 32), bf16),
            vmem((2 * ch, 18 * ch), bf16),
            vmem((2 * ch, 18 * ch), bf16),
            vmem((2 * ch, 1), f32),
            vmem((4, 128, 128), f32),
            vmem((3 * n_plane, 32, 128), f32),
            vmem((3 * n_date, 32, 128), f32),
            vmem((n_plane, 24, 128), f32),
            vmem((n_date, 24, 128), f32),
            dma((2 + 2 * tr,)),
            dma((2,)),
            dma((2,)),
            dma((2,)),
            dma((12,)),
            dma((4,)),
        ],
        compiler_params=pltpu.CompilerParams(
            collective_id=0, has_side_effects=True, vmem_limit_bytes=48 * 1024 * 1024
        ),
    )(images, index, tgt, w_lift, b_lift, w_mid, b_mid, w_proj)
    denoised, grad_lift, lift_bias, grad_mid, mid_bias, grad_proj = pl.pallas_call(
        functools.partial(whole_finish, (n_plane, tr, tc, ch)),
        out_shape=(
            shape((2, tr, count, tc), f32),
            shape((3, 3, 2, ch), f32),
            shape((2, ch), f32),
            shape((2, 3, 3, ch, ch), f32),
            shape((2, ch), f32),
            shape((3, 3, 2, ch), f32),
        ),
        in_specs=[pl.BlockSpec(memory_space=vmem)] * 3,
        out_specs=(pl.BlockSpec(memory_space=vmem),) * 6,
        compiler_params=pltpu.CompilerParams(vmem_limit_bytes=8 * 1024 * 1024),
    )(den, sums, small)
    return (
        denoised.transpose(0, 2, 1, 3),
        grad_lift.transpose(2, 0, 1, 3),
        lift_bias,
        grad_mid,
        mid_bias,
        grad_proj.transpose(2, 0, 1, 3),
    )


def local(slc, pairs, target, w_lift, b_lift, w_mid, b_mid, w_proj):
    n_row, n_col = lax.axis_size("row"), lax.axis_size("col")
    count, tr, tc = target.shape[1:]
    whole = (
        count == n_row * n_col
        and tc * n_col == 128
        and (n_row * tr) % 2 == 0
        and 2 * tr <= 8
        and count == 8
        and n_row % 2 == 0
        and w_mid.shape[-1] == 64
        and (2 * slc.shape[1] * slc.shape[3] // 128) % 16 == 0
    )
    return (whole_local if whole else halo_local)(
        slc, pairs, target, w_lift, b_lift, w_mid, b_mid, w_proj
    )


def solution(mesh):
    in_specs = (
        P(None, "date", "row", "col"),
        P("date", None),
        P(None, "date", "row", "col"),
        P(),
        P(),
        P(),
        P(),
        P(),
    )
    out_specs = (P(None, "date", "row", "col"), P(), P(), P(), P(), P())
    return jax.shard_map(local, mesh=mesh, in_specs=in_specs, out_specs=out_specs, check_vma=False)
```

```python
import functools
import math

import jax
import jax.numpy as jnp
from jax import lax
from jax.experimental import pallas as pl
from jax.experimental.pallas import tpu as pltpu
from jax.sharding import PartitionSpec as P

MESH = pl.DeviceIdType.MESH

LR = 2
LC = 4


def mm(a, b):
    return jnp.dot(a, b, preferred_element_type=jnp.float32)


def mm_t(a, b):
    return lax.dot_general(a, b, (((1,), (1,)), ((), ())), preferred_element_type=jnp.float32)


def step_kernel(
    dims, scale,
    slc_ref, pick_ref, avg_ref, tgt_ref, wl_any, bl_any, wmid_any, bmid_any, wproj_any,
    den_ref, o_ref, small_ref,
    pool, look_f, look_s, look_r, tgt_r, fld, tfld, i3a, i3b, h2s, tsum, dn3, dnm3, dp2m, dp1, outs, x_ref,
    wl_in, bl_in, wm_in, bm_in, wj_in, w_sem, w1_ref, wp_ref, wpb_ref, wf_ref, wb_ref, bm_ref, wtmp,
    plane_in, date_in, small_in, small_date, small_sem, small_date_sem, slab_sem, look_sem, tgt_sem, den_sem, plane_sem, date_sem, gather_sem,
):
    n_row, n_col, n_date, pp, tr, tc = dims
    r, c, d = lax.axis_index("row"), lax.axis_index("col"), lax.axis_index("date")
    n_plane = n_row * n_col
    me = r * n_col + c
    rows = n_row * tr
    gap = rows + 1
    nb = gap * pp
    n = nb * 128
    base = (128 - tc) // 2
    pairs = pp * n_row
    f32, bf16 = jnp.float32, jnp.bfloat16

    def plane_peer(k):
        peer = lax.rem(me + k, n_plane)
        return peer, (lax.div(peer, n_col), lax.rem(peer, n_col), d)

    def date_peer(k):
        return (r, c, lax.rem(d + k, n_date))

    def remote(src, dst, sems, at, where):
        copy = pltpu.make_async_remote_copy(
            src_ref=src, dst_ref=dst, send_sem=sems.at[0, at], recv_sem=sems.at[1, at],
            device_id=where, device_id_type=MESH,
        )
        copy.start()
        return copy

    fetches = []
    wide = zip((wl_any, bl_any, wmid_any, bmid_any, wproj_any), (wl_in, bl_in, wm_in, bm_in, wj_in))
    for k, (src, dst) in enumerate(wide):
        copy = pltpu.make_async_copy(src, dst, w_sem.at[k])
        copy.start()
        fetches.append(copy)
    barrier = pltpu.get_barrier_semaphore()
    for k in range(1, n_plane):
        pl.semaphore_signal(barrier, inc=1, device_id=plane_peer(k)[1], device_id_type=MESH)
    for k in range(1, n_date):
        pl.semaphore_signal(barrier, inc=1, device_id=date_peer(k), device_id_type=MESH)
    pl.semaphore_wait(barrier, n_plane + n_date - 2)

    sent = []
    slabs = [remote(slc_ref, pool.at[k - 1], slab_sem, k, date_peer(n_date - k)) for k in (1, 2)]

    def exchange(src, dst, sems):
        copies = []
        for way in range(3):
            col = lax.rem(c + (0, 1, n_col - 1)[way], n_col)
            for o in range(n_row):
                k = lax.rem(r + o, n_row)
                at = way * n_row + o
                if way == 0 and o == 0:
                    copy = pltpu.make_async_copy(src.at[k], dst.at[0, r], sems.at[0, at])
                    copy.start()
                    copies.append((copy, True))
                else:
                    copies.append((remote(src.at[k], dst.at[way, r], sems, at, (k, col, d)), False))
        return copies

    tgt_copies = exchange(tgt_ref, tgt_r, tgt_sem)
    for ref in (fld, tfld, dn3, dnm3, tsum):
        ref[...] = jnp.zeros_like(ref)
    edge = jnp.zeros((i3a.shape[0], 128), bf16)
    for ref in (i3a, i3b):
        ref[:, 0:128] = edge
        ref[:, (nb + 1) * 128 : (nb + 2) * 128] = edge
    x_ref[...] = jnp.zeros_like(x_ref)
    lane = lax.broadcasted_iota(jnp.int32, (1, 128), 1)
    spot = c * tc + lane - base
    inside = (spot >= 0) & (spot < n_col * tc)
    own = (lane >= base) & (lane < base + tc)
    for copy in fetches:
        copy.wait()
    wtmp[...] = jnp.zeros_like(wtmp)

    def joined(a, b):
        return jnp.concatenate([a, b], axis=1)

    for t in range(3):
        for u in range(3):
            pair = wl_in[t, u].astype(f32)
            at = 8 * t + 2 * u
            wtmp[0, at : at + 1, :] = joined(pair[0:1], pair[1:2])
            wtmp[0, at + 1 : at + 2, :] = joined(-pair[1:2], pair[0:1])
            pair = wj_in[t, u].astype(f32)
            real, imag = joined(pair[0:1], -pair[1:2]), joined(pair[1:2], pair[0:1])
            flip = 8 * (2 - t) + 2 * (2 - u)
            wtmp[1, at : at + 1, :] = real
            wtmp[1, at + 1 : at + 2, :] = imag
            wtmp[2, flip : flip + 1, :] = real
            wtmp[2, flip + 1 : flip + 2, :] = imag
            wr, wi = wm_in[0, t, u].astype(f32), wm_in[1, t, u].astype(f32)
            block = jnp.concatenate([joined(wr, wi), joined(-wi, wr)], axis=0)
            wb_ref[2 - t, :, (2 - u) * 128 : (3 - u) * 128] = block.astype(bf16)
            wf_ref[t, :, u * 128 : (u + 1) * 128] = block.T.astype(bf16)
    bias = bl_in[...].astype(f32)
    wtmp[0, 14:15, :] = joined(bias[0:1], bias[1:2])
    bias = bm_in[...].astype(f32)
    wtmp[3, 0:1, :] = joined(bias[0:1], bias[1:2])
    w1_ref[...] = wtmp[0].T[:, 0:32].astype(bf16)
    wp_ref[...] = wtmp[1, 0:32].astype(bf16)
    wpb_ref[...] = wtmp[2].T[:, 0:32].astype(bf16)
    bm_ref[...] = wtmp[3].T[:, 0:1]
    for copy in slabs:
        copy.wait_recv()
    sent += slabs

    depth = slc_ref.shape[0]
    picked = (
        mm(pick_ref[:, :depth], slc_ref[...])
        + mm(pick_ref[:, depth : 2 * depth], pool[0])
        + mm(pick_ref[:, 2 * depth :], pool[1])
    )
    parts = slc_ref.shape[1] // (LR * tr)
    halves = tc * LC // parts
    sides = []
    for h in range(halves):
        at = [picked[q * pairs : (q + 1) * pairs] for q in (h, halves + h, 2 * halves + h, 3 * halves + h)]
        a0, a1, b0, b1 = at
        rowsum = []
        for prod in (a0 * b0 + a1 * b1, a1 * b0 - a0 * b1):
            for t in range(tr):
                rowsum.append(
                    sum(prod[:, (t * LR + q) * parts : (t * LR + q + 1) * parts] for q in range(LR))
                )
        sides.append(jnp.concatenate(rowsum, axis=0))
    looked = jnp.dot(
        jnp.concatenate(sides, axis=1), avg_ref[...],
        precision=lax.Precision.HIGHEST, preferred_element_type=f32,
    )
    look_f[...] = jnp.zeros_like(look_f)
    for k in range(n_row):
        for q in range(2 * tr):
            look_f[k, q * pp : (q + 1) * pp, :] = looked[q * pairs + k * pp : q * pairs + (k + 1) * pp]
    look_s[...] = look_f[...].astype(bf16)
    look_copies = exchange(look_s, look_r, look_sem)

    def settle(copies):
        for copy, near in copies:
            if near:
                copy.wait()
            else:
                copy.wait_recv()
                sent.append(copy)

    def assemble(ref, s):
        mid = pltpu.roll(ref[0, s].astype(f32), base, 1)
        low = pltpu.roll(ref[1, s].astype(f32), (base - tc) % 128, 1)
        high = pltpu.roll(ref[2, s].astype(f32), base + tc, 1)
        joined = jnp.where(own, mid, jnp.where(lane < base, low, high))
        near = (lane >= base - 5) & (lane < base + tc + 5)
        return jnp.where(inside & near, joined, 0.0)

    settle(tgt_copies)
    for s in range(n_row):
        block = assemble(tgt_r, s)
        for z in range(2):
            for t in range(tr):
                for p in range(pp):
                    i = (z * tr + t) * pp + p
                    b = p * gap + s * tr + t
                    tfld[z : z + 1, b * 128 : (b + 1) * 128] = block[i : i + 1]
    settle(look_copies)
    for s in range(n_row):
        block = assemble(look_r, s)
        for u, turned in enumerate((pltpu.roll(block, 1, 1), block, pltpu.roll(block, 127, 1))):
            for z in range(2):
                for t in range(tr):
                    for p in range(pp):
                        i = (z * tr + t) * pp + p
                        b = p * gap + s * tr + t + 1
                        fld[2 * u + z : 2 * u + z + 1, b * 128 : (b + 1) * 128] = turned[i : i + 1]
    fld[6:7, :] = jnp.ones((1, (nb + 2) * 128), f32)

    def taps(ref, at, width):
        three = [ref[:, pl.ds(pl.multiple_of(at + t * 128, 128), width)] for t in range(3)]
        return jnp.concatenate(three + [jnp.zeros((8, width), f32)], axis=0).astype(bf16)

    def turned_store(ref, value, at):
        for u, turn in enumerate((1, 0, 127)):
            for q in range(2):
                piece = value[:, q * 128 : (q + 1) * 128]
                if turn:
                    piece = pltpu.roll(piece, turn, 1)
                ref[u * 128 : (u + 1) * 128, pl.ds(pl.multiple_of(at + (q + 1) * 128, 128), 128)] = (
                    piece.astype(bf16)
                )

    def good(b):
        one = [inside & (lax.rem(b + q, gap) != gap - 1) for q in range(2)]
        return jnp.concatenate(one, axis=1)

    own2 = jnp.concatenate([own, own], axis=1)

    def rounded(value):
        return value.astype(bf16).astype(f32)

    def lift(i, carry):
        at = pl.multiple_of(i * 256, 256)
        pre1 = mm(w1_ref[...], taps(fld, at, 256))
        turned_store(i3a, rounded(jnp.where(good(2 * i), jnp.maximum(pre1, 0.0), 0.0)), at)
        return carry

    lax.fori_loop(0, nb // 2, lift, 0, unroll=True)

    def conv(w_ref, ref, at):
        total = 0.0
        for t in range(3):
            total = total + mm(w_ref[t], ref[:, pl.ds(pl.multiple_of(at + t * 128, 128), 256)])
        return total

    def mid(i, carry):
        at = pl.multiple_of(i * 256, 256)
        pre2 = conv(wf_ref, i3a, at) + bm_ref[...]
        h2 = jnp.where(good(2 * i), jnp.maximum(pre2, 0.0), 0.0).astype(bf16)
        h2s[:, pl.ds(at, 256)] = h2
        tsum[:, pl.ds(pl.multiple_of(at + 128, 128), 256)] = mm(wp_ref[...], h2)
        return carry

    lax.fori_loop(0, nb // 2, mid, 0, unroll=True)

    six = sum(tsum[8 * t : 8 * t + 8, t * 128 : t * 128 + n] for t in range(3))
    noise = pltpu.roll(six, 1, 1)[0:2] + six[2:4] + pltpu.roll(six, n - 1, 1)[4:6]
    den = fld[2:4, 128 : 128 + n] - noise
    shifted = pltpu.roll(den, n - base, 1)
    outs[...] = jnp.zeros_like(outs)
    for s in range(n_row):
        for z in range(2):
            for t in range(tr):
                for p in range(pp):
                    i = (z * tr + t) * pp + p
                    b = p * gap + s * tr + t
                    outs[s, i : i + 1, :] = shifted[z : z + 1, b * 128 : (b + 1) * 128]
    den_copies = []
    for o in range(n_row):
        k = lax.rem(r + o, n_row)
        if o == 0:
            copy = pltpu.make_async_copy(outs.at[k], den_ref.at[r], den_sem.at[0, o])
            copy.start()
            den_copies.append((copy, True))
        else:
            den_copies.append((remote(outs.at[k], den_ref.at[r], den_sem, o, (k, c, d)), False))
    dn = rounded((tfld[0:2, :] - den) * scale)
    rowok = [jnp.full((1, 128), b % gap != gap - 1) for b in range(nb)]
    mask = jnp.concatenate([inside & ok for ok in rowok], axis=1)
    own_all = jnp.concatenate([own & ok for ok in rowok], axis=1)
    for ref, keep in ((dn3, mask), (dnm3, own_all)):
        kept = jnp.where(keep, dn, 0.0)
        ref[0:2, 128 : 128 + n] = pltpu.roll(kept, 1, 1)
        ref[2:4, 128 : 128 + n] = kept
        ref[4:6, 128 : 128 + n] = pltpu.roll(kept, n - 1, 1)

    def back2(i, carry):
        at = pl.multiple_of(i * 256, 256)
        grad = mm(wpb_ref[...], taps(dn3, at, 256))
        grad = rounded(jnp.where(h2s[:, pl.ds(at, 256)].astype(f32) > 0, grad, 0.0))
        turned_store(i3b, grad, at)
        dp2m[:, pl.ds(at, 256)] = jnp.where(own2, grad, 0.0).astype(bf16)
        return carry

    lax.fori_loop(0, nb // 2, back2, 0, unroll=True)

    sign = jnp.where(lane < 64, 1.0, -1.0)
    for t in range(3):
        gram = mm_t(i3a[:, t * 128 : t * 128 + n], dp2m[...])
        for u in range(3):
            upper = gram[u * 128 : u * 128 + 64]
            lower = gram[u * 128 + 64 : u * 128 + 128]
            x_ref[(3 * t + u) * 64 : (3 * t + u) * 64 + 64, :] = upper + sign * pltpu.roll(lower, 64, 1)
    x_ref[576:600, :] = mm_t(taps(dnm3, 0, n), h2s[...])[0:24]
    x_ref[600:608, :] = mm_t(jnp.ones((16, n), bf16), dp2m[...])[0:8]

    piece = plane_in.shape[1]

    def slot(ref, k):
        return ref.at[pl.ds(pl.multiple_of(k * piece, 8), piece)]

    scatter = []
    for k in range(1, n_plane):
        peer, where = plane_peer(k)
        scatter.append(remote(slot(x_ref, peer), plane_in.at[k], plane_sem, k, where))

    def back1(i, carry):
        at = pl.multiple_of(i * 256, 256)
        h1 = i3a[128:256, pl.ds(pl.multiple_of(at + 128, 128), 256)].astype(f32)
        grad = jnp.where((h1 > 0) & own2, conv(wb_ref, i3b, at), 0.0)
        dp1[:, pl.ds(at, 256)] = grad.astype(bf16)
        return carry

    lax.fori_loop(0, nb // 2, back1, 0, unroll=True)

    small_in[me] = mm_t(taps(fld, 0, n), dp1[...])[0:24]
    small = [
        remote(small_in.at[me], small_in.at[me], small_sem, k, plane_peer(k)[1]) for k in range(1, n_plane)
    ]
    part = slot(x_ref, me)[...]
    for k, copy in zip(range(1, n_plane), scatter):
        copy.wait_recv()
        part = part + plane_in[k]
    date_in[d] = part
    spread = [remote(date_in.at[d], date_in.at[d], date_sem, k, date_peer(k)) for k in range(1, n_date)]

    def total(ref, count):
        return functools.reduce(lambda a, b: a + b, [ref[k] for k in range(count)])

    for copy in small:
        copy.wait_recv()
    small_date[d] = total(small_in, n_plane)
    small_spread = [
        remote(small_date.at[d], small_date.at[d], small_date_sem, k, date_peer(k)) for k in range(1, n_date)
    ]
    for copy in spread:
        copy.wait_recv()
    slot(o_ref, me)[...] = total(date_in, n_date)
    gather = [
        remote(slot(o_ref, me), slot(o_ref, me), gather_sem, k, plane_peer(k)[1])
        for k in range(1, n_plane)
    ]
    for copy in small_spread:
        copy.wait_recv()
    small_ref[...] = total(small_date, n_date)
    settle(den_copies)
    for copy in gather:
        copy.wait_recv()
    for copy in sent + scatter + small + spread + small_spread + gather:
        copy.wait_send()


def finish_kernel(dims, den, sums, small, den_out, lift_out, lbias_out, mid_out, mbias_out, proj_out):
    n_row, pp, tr, tc, ch = dims
    for k in range(n_row):
        for z in range(2):
            for t in range(tr):
                at = (z * tr + t) * pp
                den_out[z, t, k * pp : (k + 1) * pp, :] = den[k, at : at + pp, 0:tc]
    finish_grads(ch, sums, small, lift_out, lbias_out, mid_out, mbias_out, proj_out)


def finish_grads(ch, sums, small, lift_out, lbias_out, mid_out, mbias_out, proj_out):
    for t in range(3):
        for u in range(3):
            at = 8 * t + 2 * u
            upper, lower = small[at : at + 1, :], small[at + 1 : at + 2, :]
            lift_out[t, u, 0:1, :] = upper[:, 0:ch] + lower[:, ch:]
            lift_out[t, u, 1:2, :] = upper[:, ch:] - lower[:, 0:ch]
            at = 576 + 8 * (2 - t) + 2 * (2 - u)
            upper, lower = sums[at : at + 1, :], sums[at + 1 : at + 2, :]
            proj_out[t, u, 0:1, :] = upper[:, 0:ch] + lower[:, ch:]
            proj_out[t, u, 1:2, :] = lower[:, 0:ch] - upper[:, ch:]
            at = (3 * t + u) * ch
            for z in range(2):
                mid_out[z, t, u] = sums[at : at + ch, z * ch : (z + 1) * ch]
    for z in range(2):
        lbias_out[z : z + 1, :] = small[14:15, z * ch : (z + 1) * ch]
        mbias_out[z : z + 1, :] = sums[600:601, z * ch : (z + 1) * ch]


def halo_local(slc, pairs, target, w_lift, b_lift, w_mid, b_mid, w_proj):
    n_row, n_col, n_date = (lax.axis_size(axis) for axis in ("row", "col", "date"))
    dates, srows, scols = slc.shape[1:]
    count, tr, tc = target.shape[1:]
    ch = w_mid.shape[-1]
    pp = count // n_row
    halves = scols // 128
    bf16, f32 = jnp.bfloat16, jnp.float32
    rows = 2 * tr * pp
    pad_rows = -(-rows // 16) * 16
    packed = slc.reshape(2, dates, srows, halves, 128).transpose(1, 0, 3, 2, 4)
    packed = packed.reshape(dates * 2 * halves, srows * 128)
    index = (pairs - lax.axis_index("date") * dates).T
    kinds = 2 * halves
    want = (index[:, None, :] * kinds + jnp.arange(kinds, dtype=jnp.int32)[None, :, None]).reshape(-1)
    pick = (want[:, None] == jnp.arange(3 * dates * kinds, dtype=jnp.int32)[None, :]).astype(bf16)
    spots = jnp.arange(scols, dtype=jnp.int32)[:, None] // LC
    avg = jnp.where(spots == jnp.arange(128, dtype=jnp.int32)[None, :], 1.0 / (LR * LC), 0.0).astype(f32)
    tgt = target.reshape(2, n_row, pp, tr, tc).transpose(1, 0, 3, 2, 4).reshape(n_row, rows, tc)
    tgt = jnp.pad(tgt, ((0, 0), (0, pad_rows - rows), (0, 128 - tc)))
    w_lift, w_proj = w_lift.transpose(1, 2, 0, 3), w_proj.transpose(1, 2, 0, 3)
    scale = 1.0 / math.sqrt(2.0 * count * n_date * tr * n_row * tc * n_col)
    nb = (n_row * tr + 1) * pp
    n, wide = nb * 128, (nb + 2) * 128
    n_plane = n_row * n_col
    piece = -(-608 // (8 * n_plane)) * 8
    dma = pltpu.SemaphoreType.DMA
    vmem = pltpu.VMEM
    den, sums, small = pl.pallas_call(
        functools.partial(step_kernel, (n_row, n_col, n_date, pp, tr, tc), scale),
        out_shape=(
            jax.ShapeDtypeStruct((n_row, pad_rows, 128), f32),
            jax.ShapeDtypeStruct((n_plane * piece, 128), f32),
            jax.ShapeDtypeStruct((24, 128), f32),
        ),
        in_specs=[pl.BlockSpec(memory_space=vmem)] * 4 + [pl.BlockSpec(memory_space=pl.ANY)] * 5,
        out_specs=(pl.BlockSpec(memory_space=vmem),) * 3,
        scratch_shapes=[
            vmem((2,) + packed.shape, bf16),
            vmem((n_row, pad_rows, 128), f32),
            vmem((n_row, pad_rows, 128), bf16),
            vmem((3, n_row, pad_rows, 128), bf16),
            vmem((3, n_row, pad_rows, 128), f32),
            vmem((8, wide), f32),
            vmem((8, n), f32),
            vmem((6 * ch, wide), bf16),
            vmem((6 * ch, wide), bf16),
            vmem((2 * ch, n), bf16),
            vmem((32, wide), f32),
            vmem((8, wide), f32),
            vmem((8, wide), f32),
            vmem((2 * ch, n), bf16),
            vmem((2 * ch, n), bf16),
            vmem((n_row, pad_rows, 128), f32),
            vmem((n_plane * piece, 128), f32),
            vmem(w_lift.shape, bf16),
            vmem(b_lift.shape, bf16),
            vmem(w_mid.shape, bf16),
            vmem(b_mid.shape, bf16),
            vmem(w_proj.shape, bf16),
            dma((5,)),
            vmem((2 * ch, 32), bf16),
            vmem((32, 2 * ch), bf16),
            vmem((2 * ch, 32), bf16),
            vmem((3, 2 * ch, 6 * ch), bf16),
            vmem((3, 2 * ch, 6 * ch), bf16),
            vmem((2 * ch, 1), f32),
            vmem((4, 128, 128), f32),
            vmem((n_plane, piece, 128), f32),
            vmem((n_date, piece, 128), f32),
            vmem((n_plane, 24, 128), f32),
            vmem((n_date, 24, 128), f32),
            dma((2, n_plane)),
            dma((2, n_date)),
            dma((2, 3)),
            dma((2, 3 * n_row)),
            dma((2, 3 * n_row)),
            dma((2, n_row)),
            dma((2, n_plane)),
            dma((2, n_date)),
            dma((2, n_plane)),
        ],
        compiler_params=pltpu.CompilerParams(
            collective_id=0, has_side_effects=True, vmem_limit_bytes=48 * 1024 * 1024
        ),
    )(packed, pick, avg, tgt, w_lift, b_lift, w_mid, b_mid, w_proj)
    shape = jax.ShapeDtypeStruct
    denoised, grad_lift, lift_bias, grad_mid, mid_bias, grad_proj = pl.pallas_call(
        functools.partial(finish_kernel, (n_row, pp, tr, tc, ch)),
        out_shape=(
            shape((2, tr, count, tc), f32),
            shape((3, 3, 2, ch), f32),
            shape((2, ch), f32),
            shape((2, 3, 3, ch, ch), f32),
            shape((2, ch), f32),
            shape((3, 3, 2, ch), f32),
        ),
        in_specs=[pl.BlockSpec(memory_space=vmem)] * 3,
        out_specs=(pl.BlockSpec(memory_space=vmem),) * 6,
        compiler_params=pltpu.CompilerParams(vmem_limit_bytes=8 * 1024 * 1024),
    )(den, sums, small)
    return (
        denoised.transpose(0, 2, 1, 3),
        grad_lift.transpose(2, 0, 1, 3),
        lift_bias,
        grad_mid,
        mid_bias,
        grad_proj.transpose(2, 0, 1, 3),
    )


def whole_kernel(
    dims, scale,
    slc_any, idx_any, tgt_any, wl_any, bl_any, wmid_any, bmid_any, wproj_any,
    den_ref, o_ref, small_ref,
    raw, pool, idx_in, tgt_in, look_s, look_r, tgt_s, tgt_r, fld, tfld, i3a, i3b, h2s, tsum, dn3, dp1, outs, x_ref,
    wl_in, bl_in, wm_in, bm_in, wj_in, w_sem, w1_ref, wp_ref, wpb_ref, wf_ref, wb_ref, bm_ref, wtmp,
    plane_in, date_in, small_in, small_date, slab_sem, look_sem, tgt_sem, den_sem, sum_sem, small_sem,
):
    n_row, n_col, n_date, dates, tr, tc = dims
    r, c, d = lax.axis_index("row"), lax.axis_index("col"), lax.axis_index("date")
    n_plane = n_row * n_col
    me = r * n_col + c
    pairs = n_plane
    nb = n_row * tr
    n = nb * 128
    wide = n + 256
    f32, bf16 = jnp.float32, jnp.bfloat16

    def wrapped(value, size):
        return jnp.where(value >= size, value - size, value)

    plane_peers = []
    for k in range(1, n_plane):
        row, col = wrapped(r + k // n_col, n_row), wrapped(c + k % n_col, n_col)
        plane_peers.append((row * n_col + col, (row, col, d)))
    date_peers = [(r, c, wrapped(d + k, n_date)) for k in range(1, n_date)]

    def remote_of(src, dst, send_sem, recv_sem, where):
        return pltpu.make_async_remote_copy(
            src_ref=src, dst_ref=dst, send_sem=send_sem, recv_sem=recv_sem,
            device_id=where, device_id_type=MESH,
        )

    def wait_bytes(ref, sem):
        pltpu.make_async_copy(ref, ref, sem).wait()

    barrier = pltpu.get_barrier_semaphore()
    for where in date_peers + [where for _, where in plane_peers]:
        pl.semaphore_signal(barrier, inc=1, device_id=where, device_id_type=MESH)
    fetches = []
    wide_in = zip(
        (slc_any, idx_any, tgt_any, wl_any, bl_any, wmid_any, bmid_any, wproj_any),
        (raw.at[0], idx_in, tgt_in, wl_in, bl_in, wm_in, bm_in, wj_in),
    )
    for k, (src, dst) in enumerate(wide_in):
        copy = pltpu.make_async_copy(src, dst, w_sem.at[min(k, 3)])
        copy.start()
        fetches.append(copy)
    pl.semaphore_wait(barrier, n_plane + n_date - 2)

    halves = tc * LC // 128
    chunk = LR * 128
    depth = pool.shape[0] // (3 * halves)

    def slab_copy(way, t):
        rows = pl.ds(t * LR, LR)
        where = (r, c, lax.max(d - way, 0))
        return remote_of(
            slc_any.at[:, rows], raw.at[way, :, rows], slab_sem.at[way - 1], slab_sem.at[2 + (way - 1) * tr + t], where
        )

    sends = (d > 0, d > 1)
    gets = (d < n_date - 1, d < n_date - 2)
    for t in range(tr):
        for way in (2, 1):

            @pl.when(sends[way - 1])
            def _():
                slab_copy(way, t).start()

    pool[...] = jnp.zeros_like(pool)
    for ref in (fld, tfld, dn3, tsum, tgt_s, look_s):
        ref[...] = jnp.zeros_like(ref)
    edge = jnp.zeros((i3a.shape[0], 128), bf16)
    for ref in (i3a, i3b):
        ref[:, 0:128] = edge
        ref[:, (nb + 1) * 128 : (nb + 2) * 128] = edge
    x_ref[608:, :] = jnp.zeros((x_ref.shape[0] - 608, 128), f32)
    outs[...] = jnp.zeros_like(outs)
    lane = lax.broadcasted_iota(jnp.int32, (1, 128), 1)
    for copy in fetches[:3]:
        copy.wait()

    def to_lane(value):
        return pltpu.roll(jnp.concatenate([value, jnp.zeros((value.shape[0], 128 - tc), f32)], axis=1), c * tc, 1)

    for z in range(2):
        for t in range(tr):
            block = to_lane(tgt_in[z, t])
            for k in range(pairs):
                tgt_s[k, z * tr + t : z * tr + t + 1, :] = block[k : k + 1]

    def exchange(src, dst, sems):
        dst[me] = src[me]
        for peer, where in plane_peers:
            remote_of(src.at[peer], dst.at[me], sems.at[0], sems.at[1], where).start()

    def arrived(dst, sems):
        wait_bytes(dst.at[pl.ds(0, n_plane - 1)], sems.at[1])

    def departed(src, sems):
        wait_bytes(src.at[pl.ds(0, n_plane - 1)], sems.at[0])

    kinds = 2 * halves
    index = idx_in[...] - d * dates
    spread_lanes = jnp.concatenate([index[0:1]] * kinds + [index[1:2]] * kinds, axis=1)
    row_of = lax.broadcasted_iota(jnp.int32, (depth * halves, 2 * kinds * pairs), 0)
    lane_of = lax.broadcasted_iota(jnp.int32, (depth * halves, 2 * kinds * pairs), 1)
    inner = lax.rem(row_of, depth)
    kind = lax.rem(inner, 2) * halves + lax.div(row_of, depth)
    same_kind = (kind == lax.rem(lax.div(lane_of, pairs), kinds)) & (inner < 2 * dates)
    picks = []
    for s in range(3):
        hit = same_kind & (lax.div(inner, 2) + s * dates == spread_lanes)
        picks.append(jnp.where(hit, 1.0, 0.0).astype(f32))
    pick = jnp.concatenate(picks, axis=0).T.astype(bf16)
    spots = lax.broadcasted_iota(jnp.int32, (tc * LC, 128), 0)
    avg_lane = lax.broadcasted_iota(jnp.int32, (tc * LC, 128), 1)
    avg = jnp.where(lax.div(spots, LC) + c * tc == avg_lane, 1.0 / (LR * LC), 0.0).astype(bf16)

    exchange(tgt_s, tgt_r, tgt_sem)

    for copy in fetches[3:]:
        copy.wait()
    wtmp[...] = jnp.zeros_like(wtmp)

    def joined(a, b):
        return jnp.concatenate([a, b], axis=1)

    for t in range(3):
        for u in range(3):
            pair = wl_in[t, u].astype(f32)
            at = 8 * t + 2 * u
            wtmp[0, at : at + 1, :] = joined(pair[0:1], pair[1:2])
            wtmp[0, at + 1 : at + 2, :] = joined(-pair[1:2], pair[0:1])
            pair = wj_in[t, u].astype(f32)
            real, imag = joined(pair[0:1], -pair[1:2]), joined(pair[1:2], pair[0:1])
            flip = 8 * (2 - t) + 2 * (2 - u)
            wtmp[1, at : at + 1, :] = real
            wtmp[1, at + 1 : at + 2, :] = imag
            wtmp[2, flip : flip + 1, :] = real
            wtmp[2, flip + 1 : flip + 2, :] = imag
            wr, wi = wm_in[0, t, u].astype(f32), wm_in[1, t, u].astype(f32)
            block = jnp.concatenate([joined(wr, wi), joined(-wi, wr)], axis=0)
            wb_ref[(2 - t) * 128 : (3 - t) * 128, (2 - u) * 128 : (3 - u) * 128] = block.astype(bf16)
            wf_ref[t * 128 : (t + 1) * 128, u * 128 : (u + 1) * 128] = block.T.astype(bf16)
    bias = bl_in[...].astype(f32)
    wtmp[0, 14:15, :] = joined(bias[0:1], bias[1:2])
    bias = bm_in[...].astype(f32)
    wtmp[3, 0:1, :] = joined(bias[0:1], bias[1:2])
    w1_ref[...] = wtmp[0].T[:, 0:32].astype(bf16)
    wp_ref[...] = wtmp[1, 0:32].astype(bf16)
    wpb_ref[...] = wtmp[2].T[:, 0:32].astype(bf16)
    bm_ref[...] = wtmp[3].T[:, 0:1]
    fld[6:7, :] = jnp.ones((1, wide), f32)

    def rounded(value):
        return value.astype(bf16).astype(f32)

    def pack(way, t):
        for q in range(LR):
            for h in range(halves):
                at = (way * halves + h) * depth
                lanes = slice((t * LR + q) * 128, (t * LR + q + 1) * 128)
                pool[at : at + 2 * dates, lanes] = raw[way, :, t * LR + q, :, h * 128 : (h + 1) * 128].reshape(
                    2 * dates, 128
                )

    for t in range(tr):
        pack(0, t)
    for t in range(tr):
        for way in (1, 2):

            @pl.when(gets[way - 1])
            def _():
                slab_copy(way, t).wait_recv()
                pack(way, t)

        picked = mm(pick, pool[:, t * chunk : (t + 1) * chunk])
        sides = []
        for h in range(halves):
            a0, a1, b0, b1 = [picked[q * pairs : (q + 1) * pairs] for q in (h, halves + h, 2 * halves + h, 3 * halves + h)]
            both = []
            for prod in (a0 * b0 + a1 * b1, a1 * b0 - a0 * b1):
                both.append(sum(prod[:, q * 128 : (q + 1) * 128] for q in range(LR)))
            sides.append(jnp.concatenate(both, axis=0))
        summed = jnp.concatenate(sides, axis=1)
        high = summed.astype(bf16)
        rest = summed - high.astype(f32)
        middle = rest.astype(bf16)
        low = (rest - middle.astype(f32)).astype(bf16)
        three = mm(jnp.concatenate([high, middle, low], axis=0), avg)
        looked = rounded(three[0 : 2 * pairs] + (three[2 * pairs : 4 * pairs] + three[4 * pairs :]))
        for z in range(2):
            for k in range(pairs):
                at = z * tr + t
                look_s[k, at : at + 1, :] = looked[z * pairs + k : z * pairs + k + 1]
    exchange(look_s, look_r, look_sem)

    first, last = lane == 0, lane == 127

    def right(value):
        return jnp.where(first, jnp.zeros_like(value), pltpu.roll(value, 1, 1))

    def left(value):
        return jnp.where(last, jnp.zeros_like(value), pltpu.roll(value, 127, 1))

    def assemble(ref, s):
        return functools.reduce(lambda a, b: a + b, [ref[s * n_col + q] for q in range(n_col)])

    arrived(tgt_r, tgt_sem)
    for s in range(n_row):
        block = assemble(tgt_r, s)
        for z in range(2):
            for t in range(tr):
                b = s * tr + t
                tfld[z : z + 1, b * 128 : (b + 1) * 128] = block[z * tr + t : z * tr + t + 1]
    arrived(look_r, look_sem)
    for s in range(n_row):
        block = assemble(look_r, s)
        for u, turned in enumerate((right(block), block, left(block))):
            for z in range(2):
                for t in range(tr):
                    b = s * tr + t + 1
                    fld[2 * u + z : 2 * u + z + 1, b * 128 : (b + 1) * 128] = turned[z * tr + t : z * tr + t + 1]

    def taps(ref, at, width):
        three = [ref[:, at + t * 128 : at + t * 128 + width] for t in range(3)]
        return jnp.concatenate(three + [jnp.zeros((8, width), f32)], axis=0).astype(bf16)

    def turned_store(ref, value, at):
        for q in range(2):
            piece = value[:, q * 128 : (q + 1) * 128].astype(bf16)
            lanes = slice(at + (q + 1) * 128, at + (q + 2) * 128)
            for u, turned in enumerate((right(piece), piece, left(piece))):
                ref[u * 128 : (u + 1) * 128, lanes] = turned

    for at in range(0, n, 256):
        pre1 = mm(w1_ref[...], taps(fld, at, 256))
        turned_store(i3a, jnp.maximum(pre1, 0.0), at)

    def conv(w_ref, ref):
        parts = [mm(w_ref[...], ref[:, at + 128 : at + 384]) for at in range(0, n, 256)]
        edge = jnp.zeros((128, 128), f32)
        for p, part in enumerate(parts):
            above = parts[p - 1][0:128, 128:256] if p else edge
            below = parts[p + 1][256:384, 0:128] if p + 1 < len(parts) else edge
            yield (
                jnp.concatenate([above, part[0:128, 0:128]], axis=1)
                + part[128:256]
                + jnp.concatenate([part[256:384, 128:256], below], axis=1)
            )

    for p, summed in enumerate(conv(wf_ref, i3a)):
        at = p * 256
        pre2 = summed + bm_ref[...]
        h2 = jnp.maximum(pre2, 0.0).astype(bf16)
        h2s[:, at : at + 256] = h2
        tsum[:, at + 128 : at + 384] = mm(wp_ref[...], h2)

    wide_lane = lax.rem(lax.broadcasted_iota(jnp.int32, (1, n), 1), 128)
    wide_first, wide_last = wide_lane == 0, wide_lane == 127

    def wide_right(value):
        return jnp.where(wide_first, 0.0, pltpu.roll(value, 1, 1))

    def wide_left(value):
        return jnp.where(wide_last, 0.0, pltpu.roll(value, n - 1, 1))

    six = sum(tsum[8 * t : 8 * t + 8, t * 128 : t * 128 + n] for t in range(3))
    noise = wide_right(six)[0:2] + six[2:4] + wide_left(six)[4:6]
    den = fld[2:4, 128 : 128 + n] - noise
    for q in range(n_col):
        shifted = pltpu.roll(den, n - q * tc, 1) if q else den
        for s in range(n_row):
            for z in range(2):
                for t in range(tr):
                    i, b = z * tr + t, s * tr + t
                    outs[s * n_col + q, i : i + 1, :] = shifted[z : z + 1, b * 128 : (b + 1) * 128]
    exchange(outs, den_ref, den_sem)
    dn = rounded((tfld[0:2, :] - den) * scale)
    dn3[0:2, 128 : 128 + n] = wide_right(dn)
    dn3[2:4, 128 : 128 + n] = dn
    dn3[4:6, 128 : 128 + n] = wide_left(dn)

    for at in range(0, n, 256):
        grad = mm(wpb_ref[...], taps(dn3, at, 256))
        grad = jnp.where(h2s[:, at : at + 256].astype(f32) > 0, grad, 0.0)
        turned_store(i3b, grad, at)

    sizes = (192, 192, 256)
    bases = (0, 192, 384)
    per = [size // n_plane for size in sizes]
    count = len(sizes)

    def piece(ref, j, at):
        return ref.at[pl.ds(pl.multiple_of(bases[j] + at * per[j], 8), per[j])]

    def scatter(j):
        for k, (peer, where) in enumerate(plane_peers):
            dst = plane_in.at[j * n_plane + k, pl.ds(0, per[j])]
            remote_of(piece(x_ref, j, peer), dst, sum_sem.at[0], sum_sem.at[3 + j], where).start()

    def across(j):
        wait_bytes(plane_in.at[pl.ds(j * n_plane, n_plane - 1), pl.ds(0, per[j])], sum_sem.at[3 + j])
        part = piece(x_ref, j, me)[...]
        for k in range(n_plane - 1):
            part = part + plane_in[j * n_plane + k, 0 : per[j]]
        slot = date_in.at[j * n_date + d, pl.ds(0, per[j])]
        slot[...] = part
        for where in date_peers:
            remote_of(slot, slot, sum_sem.at[1], sum_sem.at[3 + count + j], where).start()

    def spread(j):
        wait_bytes(date_in.at[pl.ds(j * n_date, n_date - 1), pl.ds(0, per[j])], sum_sem.at[3 + count + j])
        mine = piece(o_ref, j, me)
        mine[...] = functools.reduce(lambda a, b: a + b, [date_in[j * n_date + k, 0 : per[j]] for k in range(n_date)])
        for _, where in plane_peers:
            remote_of(mine, mine, sum_sem.at[2], sum_sem.at[3 + 2 * count + j], where).start()

    sign = jnp.where(lane < 64, 1.0, -1.0)
    dp2 = i3b[128:256, 128 : 128 + n]
    x_ref[576:600, :] = mm_t(taps(dn3, 0, n), h2s[...])[0:24]
    for t in range(3):
        rows = i3a[:, t * 128 : t * 128 + n]
        if t == 2:
            rows = jnp.concatenate([rows, jnp.ones((16, n), bf16)], axis=0)
        gram = mm_t(rows, dp2)
        for u in range(3):
            upper = gram[u * 128 : u * 128 + 64]
            lower = gram[u * 128 + 64 : u * 128 + 128]
            x_ref[(3 * t + u) * 64 : (3 * t + u) * 64 + 64, :] = upper + sign * pltpu.roll(lower, 64, 1)
        if t == 2:
            x_ref[600:608, :] = gram[384:392]
        scatter(t)

    for p, summed in enumerate(conv(wb_ref, i3b)):
        at = p * 256
        h1 = i3a[128:256, at + 128 : at + 384].astype(f32)
        grad = jnp.where(h1 > 0, summed, 0.0)
        dp1[:, at : at + 256] = grad.astype(bf16)
    small_in[me] = mm_t(taps(fld, 0, n), dp1[...])[0:24]
    for _, where in plane_peers:
        remote_of(small_in.at[me], small_in.at[me], small_sem.at[0], small_sem.at[1], where).start()
    for j in range(count):
        across(j)
    wait_bytes(small_in.at[pl.ds(0, n_plane - 1)], small_sem.at[1])
    small_date[d] = functools.reduce(lambda a, b: a + b, [small_in[k] for k in range(n_plane)])
    for where in date_peers:
        remote_of(small_date.at[d], small_date.at[d], small_sem.at[2], small_sem.at[3], where).start()
    for j in range(count):
        spread(j)
    wait_bytes(small_date.at[pl.ds(0, n_date - 1)], small_sem.at[3])
    small_ref[...] = functools.reduce(lambda a, b: a + b, [small_date[k] for k in range(n_date)])
    arrived(den_ref, den_sem)
    for j in range(count):
        wait_bytes(o_ref.at[pl.ds(0, (n_plane - 1) * per[j])], sum_sem.at[3 + 2 * count + j])
    for way in (1, 2):

        @pl.when(sends[way - 1])
        def _():
            wait_bytes(raw.at[0], slab_sem.at[way - 1])

    departed(tgt_s, tgt_sem)
    departed(look_s, look_sem)
    departed(outs, den_sem)
    wait_bytes(small_in.at[pl.ds(0, n_plane - 1)], small_sem.at[0])
    wait_bytes(small_date.at[pl.ds(0, n_date - 1)], small_sem.at[2])
    for q, rows in enumerate(((n_plane - 1) * sum(per), (n_date - 1) * sum(per), (n_plane - 1) * sum(per))):
        wait_bytes(x_ref.at[pl.ds(0, rows)], sum_sem.at[q])


def whole_finish(dims, den, sums, small, den_out, lift_out, lbias_out, mid_out, mbias_out, proj_out):
    n_plane, tr, tc, ch = dims
    for z in range(2):
        for t in range(tr):
            for k in range(n_plane):
                den_out[z, t, k : k + 1, :] = den[k, z * tr + t : z * tr + t + 1, 0:tc]
    finish_grads(ch, sums, small, lift_out, lbias_out, mid_out, mbias_out, proj_out)


def whole_local(slc, pairs, target, w_lift, b_lift, w_mid, b_mid, w_proj):
    n_row, n_col, n_date = (lax.axis_size(axis) for axis in ("row", "col", "date"))
    dates, srows, scols = slc.shape[1:]
    count, tr, tc = target.shape[1:]
    ch = w_mid.shape[-1]
    halves = scols // 128
    bf16, f32 = jnp.bfloat16, jnp.float32
    images = slc.transpose(1, 2, 0, 3)
    depth = -(-2 * dates // 16) * 16
    tgt = target.transpose(0, 2, 1, 3)
    w_lift, w_proj = w_lift.transpose(1, 2, 0, 3), w_proj.transpose(1, 2, 0, 3)
    scale = 1.0 / math.sqrt(2.0 * count * n_date * tr * n_row * tc * n_col)
    nb = n_row * tr
    n, wide = nb * 128, (nb + 2) * 128
    n_plane = n_row * n_col
    zt = -(-2 * tr // 8) * 8
    dma = pltpu.SemaphoreType.DMA
    vmem = pltpu.VMEM
    shape = jax.ShapeDtypeStruct
    images, index, tgt, w_lift, b_lift, w_mid, b_mid, w_proj = (
        pltpu.with_memory_space_constraint(x, pltpu.HBM)
        for x in (images, pairs.T, tgt, w_lift, b_lift, w_mid, b_mid, w_proj)
    )
    den, sums, small = pl.pallas_call(
        functools.partial(whole_kernel, (n_row, n_col, n_date, dates, tr, tc), scale),
        out_shape=(
            shape((n_plane, zt, 128), f32),
            shape((640, 128), f32),
            shape((24, 128), f32),
        ),
        in_specs=[pl.BlockSpec(memory_space=pltpu.HBM)] * 8,
        out_specs=(pl.BlockSpec(memory_space=vmem),) * 3,
        scratch_shapes=[
            vmem((3,) + images.shape, bf16),
            vmem((3 * halves * depth, srows * 128), bf16),
            vmem((2, count), jnp.int32),
            vmem(tgt.shape, f32),
            vmem((n_plane, zt, 128), f32),
            vmem((n_plane, zt, 128), f32),
            vmem((n_plane, zt, 128), f32),
            vmem((n_plane, zt, 128), f32),
            vmem((8, wide), f32),
            vmem((8, n), f32),
            vmem((6 * ch, wide), bf16),
            vmem((6 * ch, wide), bf16),
            vmem((2 * ch, n), bf16),
            vmem((32, wide), f32),
            vmem((8, wide), f32),
            vmem((2 * ch, n), bf16),
            vmem((n_plane, zt, 128), f32),
            vmem((640, 128), f32),
            vmem(w_lift.shape, bf16),
            vmem(b_lift.shape, bf16),
            vmem(w_mid.shape, bf16),
            vmem(b_mid.shape, bf16),
            vmem(w_proj.shape, bf16),
            dma((4,)),
            vmem((2 * ch, 32), bf16),
            vmem((32, 2 * ch), bf16),
            vmem((2 * ch, 32), bf16),
            vmem((6 * ch, 6 * ch), bf16),
            vmem((6 * ch, 6 * ch), bf16),
            vmem((2 * ch, 1), f32),
            vmem((4, 128, 128), f32),
            vmem((3 * n_plane, 32, 128), f32),
            vmem((3 * n_date, 32, 128), f32),
            vmem((n_plane, 24, 128), f32),
            vmem((n_date, 24, 128), f32),
            dma((2 + 2 * tr,)),
            dma((2,)),
            dma((2,)),
            dma((2,)),
            dma((12,)),
            dma((4,)),
        ],
        compiler_params=pltpu.CompilerParams(
            collective_id=0, has_side_effects=True, vmem_limit_bytes=48 * 1024 * 1024
        ),
    )(images, index, tgt, w_lift, b_lift, w_mid, b_mid, w_proj)
    denoised, grad_lift, lift_bias, grad_mid, mid_bias, grad_proj = pl.pallas_call(
        functools.partial(whole_finish, (n_plane, tr, tc, ch)),
        out_shape=(
            shape((2, tr, count, tc), f32),
            shape((3, 3, 2, ch), f32),
            shape((2, ch), f32),
            shape((2, 3, 3, ch, ch), f32),
            shape((2, ch), f32),
            shape((3, 3, 2, ch), f32),
        ),
        in_specs=[pl.BlockSpec(memory_space=vmem)] * 3,
        out_specs=(pl.BlockSpec(memory_space=vmem),) * 6,
        compiler_params=pltpu.CompilerParams(vmem_limit_bytes=8 * 1024 * 1024),
    )(den, sums, small)
    return (
        denoised.transpose(0, 2, 1, 3),
        grad_lift.transpose(2, 0, 1, 3),
        lift_bias,
        grad_mid,
        mid_bias,
        grad_proj.transpose(2, 0, 1, 3),
    )


def local(slc, pairs, target, w_lift, b_lift, w_mid, b_mid, w_proj):
    n_row, n_col = lax.axis_size("row"), lax.axis_size("col")
    count, tr, tc = target.shape[1:]
    whole = (
        count == n_row * n_col
        and tc * n_col == 128
        and (n_row * tr) % 2 == 0
        and 2 * tr <= 8
        and count == 8
        and n_row % 2 == 0
        and w_mid.shape[-1] == 64
        and (2 * slc.shape[1] * slc.shape[3] // 128) % 16 == 0
    )
    return (whole_local if whole else halo_local)(
        slc, pairs, target, w_lift, b_lift, w_mid, b_mid, w_proj
    )


def solution(mesh):
    in_specs = (
        P(None, "date", "row", "col"),
        P("date", None),
        P(None, "date", "row", "col"),
        P(),
        P(),
        P(),
        P(),
        P(),
    )
    out_specs = (P(None, "date", "row", "col"), P(), P(), P(), P(), P())
    return jax.shard_map(local, mesh=mesh, in_specs=in_specs, out_specs=out_specs, check_vma=False)
```

```python
import functools
import math

import jax
import jax.numpy as jnp
from jax import lax
from jax.experimental import pallas as pl
from jax.experimental.pallas import tpu as pltpu
from jax.sharding import PartitionSpec as P

MESH = pl.DeviceIdType.MESH

LR = 2
LC = 4


def mm(a, b):
    return jnp.dot(a, b, preferred_element_type=jnp.float32)


def mm_t(a, b):
    return lax.dot_general(a, b, (((1,), (1,)), ((), ())), preferred_element_type=jnp.float32)


def step_kernel(
    dims, scale,
    slc_ref, pick_ref, avg_ref, tgt_ref, wl_any, bl_any, wmid_any, bmid_any, wproj_any,
    den_ref, o_ref, small_ref,
    pool, look_f, look_s, look_r, tgt_r, fld, tfld, i3a, i3b, h2s, tsum, dn3, dnm3, dp2m, dp1, outs, x_ref,
    wl_in, bl_in, wm_in, bm_in, wj_in, w_sem, w1_ref, wp_ref, wpb_ref, wf_ref, wb_ref, bm_ref, wtmp,
    plane_in, date_in, small_in, small_date, small_sem, small_date_sem, slab_sem, look_sem, tgt_sem, den_sem, plane_sem, date_sem, gather_sem,
):
    n_row, n_col, n_date, pp, tr, tc = dims
    r, c, d = lax.axis_index("row"), lax.axis_index("col"), lax.axis_index("date")
    n_plane = n_row * n_col
    me = r * n_col + c
    rows = n_row * tr
    gap = rows + 1
    nb = gap * pp
    n = nb * 128
    base = (128 - tc) // 2
    pairs = pp * n_row
    f32, bf16 = jnp.float32, jnp.bfloat16

    def plane_peer(k):
        peer = lax.rem(me + k, n_plane)
        return peer, (lax.div(peer, n_col), lax.rem(peer, n_col), d)

    def date_peer(k):
        return (r, c, lax.rem(d + k, n_date))

    def remote(src, dst, sems, at, where):
        copy = pltpu.make_async_remote_copy(
            src_ref=src, dst_ref=dst, send_sem=sems.at[0, at], recv_sem=sems.at[1, at],
            device_id=where, device_id_type=MESH,
        )
        copy.start()
        return copy

    fetches = []
    wide = zip((wl_any, bl_any, wmid_any, bmid_any, wproj_any), (wl_in, bl_in, wm_in, bm_in, wj_in))
    for k, (src, dst) in enumerate(wide):
        copy = pltpu.make_async_copy(src, dst, w_sem.at[k])
        copy.start()
        fetches.append(copy)
    barrier = pltpu.get_barrier_semaphore()
    for k in range(1, n_plane):
        pl.semaphore_signal(barrier, inc=1, device_id=plane_peer(k)[1], device_id_type=MESH)
    for k in range(1, n_date):
        pl.semaphore_signal(barrier, inc=1, device_id=date_peer(k), device_id_type=MESH)
    pl.semaphore_wait(barrier, n_plane + n_date - 2)

    sent = []
    slabs = [remote(slc_ref, pool.at[k - 1], slab_sem, k, date_peer(n_date - k)) for k in (1, 2)]

    def exchange(src, dst, sems):
        copies = []
        for way in range(3):
            col = lax.rem(c + (0, 1, n_col - 1)[way], n_col)
            for o in range(n_row):
                k = lax.rem(r + o, n_row)
                at = way * n_row + o
                if way == 0 and o == 0:
                    copy = pltpu.make_async_copy(src.at[k], dst.at[0, r], sems.at[0, at])
                    copy.start()
                    copies.append((copy, True))
                else:
                    copies.append((remote(src.at[k], dst.at[way, r], sems, at, (k, col, d)), False))
        return copies

    tgt_copies = exchange(tgt_ref, tgt_r, tgt_sem)
    for ref in (fld, tfld, dn3, dnm3, tsum):
        ref[...] = jnp.zeros_like(ref)
    edge = jnp.zeros((i3a.shape[0], 128), bf16)
    for ref in (i3a, i3b):
        ref[:, 0:128] = edge
        ref[:, (nb + 1) * 128 : (nb + 2) * 128] = edge
    x_ref[...] = jnp.zeros_like(x_ref)
    lane = lax.broadcasted_iota(jnp.int32, (1, 128), 1)
    spot = c * tc + lane - base
    inside = (spot >= 0) & (spot < n_col * tc)
    own = (lane >= base) & (lane < base + tc)
    for copy in fetches:
        copy.wait()
    wtmp[...] = jnp.zeros_like(wtmp)

    def joined(a, b):
        return jnp.concatenate([a, b], axis=1)

    for t in range(3):
        for u in range(3):
            pair = wl_in[t, u].astype(f32)
            at = 8 * t + 2 * u
            wtmp[0, at : at + 1, :] = joined(pair[0:1], pair[1:2])
            wtmp[0, at + 1 : at + 2, :] = joined(-pair[1:2], pair[0:1])
            pair = wj_in[t, u].astype(f32)
            real, imag = joined(pair[0:1], -pair[1:2]), joined(pair[1:2], pair[0:1])
            flip = 8 * (2 - t) + 2 * (2 - u)
            wtmp[1, at : at + 1, :] = real
            wtmp[1, at + 1 : at + 2, :] = imag
            wtmp[2, flip : flip + 1, :] = real
            wtmp[2, flip + 1 : flip + 2, :] = imag
            wr, wi = wm_in[0, t, u].astype(f32), wm_in[1, t, u].astype(f32)
            block = jnp.concatenate([joined(wr, wi), joined(-wi, wr)], axis=0)
            wb_ref[2 - t, :, (2 - u) * 128 : (3 - u) * 128] = block.astype(bf16)
            wf_ref[t, :, u * 128 : (u + 1) * 128] = block.T.astype(bf16)
    bias = bl_in[...].astype(f32)
    wtmp[0, 14:15, :] = joined(bias[0:1], bias[1:2])
    bias = bm_in[...].astype(f32)
    wtmp[3, 0:1, :] = joined(bias[0:1], bias[1:2])
    w1_ref[...] = wtmp[0].T[:, 0:32].astype(bf16)
    wp_ref[...] = wtmp[1, 0:32].astype(bf16)
    wpb_ref[...] = wtmp[2].T[:, 0:32].astype(bf16)
    bm_ref[...] = wtmp[3].T[:, 0:1]
    for copy in slabs:
        copy.wait_recv()
    sent += slabs

    depth = slc_ref.shape[0]
    picked = (
        mm(pick_ref[:, :depth], slc_ref[...])
        + mm(pick_ref[:, depth : 2 * depth], pool[0])
        + mm(pick_ref[:, 2 * depth :], pool[1])
    )
    parts = slc_ref.shape[1] // (LR * tr)
    halves = tc * LC // parts
    sides = []
    for h in range(halves):
        at = [picked[q * pairs : (q + 1) * pairs] for q in (h, halves + h, 2 * halves + h, 3 * halves + h)]
        a0, a1, b0, b1 = at
        rowsum = []
        for prod in (a0 * b0 + a1 * b1, a1 * b0 - a0 * b1):
            for t in range(tr):
                rowsum.append(
                    sum(prod[:, (t * LR + q) * parts : (t * LR + q + 1) * parts] for q in range(LR))
                )
        sides.append(jnp.concatenate(rowsum, axis=0))
    looked = jnp.dot(
        jnp.concatenate(sides, axis=1), avg_ref[...],
        precision=lax.Precision.HIGHEST, preferred_element_type=f32,
    )
    look_f[...] = jnp.zeros_like(look_f)
    for k in range(n_row):
        for q in range(2 * tr):
            look_f[k, q * pp : (q + 1) * pp, :] = looked[q * pairs + k * pp : q * pairs + (k + 1) * pp]
    look_s[...] = look_f[...].astype(bf16)
    look_copies = exchange(look_s, look_r, look_sem)

    def settle(copies):
        for copy, near in copies:
            if near:
                copy.wait()
            else:
                copy.wait_recv()
                sent.append(copy)

    def assemble(ref, s):
        mid = pltpu.roll(ref[0, s].astype(f32), base, 1)
        low = pltpu.roll(ref[1, s].astype(f32), (base - tc) % 128, 1)
        high = pltpu.roll(ref[2, s].astype(f32), base + tc, 1)
        joined = jnp.where(own, mid, jnp.where(lane < base, low, high))
        near = (lane >= base - 5) & (lane < base + tc + 5)
        return jnp.where(inside & near, joined, 0.0)

    settle(tgt_copies)
    for s in range(n_row):
        block = assemble(tgt_r, s)
        for z in range(2):
            for t in range(tr):
                for p in range(pp):
                    i = (z * tr + t) * pp + p
                    b = p * gap + s * tr + t
                    tfld[z : z + 1, b * 128 : (b + 1) * 128] = block[i : i + 1]
    settle(look_copies)
    for s in range(n_row):
        block = assemble(look_r, s)
        for u, turned in enumerate((pltpu.roll(block, 1, 1), block, pltpu.roll(block, 127, 1))):
            for z in range(2):
                for t in range(tr):
                    for p in range(pp):
                        i = (z * tr + t) * pp + p
                        b = p * gap + s * tr + t + 1
                        fld[2 * u + z : 2 * u + z + 1, b * 128 : (b + 1) * 128] = turned[i : i + 1]
    fld[6:7, :] = jnp.ones((1, (nb + 2) * 128), f32)

    def taps(ref, at, width):
        three = [ref[:, pl.ds(pl.multiple_of(at + t * 128, 128), width)] for t in range(3)]
        return jnp.concatenate(three + [jnp.zeros((8, width), f32)], axis=0).astype(bf16)

    def turned_store(ref, value, at):
        for u, turn in enumerate((1, 0, 127)):
            for q in range(2):
                piece = value[:, q * 128 : (q + 1) * 128]
                if turn:
                    piece = pltpu.roll(piece, turn, 1)
                ref[u * 128 : (u + 1) * 128, pl.ds(pl.multiple_of(at + (q + 1) * 128, 128), 128)] = (
                    piece.astype(bf16)
                )

    def good(b):
        one = [inside & (lax.rem(b + q, gap) != gap - 1) for q in range(2)]
        return jnp.concatenate(one, axis=1)

    own2 = jnp.concatenate([own, own], axis=1)

    def rounded(value):
        return value.astype(bf16).astype(f32)

    def lift(i, carry):
        at = pl.multiple_of(i * 256, 256)
        pre1 = mm(w1_ref[...], taps(fld, at, 256))
        turned_store(i3a, rounded(jnp.where(good(2 * i), jnp.maximum(pre1, 0.0), 0.0)), at)
        return carry

    lax.fori_loop(0, nb // 2, lift, 0, unroll=True)

    def conv(w_ref, ref, at):
        total = 0.0
        for t in range(3):
            total = total + mm(w_ref[t], ref[:, pl.ds(pl.multiple_of(at + t * 128, 128), 256)])
        return total

    def mid(i, carry):
        at = pl.multiple_of(i * 256, 256)
        pre2 = conv(wf_ref, i3a, at) + bm_ref[...]
        h2 = jnp.where(good(2 * i), jnp.maximum(pre2, 0.0), 0.0).astype(bf16)
        h2s[:, pl.ds(at, 256)] = h2
        tsum[:, pl.ds(pl.multiple_of(at + 128, 128), 256)] = mm(wp_ref[...], h2)
        return carry

    lax.fori_loop(0, nb // 2, mid, 0, unroll=True)

    six = sum(tsum[8 * t : 8 * t + 8, t * 128 : t * 128 + n] for t in range(3))
    noise = pltpu.roll(six, 1, 1)[0:2] + six[2:4] + pltpu.roll(six, n - 1, 1)[4:6]
    den = fld[2:4, 128 : 128 + n] - noise
    shifted = pltpu.roll(den, n - base, 1)
    outs[...] = jnp.zeros_like(outs)
    for s in range(n_row):
        for z in range(2):
            for t in range(tr):
                for p in range(pp):
                    i = (z * tr + t) * pp + p
                    b = p * gap + s * tr + t
                    outs[s, i : i + 1, :] = shifted[z : z + 1, b * 128 : (b + 1) * 128]
    den_copies = []
    for o in range(n_row):
        k = lax.rem(r + o, n_row)
        if o == 0:
            copy = pltpu.make_async_copy(outs.at[k], den_ref.at[r], den_sem.at[0, o])
            copy.start()
            den_copies.append((copy, True))
        else:
            den_copies.append((remote(outs.at[k], den_ref.at[r], den_sem, o, (k, c, d)), False))
    dn = rounded((tfld[0:2, :] - den) * scale)
    rowok = [jnp.full((1, 128), b % gap != gap - 1) for b in range(nb)]
    mask = jnp.concatenate([inside & ok for ok in rowok], axis=1)
    own_all = jnp.concatenate([own & ok for ok in rowok], axis=1)
    for ref, keep in ((dn3, mask), (dnm3, own_all)):
        kept = jnp.where(keep, dn, 0.0)
        ref[0:2, 128 : 128 + n] = pltpu.roll(kept, 1, 1)
        ref[2:4, 128 : 128 + n] = kept
        ref[4:6, 128 : 128 + n] = pltpu.roll(kept, n - 1, 1)

    def back2(i, carry):
        at = pl.multiple_of(i * 256, 256)
        grad = mm(wpb_ref[...], taps(dn3, at, 256))
        grad = rounded(jnp.where(h2s[:, pl.ds(at, 256)].astype(f32) > 0, grad, 0.0))
        turned_store(i3b, grad, at)
        dp2m[:, pl.ds(at, 256)] = jnp.where(own2, grad, 0.0).astype(bf16)
        return carry

    lax.fori_loop(0, nb // 2, back2, 0, unroll=True)

    sign = jnp.where(lane < 64, 1.0, -1.0)
    for t in range(3):
        gram = mm_t(i3a[:, t * 128 : t * 128 + n], dp2m[...])
        for u in range(3):
            upper = gram[u * 128 : u * 128 + 64]
            lower = gram[u * 128 + 64 : u * 128 + 128]
            x_ref[(3 * t + u) * 64 : (3 * t + u) * 64 + 64, :] = upper + sign * pltpu.roll(lower, 64, 1)
    x_ref[576:600, :] = mm_t(taps(dnm3, 0, n), h2s[...])[0:24]
    x_ref[600:608, :] = mm_t(jnp.ones((16, n), bf16), dp2m[...])[0:8]

    piece = plane_in.shape[1]

    def slot(ref, k):
        return ref.at[pl.ds(pl.multiple_of(k * piece, 8), piece)]

    scatter = []
    for k in range(1, n_plane):
        peer, where = plane_peer(k)
        scatter.append(remote(slot(x_ref, peer), plane_in.at[k], plane_sem, k, where))

    def back1(i, carry):
        at = pl.multiple_of(i * 256, 256)
        h1 = i3a[128:256, pl.ds(pl.multiple_of(at + 128, 128), 256)].astype(f32)
        grad = jnp.where((h1 > 0) & own2, conv(wb_ref, i3b, at), 0.0)
        dp1[:, pl.ds(at, 256)] = grad.astype(bf16)
        return carry

    lax.fori_loop(0, nb // 2, back1, 0, unroll=True)

    small_in[me] = mm_t(taps(fld, 0, n), dp1[...])[0:24]
    small = [
        remote(small_in.at[me], small_in.at[me], small_sem, k, plane_peer(k)[1]) for k in range(1, n_plane)
    ]
    part = slot(x_ref, me)[...]
    for k, copy in zip(range(1, n_plane), scatter):
        copy.wait_recv()
        part = part + plane_in[k]
    date_in[d] = part
    spread = [remote(date_in.at[d], date_in.at[d], date_sem, k, date_peer(k)) for k in range(1, n_date)]

    def total(ref, count):
        return functools.reduce(lambda a, b: a + b, [ref[k] for k in range(count)])

    for copy in small:
        copy.wait_recv()
    small_date[d] = total(small_in, n_plane)
    small_spread = [
        remote(small_date.at[d], small_date.at[d], small_date_sem, k, date_peer(k)) for k in range(1, n_date)
    ]
    for copy in spread:
        copy.wait_recv()
    slot(o_ref, me)[...] = total(date_in, n_date)
    gather = [
        remote(slot(o_ref, me), slot(o_ref, me), gather_sem, k, plane_peer(k)[1])
        for k in range(1, n_plane)
    ]
    for copy in small_spread:
        copy.wait_recv()
    small_ref[...] = total(small_date, n_date)
    settle(den_copies)
    for copy in gather:
        copy.wait_recv()
    for copy in sent + scatter + small + spread + small_spread + gather:
        copy.wait_send()


def finish_kernel(dims, den, sums, small, den_out, lift_out, lbias_out, mid_out, mbias_out, proj_out):
    n_row, pp, tr, tc, ch = dims
    for k in range(n_row):
        for z in range(2):
            for t in range(tr):
                at = (z * tr + t) * pp
                den_out[z, t, k * pp : (k + 1) * pp, :] = den[k, at : at + pp, 0:tc]
    finish_grads(ch, sums, small, lift_out, lbias_out, mid_out, mbias_out, proj_out)


def finish_grads(ch, sums, small, lift_out, lbias_out, mid_out, mbias_out, proj_out):
    for t in range(3):
        for u in range(3):
            at = 8 * t + 2 * u
            upper, lower = small[at : at + 1, :], small[at + 1 : at + 2, :]
            lift_out[t, u, 0:1, :] = upper[:, 0:ch] + lower[:, ch:]
            lift_out[t, u, 1:2, :] = upper[:, ch:] - lower[:, 0:ch]
            at = 576 + 8 * (2 - t) + 2 * (2 - u)
            upper, lower = sums[at : at + 1, :], sums[at + 1 : at + 2, :]
            proj_out[t, u, 0:1, :] = upper[:, 0:ch] + lower[:, ch:]
            proj_out[t, u, 1:2, :] = lower[:, 0:ch] - upper[:, ch:]
            at = (3 * t + u) * ch
            for z in range(2):
                mid_out[z, t, u] = sums[at : at + ch, z * ch : (z + 1) * ch]
    for z in range(2):
        lbias_out[z : z + 1, :] = small[14:15, z * ch : (z + 1) * ch]
        mbias_out[z : z + 1, :] = sums[600:601, z * ch : (z + 1) * ch]


def halo_local(slc, pairs, target, w_lift, b_lift, w_mid, b_mid, w_proj):
    n_row, n_col, n_date = (lax.axis_size(axis) for axis in ("row", "col", "date"))
    dates, srows, scols = slc.shape[1:]
    count, tr, tc = target.shape[1:]
    ch = w_mid.shape[-1]
    pp = count // n_row
    halves = scols // 128
    bf16, f32 = jnp.bfloat16, jnp.float32
    rows = 2 * tr * pp
    pad_rows = -(-rows // 16) * 16
    packed = slc.reshape(2, dates, srows, halves, 128).transpose(1, 0, 3, 2, 4)
    packed = packed.reshape(dates * 2 * halves, srows * 128)
    index = (pairs - lax.axis_index("date") * dates).T
    kinds = 2 * halves
    want = (index[:, None, :] * kinds + jnp.arange(kinds, dtype=jnp.int32)[None, :, None]).reshape(-1)
    pick = (want[:, None] == jnp.arange(3 * dates * kinds, dtype=jnp.int32)[None, :]).astype(bf16)
    spots = jnp.arange(scols, dtype=jnp.int32)[:, None] // LC
    avg = jnp.where(spots == jnp.arange(128, dtype=jnp.int32)[None, :], 1.0 / (LR * LC), 0.0).astype(f32)
    tgt = target.reshape(2, n_row, pp, tr, tc).transpose(1, 0, 3, 2, 4).reshape(n_row, rows, tc)
    tgt = jnp.pad(tgt, ((0, 0), (0, pad_rows - rows), (0, 128 - tc)))
    w_lift, w_proj = w_lift.transpose(1, 2, 0, 3), w_proj.transpose(1, 2, 0, 3)
    scale = 1.0 / math.sqrt(2.0 * count * n_date * tr * n_row * tc * n_col)
    nb = (n_row * tr + 1) * pp
    n, wide = nb * 128, (nb + 2) * 128
    n_plane = n_row * n_col
    piece = -(-608 // (8 * n_plane)) * 8
    dma = pltpu.SemaphoreType.DMA
    vmem = pltpu.VMEM
    den, sums, small = pl.pallas_call(
        functools.partial(step_kernel, (n_row, n_col, n_date, pp, tr, tc), scale),
        out_shape=(
            jax.ShapeDtypeStruct((n_row, pad_rows, 128), f32),
            jax.ShapeDtypeStruct((n_plane * piece, 128), f32),
            jax.ShapeDtypeStruct((24, 128), f32),
        ),
        in_specs=[pl.BlockSpec(memory_space=vmem)] * 4 + [pl.BlockSpec(memory_space=pl.ANY)] * 5,
        out_specs=(pl.BlockSpec(memory_space=vmem),) * 3,
        scratch_shapes=[
            vmem((2,) + packed.shape, bf16),
            vmem((n_row, pad_rows, 128), f32),
            vmem((n_row, pad_rows, 128), bf16),
            vmem((3, n_row, pad_rows, 128), bf16),
            vmem((3, n_row, pad_rows, 128), f32),
            vmem((8, wide), f32),
            vmem((8, n), f32),
            vmem((6 * ch, wide), bf16),
            vmem((6 * ch, wide), bf16),
            vmem((2 * ch, n), bf16),
            vmem((32, wide), f32),
            vmem((8, wide), f32),
            vmem((8, wide), f32),
            vmem((2 * ch, n), bf16),
            vmem((2 * ch, n), bf16),
            vmem((n_row, pad_rows, 128), f32),
            vmem((n_plane * piece, 128), f32),
            vmem(w_lift.shape, bf16),
            vmem(b_lift.shape, bf16),
            vmem(w_mid.shape, bf16),
            vmem(b_mid.shape, bf16),
            vmem(w_proj.shape, bf16),
            dma((5,)),
            vmem((2 * ch, 32), bf16),
            vmem((32, 2 * ch), bf16),
            vmem((2 * ch, 32), bf16),
            vmem((3, 2 * ch, 6 * ch), bf16),
            vmem((3, 2 * ch, 6 * ch), bf16),
            vmem((2 * ch, 1), f32),
            vmem((4, 128, 128), f32),
            vmem((n_plane, piece, 128), f32),
            vmem((n_date, piece, 128), f32),
            vmem((n_plane, 24, 128), f32),
            vmem((n_date, 24, 128), f32),
            dma((2, n_plane)),
            dma((2, n_date)),
            dma((2, 3)),
            dma((2, 3 * n_row)),
            dma((2, 3 * n_row)),
            dma((2, n_row)),
            dma((2, n_plane)),
            dma((2, n_date)),
            dma((2, n_plane)),
        ],
        compiler_params=pltpu.CompilerParams(
            collective_id=0, has_side_effects=True, vmem_limit_bytes=48 * 1024 * 1024
        ),
    )(packed, pick, avg, tgt, w_lift, b_lift, w_mid, b_mid, w_proj)
    shape = jax.ShapeDtypeStruct
    denoised, grad_lift, lift_bias, grad_mid, mid_bias, grad_proj = pl.pallas_call(
        functools.partial(finish_kernel, (n_row, pp, tr, tc, ch)),
        out_shape=(
            shape((2, tr, count, tc), f32),
            shape((3, 3, 2, ch), f32),
            shape((2, ch), f32),
            shape((2, 3, 3, ch, ch), f32),
            shape((2, ch), f32),
            shape((3, 3, 2, ch), f32),
        ),
        in_specs=[pl.BlockSpec(memory_space=vmem)] * 3,
        out_specs=(pl.BlockSpec(memory_space=vmem),) * 6,
        compiler_params=pltpu.CompilerParams(vmem_limit_bytes=8 * 1024 * 1024),
    )(den, sums, small)
    return (
        denoised.transpose(0, 2, 1, 3),
        grad_lift.transpose(2, 0, 1, 3),
        lift_bias,
        grad_mid,
        mid_bias,
        grad_proj.transpose(2, 0, 1, 3),
    )


def whole_kernel(
    dims, scale,
    slc_any, idx_any, tgt_any, wl_any, bl_any, wmid_any, bmid_any, wproj_any,
    den_ref, o_ref, small_ref,
    raw, pool, idx_in, tgt_in, look_s, look_r, tgt_s, tgt_r, fld, tfld, i3a, i3b, h2s, tsum, dn3, dp1, outs, x_ref,
    wl_in, bl_in, wm_in, bm_in, wj_in, w_sem, w1_ref, wp_ref, wpb_ref, wf_ref, wb_ref, bm_ref, wtmp,
    plane_in, date_in, small_in, small_date, slab_sem, plain_sem, sum_sem,
):
    n_row, n_col, n_date, dates, tr, tc = dims
    r, c, d = lax.axis_index("row"), lax.axis_index("col"), lax.axis_index("date")
    n_plane = n_row * n_col
    me = r * n_col + c
    pairs = n_plane
    nb = n_row * tr
    n = nb * 128
    wide = n + 256
    f32, bf16 = jnp.float32, jnp.bfloat16

    def wrapped(value, size):
        return jnp.where(value >= size, value - size, value)

    plane_peers = []
    steps = [(dr, dc) for dr in range(n_row) for dc in range(n_col) if dr or dc]
    for dr, dc in sorted(steps, key=lambda s: (-min(s[1], n_col - s[1]), -min(s[0], n_row - s[0]))):
        row, col = wrapped(r + dr, n_row), wrapped(c + dc, n_col)
        plane_peers.append((row * n_col + col, (row, col, d)))
    date_peers = [(r, c, wrapped(d + k, n_date)) for k in range(1, n_date)]

    def remote_of(src, dst, send_sem, recv_sem, where):
        return pltpu.make_async_remote_copy(
            src_ref=src, dst_ref=dst, send_sem=send_sem, recv_sem=recv_sem,
            device_id=where, device_id_type=MESH,
        )

    def wait_bytes(ref, sem):
        pltpu.make_async_copy(ref, ref, sem).wait()

    barrier = pltpu.get_barrier_semaphore()
    for where in date_peers + [where for _, where in plane_peers]:
        pl.semaphore_signal(barrier, inc=1, device_id=where, device_id_type=MESH)
    fetches = []
    wide_in = zip(
        (slc_any, idx_any, tgt_any, wl_any, bl_any, wmid_any, bmid_any, wproj_any),
        (raw.at[0], idx_in, tgt_in, wl_in, bl_in, wm_in, bm_in, wj_in),
    )
    for k, (src, dst) in enumerate(wide_in):
        copy = pltpu.make_async_copy(src, dst, w_sem.at[min(k, 3)])
        copy.start()
        fetches.append(copy)
    pl.semaphore_wait(barrier, n_plane + n_date - 2)

    halves = tc * LC // 128
    sent = plain_sem.at[0]
    chunk = LR * 128
    depth = pool.shape[0] // (3 * halves)

    def slab_copy(way, t):
        rows = pl.ds(t * LR, LR)
        where = (r, c, lax.max(d - way, 0))
        return remote_of(
            slc_any.at[:, rows], raw.at[way, :, rows], sent, slab_sem.at[(way - 1) * tr + t], where
        )

    sends = (d > 0, d > 1)
    gets = (d < n_date - 1, d < n_date - 2)
    for t in range(tr):
        for way in (2, 1):

            @pl.when(sends[way - 1])
            def _():
                slab_copy(way, t).start()

    pool[...] = jnp.zeros_like(pool)
    for ref in (fld, tfld, dn3, tsum, tgt_s, look_s):
        ref[...] = jnp.zeros_like(ref)
    edge = jnp.zeros((i3a.shape[0], 128), bf16)
    for ref in (i3a, i3b):
        ref[:, 0:128] = edge
        ref[:, (nb + 1) * 128 : (nb + 2) * 128] = edge
    x_ref[608:, :] = jnp.zeros((x_ref.shape[0] - 608, 128), f32)
    outs[...] = jnp.zeros_like(outs)
    lane = lax.broadcasted_iota(jnp.int32, (1, 128), 1)
    for copy in fetches[:3]:
        copy.wait()

    def to_lane(value):
        return pltpu.roll(jnp.concatenate([value, jnp.zeros((value.shape[0], 128 - tc), f32)], axis=1), c * tc, 1)

    for z in range(2):
        for t in range(tr):
            block = to_lane(tgt_in[z, t])
            for k in range(pairs):
                tgt_s[k, z * tr + t : z * tr + t + 1, :] = block[k : k + 1]

    def exchange(src, dst, sem):
        dst[me] = src[me]
        for peer, where in plane_peers:
            remote_of(src.at[peer], dst.at[me], sent, plain_sem.at[sem], where).start()

    def arrived(dst, sem):
        wait_bytes(dst.at[pl.ds(0, n_plane - 1)], plain_sem.at[sem])

    kinds = 2 * halves
    index = idx_in[...] - d * dates
    spread_lanes = jnp.concatenate([index[0:1]] * kinds + [index[1:2]] * kinds, axis=1)
    row_of = lax.broadcasted_iota(jnp.int32, (depth * halves, 2 * kinds * pairs), 0)
    lane_of = lax.broadcasted_iota(jnp.int32, (depth * halves, 2 * kinds * pairs), 1)
    inner = lax.rem(row_of, depth)
    kind = lax.rem(inner, 2) * halves + lax.div(row_of, depth)
    same_kind = (kind == lax.rem(lax.div(lane_of, pairs), kinds)) & (inner < 2 * dates)
    picks = []
    for s in range(3):
        hit = same_kind & (lax.div(inner, 2) + s * dates == spread_lanes)
        picks.append(jnp.where(hit, 1.0, 0.0).astype(f32))
    pick = jnp.concatenate(picks, axis=0).T.astype(bf16)
    spots = lax.broadcasted_iota(jnp.int32, (tc * LC, 128), 0)
    avg_lane = lax.broadcasted_iota(jnp.int32, (tc * LC, 128), 1)
    avg = jnp.where(lax.div(spots, LC) + c * tc == avg_lane, 1.0 / (LR * LC), 0.0).astype(bf16)

    exchange(tgt_s, tgt_r, 1)

    for copy in fetches[3:]:
        copy.wait()
    wtmp[...] = jnp.zeros_like(wtmp)

    def joined(a, b):
        return jnp.concatenate([a, b], axis=1)

    for t in range(3):
        for u in range(3):
            pair = wl_in[t, u].astype(f32)
            at = 8 * t + 2 * u
            wtmp[0, at : at + 1, :] = joined(pair[0:1], pair[1:2])
            wtmp[0, at + 1 : at + 2, :] = joined(-pair[1:2], pair[0:1])
            pair = wj_in[t, u].astype(f32)
            real, imag = joined(pair[0:1], -pair[1:2]), joined(pair[1:2], pair[0:1])
            flip = 8 * (2 - t) + 2 * (2 - u)
            wtmp[1, at : at + 1, :] = real
            wtmp[1, at + 1 : at + 2, :] = imag
            wtmp[2, flip : flip + 1, :] = real
            wtmp[2, flip + 1 : flip + 2, :] = imag
            wr, wi = wm_in[0, t, u].astype(f32), wm_in[1, t, u].astype(f32)
            block = jnp.concatenate([joined(wr, wi), joined(-wi, wr)], axis=0)
            wb_ref[(2 - t) * 128 : (3 - t) * 128, (2 - u) * 128 : (3 - u) * 128] = block.astype(bf16)
            wf_ref[t * 128 : (t + 1) * 128, u * 128 : (u + 1) * 128] = block.T.astype(bf16)
    bias = bl_in[...].astype(f32)
    wtmp[0, 14:15, :] = joined(bias[0:1], bias[1:2])
    bias = bm_in[...].astype(f32)
    wtmp[3, 0:1, :] = joined(bias[0:1], bias[1:2])
    w1_ref[...] = wtmp[0].T[:, 0:32].astype(bf16)
    wp_ref[...] = wtmp[1, 0:32].astype(bf16)
    wpb_ref[...] = wtmp[2].T[:, 0:32].astype(bf16)
    bm_ref[...] = wtmp[3].T[:, 0:1]
    fld[6:7, :] = jnp.ones((1, wide), f32)

    def rounded(value):
        return value.astype(bf16).astype(f32)

    def pack(way, t):
        for q in range(LR):
            for h in range(halves):
                at = (way * halves + h) * depth
                lanes = slice((t * LR + q) * 128, (t * LR + q + 1) * 128)
                pool[at : at + 2 * dates, lanes] = raw[way, :, t * LR + q, :, h * 128 : (h + 1) * 128].reshape(
                    2 * dates, 128
                )

    for t in range(tr):
        pack(0, t)
    for t in range(tr):
        for way in (1, 2):

            @pl.when(gets[way - 1])
            def _():
                slab_copy(way, t).wait_recv()

        for way in (1, 2):

            @pl.when(gets[way - 1])
            def _():
                pack(way, t)

        picked = mm(pick, pool[:, t * chunk : (t + 1) * chunk])
        sides = []
        for h in range(halves):
            a0, a1, b0, b1 = [picked[q * pairs : (q + 1) * pairs] for q in (h, halves + h, 2 * halves + h, 3 * halves + h)]
            both = []
            for prod in (a0 * b0 + a1 * b1, a1 * b0 - a0 * b1):
                both.append(sum(prod[:, q * 128 : (q + 1) * 128] for q in range(LR)))
            sides.append(jnp.concatenate(both, axis=0))
        summed = jnp.concatenate(sides, axis=1)
        high = summed.astype(bf16)
        rest = summed - high.astype(f32)
        middle = rest.astype(bf16)
        low = (rest - middle.astype(f32)).astype(bf16)
        three = mm(jnp.concatenate([high, middle, low], axis=0), avg)
        looked = rounded(three[0 : 2 * pairs] + (three[2 * pairs : 4 * pairs] + three[4 * pairs :]))
        for z in range(2):
            for k in range(pairs):
                at = z * tr + t
                look_s[k, at : at + 1, :] = looked[z * pairs + k : z * pairs + k + 1]
    exchange(look_s, look_r, 2)

    first, last = lane == 0, lane == 127

    def right(value):
        return jnp.where(first, jnp.zeros_like(value), pltpu.roll(value, 1, 1))

    def left(value):
        return jnp.where(last, jnp.zeros_like(value), pltpu.roll(value, 127, 1))

    def assemble(ref, s):
        return functools.reduce(lambda a, b: a + b, [ref[s * n_col + q] for q in range(n_col)])

    arrived(tgt_r, 1)
    for s in range(n_row):
        block = assemble(tgt_r, s)
        for z in range(2):
            for t in range(tr):
                b = s * tr + t
                tfld[z : z + 1, b * 128 : (b + 1) * 128] = block[z * tr + t : z * tr + t + 1]
    arrived(look_r, 2)
    for s in range(n_row):
        block = assemble(look_r, s)
        for u, turned in enumerate((right(block), block, left(block))):
            for z in range(2):
                for t in range(tr):
                    b = s * tr + t + 1
                    fld[2 * u + z : 2 * u + z + 1, b * 128 : (b + 1) * 128] = turned[z * tr + t : z * tr + t + 1]

    def taps(ref, at, width):
        three = [ref[:, at + t * 128 : at + t * 128 + width] for t in range(3)]
        return jnp.concatenate(three + [jnp.zeros((8, width), f32)], axis=0).astype(bf16)

    def turned_store(ref, value, at):
        for q in range(2):
            piece = value[:, q * 128 : (q + 1) * 128].astype(bf16)
            lanes = slice(at + (q + 1) * 128, at + (q + 2) * 128)
            for u, turned in enumerate((right(piece), piece, left(piece))):
                ref[u * 128 : (u + 1) * 128, lanes] = turned

    for at in range(0, n, 256):
        pre1 = mm(w1_ref[...], taps(fld, at, 256))
        turned_store(i3a, jnp.maximum(pre1, 0.0), at)

    def conv(w_ref, ref):
        parts = [mm(w_ref[...], ref[:, at + 128 : at + 384]) for at in range(0, n, 256)]
        edge = jnp.zeros((128, 128), f32)
        for p, part in enumerate(parts):
            above = parts[p - 1][0:128, 128:256] if p else edge
            below = parts[p + 1][256:384, 0:128] if p + 1 < len(parts) else edge
            yield (
                jnp.concatenate([above, part[0:128, 0:128]], axis=1)
                + part[128:256]
                + jnp.concatenate([part[256:384, 128:256], below], axis=1)
            )

    for p, summed in enumerate(conv(wf_ref, i3a)):
        at = p * 256
        pre2 = summed + bm_ref[...]
        h2 = jnp.maximum(pre2, 0.0).astype(bf16)
        h2s[:, at : at + 256] = h2
        tsum[:, at + 128 : at + 384] = mm(wp_ref[...], h2)

    wide_lane = lax.rem(lax.broadcasted_iota(jnp.int32, (1, n), 1), 128)
    wide_first, wide_last = wide_lane == 0, wide_lane == 127

    def wide_right(value):
        return jnp.where(wide_first, 0.0, pltpu.roll(value, 1, 1))

    def wide_left(value):
        return jnp.where(wide_last, 0.0, pltpu.roll(value, n - 1, 1))

    six = sum(tsum[8 * t : 8 * t + 8, t * 128 : t * 128 + n] for t in range(3))
    noise = wide_right(six)[0:2] + six[2:4] + wide_left(six)[4:6]
    den = fld[2:4, 128 : 128 + n] - noise
    for q in range(n_col):
        shifted = pltpu.roll(den, n - q * tc, 1) if q else den
        for s in range(n_row):
            for z in range(2):
                for t in range(tr):
                    i, b = z * tr + t, s * tr + t
                    outs[s * n_col + q, i : i + 1, :] = shifted[z : z + 1, b * 128 : (b + 1) * 128]
    exchange(outs, den_ref, 3)
    dn = rounded((tfld[0:2, :] - den) * scale)
    dn3[0:2, 128 : 128 + n] = wide_right(dn)
    dn3[2:4, 128 : 128 + n] = dn
    dn3[4:6, 128 : 128 + n] = wide_left(dn)

    for at in range(0, n, 256):
        grad = mm(wpb_ref[...], taps(dn3, at, 256)).astype(bf16)
        grad = jnp.where(h2s[:, at : at + 256] > 0, grad, jnp.zeros_like(grad))
        turned_store(i3b, grad, at)

    sizes = (192, 192, 256)
    bases = (0, 192, 384)
    per = [size // n_plane for size in sizes]
    count = len(sizes)

    def piece(ref, j, at):
        return ref.at[pl.ds(pl.multiple_of(bases[j] + at * per[j], 8), per[j])]

    def scatter(j):
        for k, (peer, where) in enumerate(plane_peers):
            dst = plane_in.at[j * n_plane + k, pl.ds(0, per[j])]
            remote_of(piece(x_ref, j, peer), dst, sent, sum_sem.at[j], where).start()

    def across(j):
        wait_bytes(plane_in.at[pl.ds(j * n_plane, n_plane - 1), pl.ds(0, per[j])], sum_sem.at[j])
        part = piece(x_ref, j, me)[...]
        for k in range(n_plane - 1):
            part = part + plane_in[j * n_plane + k, 0 : per[j]]
        slot = date_in.at[j * n_date + d, pl.ds(0, per[j])]
        slot[...] = part
        for where in date_peers:
            remote_of(slot, slot, sent, sum_sem.at[count + j], where).start()

    def spread(j):
        wait_bytes(date_in.at[pl.ds(j * n_date, n_date - 1), pl.ds(0, per[j])], sum_sem.at[count + j])
        mine = piece(o_ref, j, me)
        mine[...] = functools.reduce(lambda a, b: a + b, [date_in[j * n_date + k, 0 : per[j]] for k in range(n_date)])
        for _, where in plane_peers:
            remote_of(mine, mine, sent, sum_sem.at[2 * count + j], where).start()

    sign = jnp.where(lane < 64, 1.0, -1.0)
    dp2 = i3b[128:256, 128 : 128 + n]
    x_ref[576:600, :] = mm_t(taps(dn3, 0, n), h2s[...])[0:24]
    for t in range(3):
        rows = i3a[:, t * 128 : t * 128 + n]
        if t == 2:
            rows = jnp.concatenate([rows, jnp.ones((16, n), bf16)], axis=0)
        gram = mm_t(rows, dp2)
        for u in range(3):
            upper = gram[u * 128 : u * 128 + 64]
            lower = gram[u * 128 + 64 : u * 128 + 128]
            x_ref[(3 * t + u) * 64 : (3 * t + u) * 64 + 64, :] = upper + sign * pltpu.roll(lower, 64, 1)
        if t == 2:
            x_ref[600:608, :] = gram[384:392]
        scatter(t)

    for p, summed in enumerate(conv(wb_ref, i3b)):
        at = p * 256
        grad = summed.astype(bf16)
        h1 = i3a[128:256, at + 128 : at + 384]
        dp1[:, at : at + 256] = jnp.where(h1 > 0, grad, jnp.zeros_like(grad))
    small_in[me] = mm_t(taps(fld, 0, n), dp1[...])[0:24]
    for _, where in plane_peers:
        remote_of(small_in.at[me], small_in.at[me], sent, plain_sem.at[4], where).start()
    for j in range(count):
        across(j)
    wait_bytes(small_in.at[pl.ds(0, n_plane - 1)], plain_sem.at[4])
    small_date[d] = functools.reduce(lambda a, b: a + b, [small_in[k] for k in range(n_plane)])
    for where in date_peers:
        remote_of(small_date.at[d], small_date.at[d], sent, plain_sem.at[5], where).start()
    for j in range(count):
        spread(j)
    wait_bytes(small_date.at[pl.ds(0, n_date - 1)], plain_sem.at[5])
    small_ref[...] = functools.reduce(lambda a, b: a + b, [small_date[k] for k in range(n_date)])
    arrived(den_ref, 3)
    for j in range(count):
        wait_bytes(o_ref.at[pl.ds(0, (n_plane - 1) * per[j])], sum_sem.at[2 * count + j])
    for way in (1, 2):

        @pl.when(sends[way - 1])
        def _():
            wait_bytes(raw.at[0], sent)

    for ref in (tgt_s, look_s, outs):
        wait_bytes(ref.at[pl.ds(0, n_plane - 1)], sent)
    wait_bytes(small_in.at[pl.ds(0, n_plane - 1)], sent)
    wait_bytes(small_date.at[pl.ds(0, n_date - 1)], sent)
    for rows in ((n_plane - 1) * sum(per), (n_date - 1) * sum(per), (n_plane - 1) * sum(per)):
        wait_bytes(x_ref.at[pl.ds(0, rows)], sent)


def whole_finish(dims, den, sums, small, den_out, lift_out, lbias_out, mid_out, mbias_out, proj_out):
    n_plane, tr, tc, ch = dims
    for z in range(2):
        for t in range(tr):
            for k in range(n_plane):
                den_out[z, t, k : k + 1, :] = den[k, z * tr + t : z * tr + t + 1, 0:tc]
    finish_grads(ch, sums, small, lift_out, lbias_out, mid_out, mbias_out, proj_out)


def whole_local(slc, pairs, target, w_lift, b_lift, w_mid, b_mid, w_proj):
    n_row, n_col, n_date = (lax.axis_size(axis) for axis in ("row", "col", "date"))
    dates, srows, scols = slc.shape[1:]
    count, tr, tc = target.shape[1:]
    ch = w_mid.shape[-1]
    halves = scols // 128
    bf16, f32 = jnp.bfloat16, jnp.float32
    images = slc.transpose(1, 2, 0, 3)
    depth = -(-2 * dates // 16) * 16
    tgt = target.transpose(0, 2, 1, 3)
    w_lift, w_proj = w_lift.transpose(1, 2, 0, 3), w_proj.transpose(1, 2, 0, 3)
    scale = 1.0 / math.sqrt(2.0 * count * n_date * tr * n_row * tc * n_col)
    nb = n_row * tr
    n, wide = nb * 128, (nb + 2) * 128
    n_plane = n_row * n_col
    zt = -(-2 * tr // 8) * 8
    dma = pltpu.SemaphoreType.DMA
    vmem = pltpu.VMEM
    shape = jax.ShapeDtypeStruct
    images, index, tgt, w_lift, b_lift, w_mid, b_mid, w_proj = (
        pltpu.with_memory_space_constraint(x, pltpu.HBM)
        for x in (images, pairs.T, tgt, w_lift, b_lift, w_mid, b_mid, w_proj)
    )
    den, sums, small = pl.pallas_call(
        functools.partial(whole_kernel, (n_row, n_col, n_date, dates, tr, tc), scale),
        out_shape=(
            shape((n_plane, zt, 128), f32),
            shape((640, 128), f32),
            shape((24, 128), f32),
        ),
        in_specs=[pl.BlockSpec(memory_space=pltpu.HBM)] * 8,
        out_specs=(pl.BlockSpec(memory_space=vmem),) * 3,
        scratch_shapes=[
            vmem((3,) + images.shape, bf16),
            vmem((3 * halves * depth, srows * 128), bf16),
            vmem((2, count), jnp.int32),
            vmem(tgt.shape, f32),
            vmem((n_plane, zt, 128), f32),
            vmem((n_plane, zt, 128), f32),
            vmem((n_plane, zt, 128), f32),
            vmem((n_plane, zt, 128), f32),
            vmem((8, wide), f32),
            vmem((8, n), f32),
            vmem((6 * ch, wide), bf16),
            vmem((6 * ch, wide), bf16),
            vmem((2 * ch, n), bf16),
            vmem((32, wide), f32),
            vmem((8, wide), f32),
            vmem((2 * ch, n), bf16),
            vmem((n_plane, zt, 128), f32),
            vmem((640, 128), f32),
            vmem(w_lift.shape, bf16),
            vmem(b_lift.shape, bf16),
            vmem(w_mid.shape, bf16),
            vmem(b_mid.shape, bf16),
            vmem(w_proj.shape, bf16),
            dma((4,)),
            vmem((2 * ch, 32), bf16),
            vmem((32, 2 * ch), bf16),
            vmem((2 * ch, 32), bf16),
            vmem((6 * ch, 6 * ch), bf16),
            vmem((6 * ch, 6 * ch), bf16),
            vmem((2 * ch, 1), f32),
            vmem((4, 128, 128), f32),
            vmem((3 * n_plane, 32, 128), f32),
            vmem((3 * n_date, 32, 128), f32),
            vmem((n_plane, 24, 128), f32),
            vmem((n_date, 24, 128), f32),
            dma((2 * tr,)),
            dma((6,)),
            dma((9,)),
        ],
        compiler_params=pltpu.CompilerParams(
            collective_id=0, has_side_effects=True, vmem_limit_bytes=48 * 1024 * 1024
        ),
    )(images, index, tgt, w_lift, b_lift, w_mid, b_mid, w_proj)
    denoised, grad_lift, lift_bias, grad_mid, mid_bias, grad_proj = pl.pallas_call(
        functools.partial(whole_finish, (n_plane, tr, tc, ch)),
        out_shape=(
            shape((2, tr, count, tc), f32),
            shape((3, 3, 2, ch), f32),
            shape((2, ch), f32),
            shape((2, 3, 3, ch, ch), f32),
            shape((2, ch), f32),
            shape((3, 3, 2, ch), f32),
        ),
        in_specs=[pl.BlockSpec(memory_space=vmem)] * 3,
        out_specs=(pl.BlockSpec(memory_space=vmem),) * 6,
        compiler_params=pltpu.CompilerParams(vmem_limit_bytes=8 * 1024 * 1024),
    )(den, sums, small)
    return (
        denoised.transpose(0, 2, 1, 3),
        grad_lift.transpose(2, 0, 1, 3),
        lift_bias,
        grad_mid,
        mid_bias,
        grad_proj.transpose(2, 0, 1, 3),
    )


def local(slc, pairs, target, w_lift, b_lift, w_mid, b_mid, w_proj):
    n_row, n_col = lax.axis_size("row"), lax.axis_size("col")
    count, tr, tc = target.shape[1:]
    whole = (
        count == n_row * n_col
        and tc * n_col == 128
        and (n_row * tr) % 2 == 0
        and 2 * tr <= 8
        and count == 8
        and n_row % 2 == 0
        and w_mid.shape[-1] == 64
        and (2 * slc.shape[1] * slc.shape[3] // 128) % 16 == 0
    )
    return (whole_local if whole else halo_local)(
        slc, pairs, target, w_lift, b_lift, w_mid, b_mid, w_proj
    )


def solution(mesh):
    in_specs = (
        P(None, "date", "row", "col"),
        P("date", None),
        P(None, "date", "row", "col"),
        P(),
        P(),
        P(),
        P(),
        P(),
    )
    out_specs = (P(None, "date", "row", "col"), P(), P(), P(), P(), P())
    return jax.shard_map(local, mesh=mesh, in_specs=in_specs, out_specs=out_specs, check_vma=False)
```

```python
import functools
import math

import jax
import jax.numpy as jnp
from jax import lax
from jax.experimental import pallas as pl
from jax.experimental.pallas import tpu as pltpu
from jax.sharding import PartitionSpec as P

MESH = pl.DeviceIdType.MESH

LR = 2
LC = 4


def mm(a, b):
    return jnp.dot(a, b, preferred_element_type=jnp.float32)


def mm_t(a, b):
    return lax.dot_general(a, b, (((1,), (1,)), ((), ())), preferred_element_type=jnp.float32)


def step_kernel(
    dims, scale,
    slc_ref, pick_ref, avg_ref, tgt_ref, wl_any, bl_any, wmid_any, bmid_any, wproj_any,
    den_ref, o_ref, small_ref,
    pool, look_f, look_s, look_r, tgt_r, fld, tfld, i3a, i3b, h2s, tsum, dn3, dnm3, dp2m, dp1, outs, x_ref,
    wl_in, bl_in, wm_in, bm_in, wj_in, w_sem, w1_ref, wp_ref, wpb_ref, wf_ref, wb_ref, bm_ref, wtmp,
    plane_in, date_in, small_in, small_date, small_sem, small_date_sem, slab_sem, look_sem, tgt_sem, den_sem, plane_sem, date_sem, gather_sem,
):
    n_row, n_col, n_date, pp, tr, tc = dims
    r, c, d = lax.axis_index("row"), lax.axis_index("col"), lax.axis_index("date")
    n_plane = n_row * n_col
    me = r * n_col + c
    rows = n_row * tr
    gap = rows + 1
    nb = gap * pp
    n = nb * 128
    base = (128 - tc) // 2
    pairs = pp * n_row
    f32, bf16 = jnp.float32, jnp.bfloat16

    def plane_peer(k):
        peer = lax.rem(me + k, n_plane)
        return peer, (lax.div(peer, n_col), lax.rem(peer, n_col), d)

    def date_peer(k):
        return (r, c, lax.rem(d + k, n_date))

    def remote(src, dst, sems, at, where):
        copy = pltpu.make_async_remote_copy(
            src_ref=src, dst_ref=dst, send_sem=sems.at[0, at], recv_sem=sems.at[1, at],
            device_id=where, device_id_type=MESH,
        )
        copy.start()
        return copy

    fetches = []
    wide = zip((wl_any, bl_any, wmid_any, bmid_any, wproj_any), (wl_in, bl_in, wm_in, bm_in, wj_in))
    for k, (src, dst) in enumerate(wide):
        copy = pltpu.make_async_copy(src, dst, w_sem.at[k])
        copy.start()
        fetches.append(copy)
    barrier = pltpu.get_barrier_semaphore()
    for k in range(1, n_plane):
        pl.semaphore_signal(barrier, inc=1, device_id=plane_peer(k)[1], device_id_type=MESH)
    for k in range(1, n_date):
        pl.semaphore_signal(barrier, inc=1, device_id=date_peer(k), device_id_type=MESH)
    pl.semaphore_wait(barrier, n_plane + n_date - 2)

    sent = []
    slabs = [remote(slc_ref, pool.at[k - 1], slab_sem, k, date_peer(n_date - k)) for k in (1, 2)]

    def exchange(src, dst, sems):
        copies = []
        for way in range(3):
            col = lax.rem(c + (0, 1, n_col - 1)[way], n_col)
            for o in range(n_row):
                k = lax.rem(r + o, n_row)
                at = way * n_row + o
                if way == 0 and o == 0:
                    copy = pltpu.make_async_copy(src.at[k], dst.at[0, r], sems.at[0, at])
                    copy.start()
                    copies.append((copy, True))
                else:
                    copies.append((remote(src.at[k], dst.at[way, r], sems, at, (k, col, d)), False))
        return copies

    tgt_copies = exchange(tgt_ref, tgt_r, tgt_sem)
    for ref in (fld, tfld, dn3, dnm3, tsum):
        ref[...] = jnp.zeros_like(ref)
    edge = jnp.zeros((i3a.shape[0], 128), bf16)
    for ref in (i3a, i3b):
        ref[:, 0:128] = edge
        ref[:, (nb + 1) * 128 : (nb + 2) * 128] = edge
    x_ref[...] = jnp.zeros_like(x_ref)
    lane = lax.broadcasted_iota(jnp.int32, (1, 128), 1)
    spot = c * tc + lane - base
    inside = (spot >= 0) & (spot < n_col * tc)
    own = (lane >= base) & (lane < base + tc)
    for copy in fetches:
        copy.wait()
    wtmp[...] = jnp.zeros_like(wtmp)

    def joined(a, b):
        return jnp.concatenate([a, b], axis=1)

    for t in range(3):
        for u in range(3):
            pair = wl_in[t, u].astype(f32)
            at = 8 * t + 2 * u
            wtmp[0, at : at + 1, :] = joined(pair[0:1], pair[1:2])
            wtmp[0, at + 1 : at + 2, :] = joined(-pair[1:2], pair[0:1])
            pair = wj_in[t, u].astype(f32)
            real, imag = joined(pair[0:1], -pair[1:2]), joined(pair[1:2], pair[0:1])
            flip = 8 * (2 - t) + 2 * (2 - u)
            wtmp[1, at : at + 1, :] = real
            wtmp[1, at + 1 : at + 2, :] = imag
            wtmp[2, flip : flip + 1, :] = real
            wtmp[2, flip + 1 : flip + 2, :] = imag
            wr, wi = wm_in[0, t, u].astype(f32), wm_in[1, t, u].astype(f32)
            block = jnp.concatenate([joined(wr, wi), joined(-wi, wr)], axis=0)
            wb_ref[2 - t, :, (2 - u) * 128 : (3 - u) * 128] = block.astype(bf16)
            wf_ref[t, :, u * 128 : (u + 1) * 128] = block.T.astype(bf16)
    bias = bl_in[...].astype(f32)
    wtmp[0, 14:15, :] = joined(bias[0:1], bias[1:2])
    bias = bm_in[...].astype(f32)
    wtmp[3, 0:1, :] = joined(bias[0:1], bias[1:2])
    w1_ref[...] = wtmp[0].T[:, 0:32].astype(bf16)
    wp_ref[...] = wtmp[1, 0:32].astype(bf16)
    wpb_ref[...] = wtmp[2].T[:, 0:32].astype(bf16)
    bm_ref[...] = wtmp[3].T[:, 0:1]
    for copy in slabs:
        copy.wait_recv()
    sent += slabs

    depth = slc_ref.shape[0]
    picked = (
        mm(pick_ref[:, :depth], slc_ref[...])
        + mm(pick_ref[:, depth : 2 * depth], pool[0])
        + mm(pick_ref[:, 2 * depth :], pool[1])
    )
    parts = slc_ref.shape[1] // (LR * tr)
    halves = tc * LC // parts
    sides = []
    for h in range(halves):
        at = [picked[q * pairs : (q + 1) * pairs] for q in (h, halves + h, 2 * halves + h, 3 * halves + h)]
        a0, a1, b0, b1 = at
        rowsum = []
        for prod in (a0 * b0 + a1 * b1, a1 * b0 - a0 * b1):
            for t in range(tr):
                rowsum.append(
                    sum(prod[:, (t * LR + q) * parts : (t * LR + q + 1) * parts] for q in range(LR))
                )
        sides.append(jnp.concatenate(rowsum, axis=0))
    looked = jnp.dot(
        jnp.concatenate(sides, axis=1), avg_ref[...],
        precision=lax.Precision.HIGHEST, preferred_element_type=f32,
    )
    look_f[...] = jnp.zeros_like(look_f)
    for k in range(n_row):
        for q in range(2 * tr):
            look_f[k, q * pp : (q + 1) * pp, :] = looked[q * pairs + k * pp : q * pairs + (k + 1) * pp]
    look_s[...] = look_f[...].astype(bf16)
    look_copies = exchange(look_s, look_r, look_sem)

    def settle(copies):
        for copy, near in copies:
            if near:
                copy.wait()
            else:
                copy.wait_recv()
                sent.append(copy)

    def assemble(ref, s):
        mid = pltpu.roll(ref[0, s].astype(f32), base, 1)
        low = pltpu.roll(ref[1, s].astype(f32), (base - tc) % 128, 1)
        high = pltpu.roll(ref[2, s].astype(f32), base + tc, 1)
        joined = jnp.where(own, mid, jnp.where(lane < base, low, high))
        near = (lane >= base - 5) & (lane < base + tc + 5)
        return jnp.where(inside & near, joined, 0.0)

    settle(tgt_copies)
    for s in range(n_row):
        block = assemble(tgt_r, s)
        for z in range(2):
            for t in range(tr):
                for p in range(pp):
                    i = (z * tr + t) * pp + p
                    b = p * gap + s * tr + t
                    tfld[z : z + 1, b * 128 : (b + 1) * 128] = block[i : i + 1]
    settle(look_copies)
    for s in range(n_row):
        block = assemble(look_r, s)
        for u, turned in enumerate((pltpu.roll(block, 1, 1), block, pltpu.roll(block, 127, 1))):
            for z in range(2):
                for t in range(tr):
                    for p in range(pp):
                        i = (z * tr + t) * pp + p
                        b = p * gap + s * tr + t + 1
                        fld[2 * u + z : 2 * u + z + 1, b * 128 : (b + 1) * 128] = turned[i : i + 1]
    fld[6:7, :] = jnp.ones((1, (nb + 2) * 128), f32)

    def taps(ref, at, width):
        three = [ref[:, pl.ds(pl.multiple_of(at + t * 128, 128), width)] for t in range(3)]
        return jnp.concatenate(three + [jnp.zeros((8, width), f32)], axis=0).astype(bf16)

    def turned_store(ref, value, at):
        for u, turn in enumerate((1, 0, 127)):
            for q in range(2):
                piece = value[:, q * 128 : (q + 1) * 128]
                if turn:
                    piece = pltpu.roll(piece, turn, 1)
                ref[u * 128 : (u + 1) * 128, pl.ds(pl.multiple_of(at + (q + 1) * 128, 128), 128)] = (
                    piece.astype(bf16)
                )

    def good(b):
        one = [inside & (lax.rem(b + q, gap) != gap - 1) for q in range(2)]
        return jnp.concatenate(one, axis=1)

    own2 = jnp.concatenate([own, own], axis=1)

    def rounded(value):
        return value.astype(bf16).astype(f32)

    def lift(i, carry):
        at = pl.multiple_of(i * 256, 256)
        pre1 = mm(w1_ref[...], taps(fld, at, 256))
        turned_store(i3a, rounded(jnp.where(good(2 * i), jnp.maximum(pre1, 0.0), 0.0)), at)
        return carry

    lax.fori_loop(0, nb // 2, lift, 0, unroll=True)

    def conv(w_ref, ref, at):
        total = 0.0
        for t in range(3):
            total = total + mm(w_ref[t], ref[:, pl.ds(pl.multiple_of(at + t * 128, 128), 256)])
        return total

    def mid(i, carry):
        at = pl.multiple_of(i * 256, 256)
        pre2 = conv(wf_ref, i3a, at) + bm_ref[...]
        h2 = jnp.where(good(2 * i), jnp.maximum(pre2, 0.0), 0.0).astype(bf16)
        h2s[:, pl.ds(at, 256)] = h2
        tsum[:, pl.ds(pl.multiple_of(at + 128, 128), 256)] = mm(wp_ref[...], h2)
        return carry

    lax.fori_loop(0, nb // 2, mid, 0, unroll=True)

    six = sum(tsum[8 * t : 8 * t + 8, t * 128 : t * 128 + n] for t in range(3))
    noise = pltpu.roll(six, 1, 1)[0:2] + six[2:4] + pltpu.roll(six, n - 1, 1)[4:6]
    den = fld[2:4, 128 : 128 + n] - noise
    shifted = pltpu.roll(den, n - base, 1)
    outs[...] = jnp.zeros_like(outs)
    for s in range(n_row):
        for z in range(2):
            for t in range(tr):
                for p in range(pp):
                    i = (z * tr + t) * pp + p
                    b = p * gap + s * tr + t
                    outs[s, i : i + 1, :] = shifted[z : z + 1, b * 128 : (b + 1) * 128]
    den_copies = []
    for o in range(n_row):
        k = lax.rem(r + o, n_row)
        if o == 0:
            copy = pltpu.make_async_copy(outs.at[k], den_ref.at[r], den_sem.at[0, o])
            copy.start()
            den_copies.append((copy, True))
        else:
            den_copies.append((remote(outs.at[k], den_ref.at[r], den_sem, o, (k, c, d)), False))
    dn = rounded((tfld[0:2, :] - den) * scale)
    rowok = [jnp.full((1, 128), b % gap != gap - 1) for b in range(nb)]
    mask = jnp.concatenate([inside & ok for ok in rowok], axis=1)
    own_all = jnp.concatenate([own & ok for ok in rowok], axis=1)
    for ref, keep in ((dn3, mask), (dnm3, own_all)):
        kept = jnp.where(keep, dn, 0.0)
        ref[0:2, 128 : 128 + n] = pltpu.roll(kept, 1, 1)
        ref[2:4, 128 : 128 + n] = kept
        ref[4:6, 128 : 128 + n] = pltpu.roll(kept, n - 1, 1)

    def back2(i, carry):
        at = pl.multiple_of(i * 256, 256)
        grad = mm(wpb_ref[...], taps(dn3, at, 256))
        grad = rounded(jnp.where(h2s[:, pl.ds(at, 256)].astype(f32) > 0, grad, 0.0))
        turned_store(i3b, grad, at)
        dp2m[:, pl.ds(at, 256)] = jnp.where(own2, grad, 0.0).astype(bf16)
        return carry

    lax.fori_loop(0, nb // 2, back2, 0, unroll=True)

    sign = jnp.where(lane < 64, 1.0, -1.0)
    for t in range(3):
        gram = mm_t(i3a[:, t * 128 : t * 128 + n], dp2m[...])
        for u in range(3):
            upper = gram[u * 128 : u * 128 + 64]
            lower = gram[u * 128 + 64 : u * 128 + 128]
            x_ref[(3 * t + u) * 64 : (3 * t + u) * 64 + 64, :] = upper + sign * pltpu.roll(lower, 64, 1)
    x_ref[576:600, :] = mm_t(taps(dnm3, 0, n), h2s[...])[0:24]
    x_ref[600:608, :] = mm_t(jnp.ones((16, n), bf16), dp2m[...])[0:8]

    piece = plane_in.shape[1]

    def slot(ref, k):
        return ref.at[pl.ds(pl.multiple_of(k * piece, 8), piece)]

    scatter = []
    for k in range(1, n_plane):
        peer, where = plane_peer(k)
        scatter.append(remote(slot(x_ref, peer), plane_in.at[k], plane_sem, k, where))

    def back1(i, carry):
        at = pl.multiple_of(i * 256, 256)
        h1 = i3a[128:256, pl.ds(pl.multiple_of(at + 128, 128), 256)].astype(f32)
        grad = jnp.where((h1 > 0) & own2, conv(wb_ref, i3b, at), 0.0)
        dp1[:, pl.ds(at, 256)] = grad.astype(bf16)
        return carry

    lax.fori_loop(0, nb // 2, back1, 0, unroll=True)

    small_in[me] = mm_t(taps(fld, 0, n), dp1[...])[0:24]
    small = [
        remote(small_in.at[me], small_in.at[me], small_sem, k, plane_peer(k)[1]) for k in range(1, n_plane)
    ]
    part = slot(x_ref, me)[...]
    for k, copy in zip(range(1, n_plane), scatter):
        copy.wait_recv()
        part = part + plane_in[k]
    date_in[d] = part
    spread = [remote(date_in.at[d], date_in.at[d], date_sem, k, date_peer(k)) for k in range(1, n_date)]

    def total(ref, count):
        return functools.reduce(lambda a, b: a + b, [ref[k] for k in range(count)])

    for copy in small:
        copy.wait_recv()
    small_date[d] = total(small_in, n_plane)
    small_spread = [
        remote(small_date.at[d], small_date.at[d], small_date_sem, k, date_peer(k)) for k in range(1, n_date)
    ]
    for copy in spread:
        copy.wait_recv()
    slot(o_ref, me)[...] = total(date_in, n_date)
    gather = [
        remote(slot(o_ref, me), slot(o_ref, me), gather_sem, k, plane_peer(k)[1])
        for k in range(1, n_plane)
    ]
    for copy in small_spread:
        copy.wait_recv()
    small_ref[...] = total(small_date, n_date)
    settle(den_copies)
    for copy in gather:
        copy.wait_recv()
    for copy in sent + scatter + small + spread + small_spread + gather:
        copy.wait_send()


def finish_kernel(dims, den, sums, small, den_out, lift_out, lbias_out, mid_out, mbias_out, proj_out):
    n_row, pp, tr, tc, ch = dims
    for k in range(n_row):
        for z in range(2):
            for t in range(tr):
                at = (z * tr + t) * pp
                den_out[z, t, k * pp : (k + 1) * pp, :] = den[k, at : at + pp, 0:tc]
    finish_grads(ch, sums, small, lift_out, lbias_out, mid_out, mbias_out, proj_out)


def finish_grads(ch, sums, small, lift_out, lbias_out, mid_out, mbias_out, proj_out):
    for t in range(3):
        for u in range(3):
            at = 8 * t + 2 * u
            upper, lower = small[at : at + 1, :], small[at + 1 : at + 2, :]
            lift_out[t, u, 0:1, :] = upper[:, 0:ch] + lower[:, ch:]
            lift_out[t, u, 1:2, :] = upper[:, ch:] - lower[:, 0:ch]
            at = 576 + 8 * (2 - t) + 2 * (2 - u)
            upper, lower = sums[at : at + 1, :], sums[at + 1 : at + 2, :]
            proj_out[t, u, 0:1, :] = upper[:, 0:ch] + lower[:, ch:]
            proj_out[t, u, 1:2, :] = lower[:, 0:ch] - upper[:, ch:]
            at = (3 * t + u) * ch
            for z in range(2):
                mid_out[z, t, u] = sums[at : at + ch, z * ch : (z + 1) * ch]
    for z in range(2):
        lbias_out[z : z + 1, :] = small[14:15, z * ch : (z + 1) * ch]
        mbias_out[z : z + 1, :] = sums[600:601, z * ch : (z + 1) * ch]


def halo_local(slc, pairs, target, w_lift, b_lift, w_mid, b_mid, w_proj):
    n_row, n_col, n_date = (lax.axis_size(axis) for axis in ("row", "col", "date"))
    dates, srows, scols = slc.shape[1:]
    count, tr, tc = target.shape[1:]
    ch = w_mid.shape[-1]
    pp = count // n_row
    halves = scols // 128
    bf16, f32 = jnp.bfloat16, jnp.float32
    rows = 2 * tr * pp
    pad_rows = -(-rows // 16) * 16
    packed = slc.reshape(2, dates, srows, halves, 128).transpose(1, 0, 3, 2, 4)
    packed = packed.reshape(dates * 2 * halves, srows * 128)
    index = (pairs - lax.axis_index("date") * dates).T
    kinds = 2 * halves
    want = (index[:, None, :] * kinds + jnp.arange(kinds, dtype=jnp.int32)[None, :, None]).reshape(-1)
    pick = (want[:, None] == jnp.arange(3 * dates * kinds, dtype=jnp.int32)[None, :]).astype(bf16)
    spots = jnp.arange(scols, dtype=jnp.int32)[:, None] // LC
    avg = jnp.where(spots == jnp.arange(128, dtype=jnp.int32)[None, :], 1.0 / (LR * LC), 0.0).astype(f32)
    tgt = target.reshape(2, n_row, pp, tr, tc).transpose(1, 0, 3, 2, 4).reshape(n_row, rows, tc)
    tgt = jnp.pad(tgt, ((0, 0), (0, pad_rows - rows), (0, 128 - tc)))
    w_lift, w_proj = w_lift.transpose(1, 2, 0, 3), w_proj.transpose(1, 2, 0, 3)
    scale = 1.0 / math.sqrt(2.0 * count * n_date * tr * n_row * tc * n_col)
    nb = (n_row * tr + 1) * pp
    n, wide = nb * 128, (nb + 2) * 128
    n_plane = n_row * n_col
    piece = -(-608 // (8 * n_plane)) * 8
    dma = pltpu.SemaphoreType.DMA
    vmem = pltpu.VMEM
    den, sums, small = pl.pallas_call(
        functools.partial(step_kernel, (n_row, n_col, n_date, pp, tr, tc), scale),
        out_shape=(
            jax.ShapeDtypeStruct((n_row, pad_rows, 128), f32),
            jax.ShapeDtypeStruct((n_plane * piece, 128), f32),
            jax.ShapeDtypeStruct((24, 128), f32),
        ),
        in_specs=[pl.BlockSpec(memory_space=vmem)] * 4 + [pl.BlockSpec(memory_space=pl.ANY)] * 5,
        out_specs=(pl.BlockSpec(memory_space=vmem),) * 3,
        scratch_shapes=[
            vmem((2,) + packed.shape, bf16),
            vmem((n_row, pad_rows, 128), f32),
            vmem((n_row, pad_rows, 128), bf16),
            vmem((3, n_row, pad_rows, 128), bf16),
            vmem((3, n_row, pad_rows, 128), f32),
            vmem((8, wide), f32),
            vmem((8, n), f32),
            vmem((6 * ch, wide), bf16),
            vmem((6 * ch, wide), bf16),
            vmem((2 * ch, n), bf16),
            vmem((32, wide), f32),
            vmem((8, wide), f32),
            vmem((8, wide), f32),
            vmem((2 * ch, n), bf16),
            vmem((2 * ch, n), bf16),
            vmem((n_row, pad_rows, 128), f32),
            vmem((n_plane * piece, 128), f32),
            vmem(w_lift.shape, bf16),
            vmem(b_lift.shape, bf16),
            vmem(w_mid.shape, bf16),
            vmem(b_mid.shape, bf16),
            vmem(w_proj.shape, bf16),
            dma((5,)),
            vmem((2 * ch, 32), bf16),
            vmem((32, 2 * ch), bf16),
            vmem((2 * ch, 32), bf16),
            vmem((3, 2 * ch, 6 * ch), bf16),
            vmem((3, 2 * ch, 6 * ch), bf16),
            vmem((2 * ch, 1), f32),
            vmem((4, 128, 128), f32),
            vmem((n_plane, piece, 128), f32),
            vmem((n_date, piece, 128), f32),
            vmem((n_plane, 24, 128), f32),
            vmem((n_date, 24, 128), f32),
            dma((2, n_plane)),
            dma((2, n_date)),
            dma((2, 3)),
            dma((2, 3 * n_row)),
            dma((2, 3 * n_row)),
            dma((2, n_row)),
            dma((2, n_plane)),
            dma((2, n_date)),
            dma((2, n_plane)),
        ],
        compiler_params=pltpu.CompilerParams(
            collective_id=0, has_side_effects=True, vmem_limit_bytes=48 * 1024 * 1024
        ),
    )(packed, pick, avg, tgt, w_lift, b_lift, w_mid, b_mid, w_proj)
    shape = jax.ShapeDtypeStruct
    denoised, grad_lift, lift_bias, grad_mid, mid_bias, grad_proj = pl.pallas_call(
        functools.partial(finish_kernel, (n_row, pp, tr, tc, ch)),
        out_shape=(
            shape((2, tr, count, tc), f32),
            shape((3, 3, 2, ch), f32),
            shape((2, ch), f32),
            shape((2, 3, 3, ch, ch), f32),
            shape((2, ch), f32),
            shape((3, 3, 2, ch), f32),
        ),
        in_specs=[pl.BlockSpec(memory_space=vmem)] * 3,
        out_specs=(pl.BlockSpec(memory_space=vmem),) * 6,
        compiler_params=pltpu.CompilerParams(vmem_limit_bytes=8 * 1024 * 1024),
    )(den, sums, small)
    return (
        denoised.transpose(0, 2, 1, 3),
        grad_lift.transpose(2, 0, 1, 3),
        lift_bias,
        grad_mid,
        mid_bias,
        grad_proj.transpose(2, 0, 1, 3),
    )


def whole_kernel(
    dims, scale,
    slc_any, idx_any, tgt_any, wl_any, bl_any, wmid_any, bmid_any, wproj_any,
    den_ref, o_ref, small_ref,
    raw, pool, idx_in, tgt_in, look_s, look_r, tgt_s, tgt_r, fld, tfld, i3a, i3b, h2s, tsum, dn3, dp1, outs, x_ref,
    wl_in, bl_in, wm_in, bm_in, wj_in, w_sem, w1_ref, wp_ref, wpb_ref, wf_ref, wb_ref, bm_ref, wtmp,
    plane_in, date_in, small_in, small_date, slab_sem, plain_sem, sum_sem,
):
    n_row, n_col, n_date, dates, tr, tc = dims
    r, c, d = lax.axis_index("row"), lax.axis_index("col"), lax.axis_index("date")
    n_plane = n_row * n_col
    ch = wm_in.shape[-1]
    extra = 9 * ch
    me = r * n_col + c
    pairs = n_plane
    nb = n_row * tr
    n = nb * 128
    wide = n + 256
    f32, bf16 = jnp.float32, jnp.bfloat16

    def wrapped(value, size):
        return jnp.where(value >= size, value - size, value)

    plane_peers = []
    steps = [(dr, dc) for dr in range(n_row) for dc in range(n_col) if dr or dc]
    for dr, dc in sorted(steps, key=lambda s: (-min(s[1], n_col - s[1]), -min(s[0], n_row - s[0]))):
        row, col = wrapped(r + dr, n_row), wrapped(c + dc, n_col)
        plane_peers.append((row * n_col + col, (row, col, d)))
    date_peers = [(r, c, wrapped(d + k, n_date)) for k in range(1, n_date)]

    def remote_of(src, dst, send_sem, recv_sem, where):
        return pltpu.make_async_remote_copy(
            src_ref=src, dst_ref=dst, send_sem=send_sem, recv_sem=recv_sem,
            device_id=where, device_id_type=MESH,
        )

    def wait_bytes(ref, sem):
        pltpu.make_async_copy(ref, ref, sem).wait()

    barrier = pltpu.get_barrier_semaphore()
    for where in date_peers + [where for _, where in plane_peers]:
        pl.semaphore_signal(barrier, inc=1, device_id=where, device_id_type=MESH)
    fetches = []
    wide_in = zip(
        (slc_any, idx_any, tgt_any, wl_any, bl_any, wmid_any, bmid_any, wproj_any),
        (raw.at[0], idx_in, tgt_in, wl_in, bl_in, wm_in, bm_in, wj_in),
    )
    for k, (src, dst) in enumerate(wide_in):
        copy = pltpu.make_async_copy(src, dst, w_sem.at[min(k, 3)])
        copy.start()
        fetches.append(copy)
    pl.semaphore_wait(barrier, n_plane + n_date - 2)

    halves = tc * LC // 128
    sent = plain_sem.at[0]
    chunk = LR * 128
    depth = pool.shape[0] // (3 * halves)

    def slab_copy(way, t):
        rows = pl.ds(t * LR, LR)
        where = (r, c, lax.max(d - way, 0))
        return remote_of(
            slc_any.at[:, rows], raw.at[way, :, rows], sent, slab_sem.at[(way - 1) * tr + t], where
        )

    sends = (d > 0, d > 1)
    gets = (d < n_date - 1, d < n_date - 2)
    for t in range(tr):
        for way in (2, 1):

            @pl.when(sends[way - 1])
            def _():
                slab_copy(way, t).start()

    pool[...] = jnp.zeros_like(pool)
    for ref in (fld, tfld, dn3, tsum, tgt_s, look_s):
        ref[...] = jnp.zeros_like(ref)
    edge = jnp.zeros((i3a.shape[0], 128), bf16)
    for ref in (i3a, i3b):
        ref[:, 0:128] = edge
        ref[:, (nb + 1) * 128 : (nb + 2) * 128] = edge
    x_ref[extra + 32 :, :] = jnp.zeros((x_ref.shape[0] - extra - 32, 128), f32)
    outs[...] = jnp.zeros_like(outs)
    lane = lax.broadcasted_iota(jnp.int32, (1, 128), 1)
    for copy in fetches[:3]:
        copy.wait()

    def to_lane(value):
        return pltpu.roll(jnp.concatenate([value, jnp.zeros((value.shape[0], 128 - tc), f32)], axis=1), c * tc, 1)

    for z in range(2):
        for t in range(tr):
            block = to_lane(tgt_in[z, t])
            for k in range(pairs):
                tgt_s[k, z * tr + t : z * tr + t + 1, :] = block[k : k + 1]

    def exchange(src, dst, sem):
        dst[me] = src[me]
        for peer, where in plane_peers:
            remote_of(src.at[peer], dst.at[me], sent, plain_sem.at[sem], where).start()

    def arrived(dst, sem):
        wait_bytes(dst.at[pl.ds(0, n_plane - 1)], plain_sem.at[sem])

    kinds = 2 * halves
    index = idx_in[...] - d * dates
    spread_lanes = jnp.concatenate([index[0:1]] * kinds + [index[1:2]] * kinds, axis=1)
    row_of = lax.broadcasted_iota(jnp.int32, (depth * halves, 2 * kinds * pairs), 0)
    lane_of = lax.broadcasted_iota(jnp.int32, (depth * halves, 2 * kinds * pairs), 1)
    inner = lax.rem(row_of, depth)
    kind = lax.rem(inner, 2) * halves + lax.div(row_of, depth)
    same_kind = (kind == lax.rem(lax.div(lane_of, pairs), kinds)) & (inner < 2 * dates)
    picks = []
    for s in range(3):
        hit = same_kind & (lax.div(inner, 2) + s * dates == spread_lanes)
        picks.append(jnp.where(hit, 1.0, 0.0).astype(f32))
    pick = jnp.concatenate(picks, axis=0).T.astype(bf16)
    spots = lax.broadcasted_iota(jnp.int32, (tc * LC, 128), 0)
    avg_lane = lax.broadcasted_iota(jnp.int32, (tc * LC, 128), 1)
    avg = jnp.where(lax.div(spots, LC) + c * tc == avg_lane, 1.0 / (LR * LC), 0.0).astype(bf16)

    exchange(tgt_s, tgt_r, 1)

    for copy in fetches[3:]:
        copy.wait()
    wtmp[...] = jnp.zeros_like(wtmp)

    def joined(a, b):
        return jnp.concatenate([a, b], axis=1)

    for t in range(3):
        for u in range(3):
            pair = wl_in[t, u].astype(f32)
            at = 8 * t + 2 * u
            wtmp[0, at : at + 1, :] = joined(pair[0:1], pair[1:2])
            wtmp[0, at + 1 : at + 2, :] = joined(-pair[1:2], pair[0:1])
            pair = wj_in[t, u].astype(f32)
            real, imag = joined(pair[0:1], -pair[1:2]), joined(pair[1:2], pair[0:1])
            flip = 8 * (2 - t) + 2 * (2 - u)
            wtmp[1, at : at + 1, :] = real
            wtmp[1, at + 1 : at + 2, :] = imag
            wtmp[2, flip : flip + 1, :] = real
            wtmp[2, flip + 1 : flip + 2, :] = imag
            wr, wi = wm_in[0, t, u].astype(f32), wm_in[1, t, u].astype(f32)
            block = jnp.concatenate([joined(wr, wi), joined(-wi, wr)], axis=0)
            wb_ref[(2 - t) * 128 : (3 - t) * 128, (2 - u) * 128 : (3 - u) * 128] = block.astype(bf16)
            wf_ref[t * 128 : (t + 1) * 128, u * 128 : (u + 1) * 128] = block.T.astype(bf16)
    bias = bl_in[...].astype(f32)
    wtmp[0, 14:15, :] = joined(bias[0:1], bias[1:2])
    bias = bm_in[...].astype(f32)
    wtmp[3, 0:1, :] = joined(bias[0:1], bias[1:2])
    w1_ref[...] = wtmp[0].T[:, 0:32].astype(bf16)
    wp_ref[...] = wtmp[1, 0:32].astype(bf16)
    wpb_ref[...] = wtmp[2].T[:, 0:32].astype(bf16)
    bm_ref[...] = wtmp[3].T[:, 0:1]
    fld[6:7, :] = jnp.ones((1, wide), f32)

    def rounded(value):
        return value.astype(bf16).astype(f32)

    def pack(way, t):
        for q in range(LR):
            for h in range(halves):
                at = (way * halves + h) * depth
                lanes = slice((t * LR + q) * 128, (t * LR + q + 1) * 128)
                pool[at : at + 2 * dates, lanes] = raw[way, :, t * LR + q, :, h * 128 : (h + 1) * 128].reshape(
                    2 * dates, 128
                )

    for t in range(tr):
        pack(0, t)
    for t in range(tr):
        for way in (1, 2):

            @pl.when(gets[way - 1])
            def _():
                slab_copy(way, t).wait_recv()

        for way in (1, 2):

            @pl.when(gets[way - 1])
            def _():
                pack(way, t)

        picked = mm(pick, pool[:, t * chunk : (t + 1) * chunk])
        sides = []
        for h in range(halves):
            a0, a1, b0, b1 = [picked[q * pairs : (q + 1) * pairs] for q in (h, halves + h, 2 * halves + h, 3 * halves + h)]
            both = []
            for prod in (a0 * b0 + a1 * b1, a1 * b0 - a0 * b1):
                both.append(sum(prod[:, q * 128 : (q + 1) * 128] for q in range(LR)))
            sides.append(jnp.concatenate(both, axis=0))
        summed = jnp.concatenate(sides, axis=1)
        high = summed.astype(bf16)
        rest = summed - high.astype(f32)
        middle = rest.astype(bf16)
        low = (rest - middle.astype(f32)).astype(bf16)
        three = mm(jnp.concatenate([high, middle, low], axis=0), avg)
        looked = rounded(three[0 : 2 * pairs] + (three[2 * pairs : 4 * pairs] + three[4 * pairs :]))
        for z in range(2):
            for k in range(pairs):
                at = z * tr + t
                look_s[k, at : at + 1, :] = looked[z * pairs + k : z * pairs + k + 1]
    exchange(look_s, look_r, 2)

    first, last = lane == 0, lane == 127

    def right(value):
        return jnp.where(first, jnp.zeros_like(value), pltpu.roll(value, 1, 1))

    def left(value):
        return jnp.where(last, jnp.zeros_like(value), pltpu.roll(value, 127, 1))

    def assemble(ref, s):
        return functools.reduce(lambda a, b: a + b, [ref[s * n_col + q] for q in range(n_col)])

    arrived(tgt_r, 1)
    for s in range(n_row):
        block = assemble(tgt_r, s)
        for z in range(2):
            for t in range(tr):
                b = s * tr + t
                tfld[z : z + 1, b * 128 : (b + 1) * 128] = block[z * tr + t : z * tr + t + 1]
    arrived(look_r, 2)
    for s in range(n_row):
        block = assemble(look_r, s)
        for u, turned in enumerate((right(block), block, left(block))):
            for z in range(2):
                for t in range(tr):
                    b = s * tr + t + 1
                    fld[2 * u + z : 2 * u + z + 1, b * 128 : (b + 1) * 128] = turned[z * tr + t : z * tr + t + 1]

    def taps(ref, at, width):
        three = [ref[:, at + t * 128 : at + t * 128 + width] for t in range(3)]
        return jnp.concatenate(three + [jnp.zeros((8, width), f32)], axis=0).astype(bf16)

    def turned_store(ref, value, at):
        for q in range(2):
            piece = value[:, q * 128 : (q + 1) * 128].astype(bf16)
            lanes = slice(at + (q + 1) * 128, at + (q + 2) * 128)
            for u, turned in enumerate((right(piece), piece, left(piece))):
                ref[u * 128 : (u + 1) * 128, lanes] = turned

    for at in range(0, n, 256):
        pre1 = mm(w1_ref[...], taps(fld, at, 256))
        turned_store(i3a, jnp.maximum(pre1, 0.0), at)

    def conv(w_ref, ref):
        parts = [mm(w_ref[...], ref[:, at + 128 : at + 384]) for at in range(0, n, 256)]
        edge = jnp.zeros((128, 128), f32)
        for p, part in enumerate(parts):
            above = parts[p - 1][0:128, 128:256] if p else edge
            below = parts[p + 1][256:384, 0:128] if p + 1 < len(parts) else edge
            yield (
                jnp.concatenate([above, part[0:128, 0:128]], axis=1)
                + part[128:256]
                + jnp.concatenate([part[256:384, 128:256], below], axis=1)
            )

    for p, summed in enumerate(conv(wf_ref, i3a)):
        at = p * 256
        pre2 = summed + bm_ref[...]
        h2 = jnp.maximum(pre2, 0.0).astype(bf16)
        h2s[:, at : at + 256] = h2
        tsum[:, at + 128 : at + 384] = mm(wp_ref[...], h2)

    wide_lane = lax.rem(lax.broadcasted_iota(jnp.int32, (1, n), 1), 128)
    wide_first, wide_last = wide_lane == 0, wide_lane == 127

    def wide_right(value):
        return jnp.where(wide_first, 0.0, pltpu.roll(value, 1, 1))

    def wide_left(value):
        return jnp.where(wide_last, 0.0, pltpu.roll(value, n - 1, 1))

    six = sum(tsum[8 * t : 8 * t + 8, t * 128 : t * 128 + n] for t in range(3))
    noise = wide_right(six)[0:2] + six[2:4] + wide_left(six)[4:6]
    den = fld[2:4, 128 : 128 + n] - noise
    for q in range(n_col):
        shifted = pltpu.roll(den, n - q * tc, 1) if q else den
        for s in range(n_row):
            for z in range(2):
                for t in range(tr):
                    i, b = z * tr + t, s * tr + t
                    outs[s * n_col + q, i : i + 1, :] = shifted[z : z + 1, b * 128 : (b + 1) * 128]
    exchange(outs, den_ref, 3)
    dn = rounded((tfld[0:2, :] - den) * scale)
    dn3[0:2, 128 : 128 + n] = wide_right(dn)
    dn3[2:4, 128 : 128 + n] = dn
    dn3[4:6, 128 : 128 + n] = wide_left(dn)

    for at in range(0, n, 256):
        grad = mm(wpb_ref[...], taps(dn3, at, 256)).astype(bf16)
        grad = jnp.where(h2s[:, at : at + 256] > 0, grad, jnp.zeros_like(grad))
        turned_store(i3b, grad, at)

    sizes = (3 * ch, 3 * ch, 4 * ch)
    bases = (0, 3 * ch, 6 * ch)
    per = [size // n_plane for size in sizes]
    count = len(sizes)

    def piece(ref, j, at):
        return ref.at[pl.ds(pl.multiple_of(bases[j] + at * per[j], 8), per[j])]

    def scatter(j):
        for k, (peer, where) in enumerate(plane_peers):
            dst = plane_in.at[j * n_plane + k, pl.ds(0, per[j])]
            remote_of(piece(x_ref, j, peer), dst, sent, sum_sem.at[j], where).start()

    def across(j):
        wait_bytes(plane_in.at[pl.ds(j * n_plane, n_plane - 1), pl.ds(0, per[j])], sum_sem.at[j])
        part = piece(x_ref, j, me)[...]
        for k in range(n_plane - 1):
            part = part + plane_in[j * n_plane + k, 0 : per[j]]
        slot = date_in.at[j * n_date + d, pl.ds(0, per[j])]
        slot[...] = part
        for where in date_peers:
            remote_of(slot, slot, sent, sum_sem.at[count + j], where).start()

    def spread(j):
        wait_bytes(date_in.at[pl.ds(j * n_date, n_date - 1), pl.ds(0, per[j])], sum_sem.at[count + j])
        mine = piece(o_ref, j, me)
        mine[...] = functools.reduce(lambda a, b: a + b, [date_in[j * n_date + k, 0 : per[j]] for k in range(n_date)])
        for _, where in plane_peers:
            remote_of(mine, mine, sent, sum_sem.at[2 * count + j], where).start()

    sign = jnp.where(lane < ch, 1.0, -1.0)
    dp2 = i3b[128:256, 128 : 128 + n]
    x_ref[extra : extra + 24, :] = mm_t(taps(dn3, 0, n), h2s[...])[0:24]
    for t in range(3):
        rows = i3a[:, t * 128 : t * 128 + n]
        if t == 2:
            rows = jnp.concatenate([rows, jnp.ones((16, n), bf16)], axis=0)
        gram = mm_t(rows, dp2)
        for u in range(3):
            upper = gram[u * 128 : u * 128 + ch]
            lower = gram[u * 128 + ch : u * 128 + 128]
            x_ref[(3 * t + u) * ch : (3 * t + u + 1) * ch, :] = upper + sign * pltpu.roll(lower, ch, 1)
        if t == 2:
            x_ref[extra + 24 : extra + 32, :] = gram[384:392]
        scatter(t)

    for p, summed in enumerate(conv(wb_ref, i3b)):
        at = p * 256
        grad = summed.astype(bf16)
        h1 = i3a[128:256, at + 128 : at + 384]
        dp1[:, at : at + 256] = jnp.where(h1 > 0, grad, jnp.zeros_like(grad))
    small_in[me] = mm_t(taps(fld, 0, n), dp1[...])[0:24]
    for _, where in plane_peers:
        remote_of(small_in.at[me], small_in.at[me], sent, plain_sem.at[4], where).start()
    for j in range(count):
        across(j)
    wait_bytes(small_in.at[pl.ds(0, n_plane - 1)], plain_sem.at[4])
    small_date[d] = functools.reduce(lambda a, b: a + b, [small_in[k] for k in range(n_plane)])
    for where in date_peers:
        remote_of(small_date.at[d], small_date.at[d], sent, plain_sem.at[5], where).start()
    for j in range(count):
        spread(j)
    wait_bytes(small_date.at[pl.ds(0, n_date - 1)], plain_sem.at[5])
    small_ref[...] = functools.reduce(lambda a, b: a + b, [small_date[k] for k in range(n_date)])
    arrived(den_ref, 3)
    for j in range(count):
        wait_bytes(o_ref.at[pl.ds(0, (n_plane - 1) * per[j])], sum_sem.at[2 * count + j])
    for way in (1, 2):

        @pl.when(sends[way - 1])
        def _():
            wait_bytes(raw.at[0], sent)

    for ref in (tgt_s, look_s, outs):
        wait_bytes(ref.at[pl.ds(0, n_plane - 1)], sent)
    wait_bytes(small_in.at[pl.ds(0, n_plane - 1)], sent)
    wait_bytes(small_date.at[pl.ds(0, n_date - 1)], sent)
    for rows in ((n_plane - 1) * sum(per), (n_date - 1) * sum(per), (n_plane - 1) * sum(per)):
        wait_bytes(x_ref.at[pl.ds(0, rows)], sent)


def whole_finish(dims, den, sums, small, den_out, lift_out, lbias_out, mid_out, mbias_out, proj_out):
    n_plane, tr, tc, ch = dims
    for z in range(2):
        for t in range(tr):
            for k in range(n_plane):
                den_out[z, t, k : k + 1, :] = den[k, z * tr + t : z * tr + t + 1, 0:tc]
    finish_grads(ch, sums, small, lift_out, lbias_out, mid_out, mbias_out, proj_out)


def whole_local(slc, pairs, target, w_lift, b_lift, w_mid, b_mid, w_proj):
    n_row, n_col, n_date = (lax.axis_size(axis) for axis in ("row", "col", "date"))
    dates, srows, scols = slc.shape[1:]
    count, tr, tc = target.shape[1:]
    ch = w_mid.shape[-1]
    halves = scols // 128
    bf16, f32 = jnp.bfloat16, jnp.float32
    images = slc.transpose(1, 2, 0, 3)
    depth = -(-2 * dates // 16) * 16
    tgt = target.transpose(0, 2, 1, 3)
    w_lift, w_proj = w_lift.transpose(1, 2, 0, 3), w_proj.transpose(1, 2, 0, 3)
    scale = 1.0 / math.sqrt(2.0 * count * n_date * tr * n_row * tc * n_col)
    nb = n_row * tr
    n, wide = nb * 128, (nb + 2) * 128
    n_plane = n_row * n_col
    zt = -(-2 * tr // 8) * 8
    dma = pltpu.SemaphoreType.DMA
    vmem = pltpu.VMEM
    shape = jax.ShapeDtypeStruct
    images, index, tgt, w_lift, b_lift, w_mid, b_mid, w_proj = (
        pltpu.with_memory_space_constraint(x, pltpu.HBM)
        for x in (images, pairs.T, tgt, w_lift, b_lift, w_mid, b_mid, w_proj)
    )
    den, sums, small = pl.pallas_call(
        functools.partial(whole_kernel, (n_row, n_col, n_date, dates, tr, tc), scale),
        out_shape=(
            shape((n_plane, zt, 128), f32),
            shape((10 * ch, 128), f32),
            shape((24, 128), f32),
        ),
        in_specs=[pl.BlockSpec(memory_space=pltpu.HBM)] * 8,
        out_specs=(pl.BlockSpec(memory_space=vmem),) * 3,
        scratch_shapes=[
            vmem((3,) + images.shape, bf16),
            vmem((3 * halves * depth, srows * 128), bf16),
            vmem((2, count), jnp.int32),
            vmem(tgt.shape, f32),
            vmem((n_plane, zt, 128), f32),
            vmem((n_plane, zt, 128), f32),
            vmem((n_plane, zt, 128), f32),
            vmem((n_plane, zt, 128), f32),
            vmem((8, wide), f32),
            vmem((8, n), f32),
            vmem((6 * ch, wide), bf16),
            vmem((6 * ch, wide), bf16),
            vmem((2 * ch, n), bf16),
            vmem((32, wide), f32),
            vmem((8, wide), f32),
            vmem((2 * ch, n), bf16),
            vmem((n_plane, zt, 128), f32),
            vmem((10 * ch, 128), f32),
            vmem(w_lift.shape, bf16),
            vmem(b_lift.shape, bf16),
            vmem(w_mid.shape, bf16),
            vmem(b_mid.shape, bf16),
            vmem(w_proj.shape, bf16),
            dma((4,)),
            vmem((2 * ch, 32), bf16),
            vmem((32, 2 * ch), bf16),
            vmem((2 * ch, 32), bf16),
            vmem((6 * ch, 6 * ch), bf16),
            vmem((6 * ch, 6 * ch), bf16),
            vmem((2 * ch, 1), f32),
            vmem((4, 128, 128), f32),
            vmem((3 * n_plane, 4 * ch // n_plane, 128), f32),
            vmem((3 * n_date, 4 * ch // n_plane, 128), f32),
            vmem((n_plane, 24, 128), f32),
            vmem((n_date, 24, 128), f32),
            dma((2 * tr,)),
            dma((6,)),
            dma((9,)),
        ],
        compiler_params=pltpu.CompilerParams(
            collective_id=0, has_side_effects=True, vmem_limit_bytes=48 * 1024 * 1024
        ),
    )(images, index, tgt, w_lift, b_lift, w_mid, b_mid, w_proj)
    denoised, grad_lift, lift_bias, grad_mid, mid_bias, grad_proj = pl.pallas_call(
        functools.partial(whole_finish, (n_plane, tr, tc, ch)),
        out_shape=(
            shape((2, tr, count, tc), f32),
            shape((3, 3, 2, ch), f32),
            shape((2, ch), f32),
            shape((2, 3, 3, ch, ch), f32),
            shape((2, ch), f32),
            shape((3, 3, 2, ch), f32),
        ),
        in_specs=[pl.BlockSpec(memory_space=vmem)] * 3,
        out_specs=(pl.BlockSpec(memory_space=vmem),) * 6,
        compiler_params=pltpu.CompilerParams(vmem_limit_bytes=8 * 1024 * 1024),
    )(den, sums, small)
    return (
        denoised.transpose(0, 2, 1, 3),
        grad_lift.transpose(2, 0, 1, 3),
        lift_bias,
        grad_mid,
        mid_bias,
        grad_proj.transpose(2, 0, 1, 3),
    )


def local(slc, pairs, target, w_lift, b_lift, w_mid, b_mid, w_proj):
    n_row, n_col = lax.axis_size("row"), lax.axis_size("col")
    count, tr, tc = target.shape[1:]
    whole = (
        count == n_row * n_col
        and tc * n_col == 128
        and (n_row * tr) % 2 == 0
        and 2 * tr <= 8
        and count == 8
        and n_row % 2 == 0
        and 2 * w_mid.shape[-1] == 128
        and (2 * slc.shape[1] * slc.shape[3] // 128) % 16 == 0
    )
    return (whole_local if whole else halo_local)(
        slc, pairs, target, w_lift, b_lift, w_mid, b_mid, w_proj
    )


def solution(mesh):
    in_specs = (
        P(None, "date", "row", "col"),
        P("date", None),
        P(None, "date", "row", "col"),
        P(),
        P(),
        P(),
        P(),
        P(),
    )
    out_specs = (P(None, "date", "row", "col"), P(), P(), P(), P(), P())
    return jax.shard_map(local, mesh=mesh, in_specs=in_specs, out_specs=out_specs, check_vma=False)
```
